128 devices in a mesh: layer: 8 (over z, y_lo), blk: 16 (over x, y_hi, core).
Axes of the slice: x: 4, y: 4 (y_hi: 2, y_lo: 2; y = y_hi * 2 + y_lo), z: 4, core: 2. Of those that a mesh axis runs over, the one named last changes fastest.
Arguments:
- iterate: bfloat16 [8, 1536, 12288], P('layer', 'blk'), may hold values from -0.0546875 to 0.0546875
Outputs:
- update: bfloat16 [8, 1536, 12288], P(None, 'blk', 'layer')
The draws below stay inside these ranges and needn't reach their ends.
All inputs are finite; a program needn't handle non-finite values.
Results may differ from the reference program's by a relative error of at most 0.0095.
Values may be sent and summed in bfloat16 or wider, within the bound.
No kernel may reach another device: no remote copies, remote signals or barrier semaphores. Data moves between devices by JAX's collectives and lax.ppermute only.
A program may use at most 128 MiB of HBM per device.

```python
import math
import jax
import jax.numpy as jnp
from jax import lax

ROWS = 1536
COLS = 12288
LAYERS = 8


def block_levels(own_key, shape, cuts, smallest, largest):
    loudness, own = 1.0, jax.random.fold_in(own_key, 6)
    for dim, parts in cuts:
        heights = jnp.exp(jax.random.uniform(jax.random.fold_in(own, dim), (parts,), jnp.float32, smallest / len(cuts), largest / len(cuts)))
        loudness = loudness * jnp.repeat(heights, shape[dim] // parts).reshape([-1 if axis == dim else 1 for axis in range(len(shape))])
    return loudness


def bell_draw(own_key, dims, width, reach, cuts=(), kind=jnp.bfloat16):
    factor_of = block_levels(own_key, dims, cuts, -0.22, 0.18) if cuts else 1.0
    entries = jax.random.normal(own_key, dims, jnp.float32) * width * factor_of
    return jnp.minimum(jnp.maximum(entries, -reach), reach).astype(kind)


def setup_inputs(seed: int = 0) -> dict:
    key_of = jax.random.split(jax.random.key(seed), 2)
    return {
        "iterate": bell_draw(key_of[0], (LAYERS, ROWS, COLS), COLS ** -0.5, 0.0546875, ((0, 8), (1, 16))),
    }


coeff_a = 3.4445
coeff_b = -4.775
coeff_c = 2.0315

def orthogonal_step(matrix):
    gram = jnp.dot(matrix, matrix.T, preferred_element_type=jnp.float32).astype(jnp.bfloat16)
    square = jnp.dot(gram, gram, preferred_element_type=jnp.float32)
    mixing = (coeff_b * gram.astype(jnp.float32) + coeff_c * square).astype(jnp.bfloat16)
    result = coeff_a * matrix.astype(jnp.float32) + jnp.dot(mixing, matrix, preferred_element_type=jnp.float32)
    scale = math.sqrt(max(ROWS, COLS))
    return (scale * result).astype(jnp.bfloat16)

def reference(iterate):
    return lax.map(orthogonal_step, iterate)
```

```python
import math

import jax
import jax.numpy as jnp
from jax import lax
from jax.experimental import pallas as pl
from jax.experimental.pallas import tpu as pltpu
from jax.sharding import Mesh, PartitionSpec as P

coeff_a = 3.4445
coeff_b = -4.775
coeff_c = 2.0315

ROWS = 1536
COLS = 12288
LANES = 128
CHIPS = 8
STRIPES = 8
PANEL = ROWS // (2 * CHIPS)
HALF = ROWS // 2
WIDTH = COLS // CHIPS
TILES = COLS // STRIPES // LANES
MIB = 1 << 20

CHIP_AXES = ("x", "yh")
ALL_CHIPS = ("z", "yl", "x", "yh")


def halves(a, b, first):
    a, b = a.astype(jnp.float32), b.astype(jnp.float32)
    low = lax.broadcasted_iota(jnp.int32, a.shape, a.ndim - 1) < LANES // 2
    if first:
        return jnp.where(low, a, pltpu.roll(b, LANES // 2, a.ndim - 1))
    return jnp.where(low, pltpu.roll(a, LANES // 2, a.ndim - 1), b)


def tile(index):
    return pl.ds(index * LANES, LANES)


def split_kernel(x_ref, out_ref):
    for p in range(CHIPS):
        for j in range(STRIPES):
            out_ref[p, :, tile(j)] = x_ref[:, tile(TILES * j + p)]
        for m in range(STRIPES // 2):
            left = x_ref[:, tile(TILES * (2 * m) + CHIPS + p // 2)]
            right = x_ref[:, tile(TILES * (2 * m + 1) + CHIPS + p // 2)]
            out_ref[p, :, tile(STRIPES + m)] = halves(left, right, p % 2 == 0).astype(out_ref.dtype)


def split_columns(x):
    return pl.pallas_call(
        split_kernel,
        out_shape=jax.ShapeDtypeStruct((CHIPS, PANEL, WIDTH), x.dtype),
        compiler_params=pltpu.CompilerParams(vmem_limit_bytes=16 * MIB),
        name="split_columns",
    )(x)


def gram_kernel(own_ref, other_ref, out_ref):
    for side, ref in enumerate((own_ref, other_ref)):
        for n in range(0, HALF, 256):
            part = lax.dot_general(
                own_ref[...], ref[pl.ds(n, 256), :], (((1,), (1,)), ((), ())), preferred_element_type=jnp.float32
            )
            out_ref[:, pl.ds(side * HALF + n, 256)] = part.astype(out_ref.dtype)


def partial_gram(own, other):
    return pl.pallas_call(
        gram_kernel,
        out_shape=jax.ShapeDtypeStruct((HALF, ROWS), own.dtype),
        compiler_params=pltpu.CompilerParams(vmem_limit_bytes=24 * MIB),
        cost_estimate=pl.CostEstimate(
            flops=2 * HALF * ROWS * WIDTH, bytes_accessed=6 * HALF * ROWS, transcendentals=0
        ),
        name="partial_gram",
    )(own, other)


def update_kernel(gram_ref, gram_other_ref, x_ref, x_other_ref, out_ref, mixing_ref):
    scale = math.sqrt(max(ROWS, COLS))
    step = 256
    for n in range(0, ROWS, step):
        m = (n + HALF) % ROWS
        square = jnp.dot(gram_ref[:, pl.ds(0, HALF)], gram_ref[:, pl.ds(n, step)], preferred_element_type=jnp.float32)
        square += jnp.dot(
            gram_ref[:, pl.ds(HALF, HALF)], gram_other_ref[:, pl.ds(m, step)], preferred_element_type=jnp.float32
        )
        gram = gram_ref[:, pl.ds(n, step)].astype(jnp.float32)
        mixing_ref[:, pl.ds(n, step)] = (coeff_b * gram + coeff_c * square).astype(mixing_ref.dtype)
    for t in range(0, TILES, 2):
        columns = pl.ds(t * LANES, 2 * LANES)
        result = jnp.dot(mixing_ref[:, pl.ds(0, HALF)], x_ref[:, columns], preferred_element_type=jnp.float32)
        result += jnp.dot(mixing_ref[:, pl.ds(HALF, HALF)], x_other_ref[:, columns], preferred_element_type=jnp.float32)
        result = scale * (coeff_a * x_ref[:, columns].astype(jnp.float32) + result)
        for i in range(2):
            block = result[:, i * LANES : (i + 1) * LANES].reshape(CHIPS, PANEL, LANES)
            j = t + i
            if j < STRIPES:
                out_ref[j, :, pl.ds(0, PANEL), :] = block.astype(out_ref.dtype)
            else:
                top, bottom = block[:, : PANEL // 2], block[:, PANEL // 2 :]
                for side in range(2):
                    packed = halves(top, bottom, side == 0).astype(out_ref.dtype)
                    out_ref[2 * (j - STRIPES) + side, :, pl.ds(PANEL, PANEL // 2), :] = packed


def update_rows(gram, gram_other, x, x_other):
    return pl.pallas_call(
        update_kernel,
        out_shape=jax.ShapeDtypeStruct((STRIPES, CHIPS, PANEL + PANEL // 2, LANES), x.dtype),
        scratch_shapes=[pltpu.VMEM((HALF, ROWS), x.dtype)],
        compiler_params=pltpu.CompilerParams(vmem_limit_bytes=32 * MIB),
        cost_estimate=pl.CostEstimate(
            flops=4 * HALF * ROWS * ROWS, bytes_accessed=10 * HALF * ROWS, transcendentals=0
        ),
        name="update_rows",
    )(gram, gram_other, x, x_other)


def join_kernel(pieces_ref, out_ref):
    for p in range(CHIPS):
        out_ref[0, :, tile(p)] = pieces_ref[0, p, pl.ds(0, PANEL), :]
    for pair in range(CHIPS // 2):
        left = pieces_ref[0, 2 * pair, pl.ds(PANEL, PANEL // 2), :]
        right = pieces_ref[0, 2 * pair + 1, pl.ds(PANEL, PANEL // 2), :]
        for part in range(2):
            joined = halves(left, right, part == 0).astype(out_ref.dtype)
            out_ref[0, pl.ds(part * PANEL // 2, PANEL // 2), tile(CHIPS + pair)] = joined


def join_columns(pieces):
    layers = pieces.shape[0]
    return pl.pallas_call(
        join_kernel,
        grid=(layers,),
        in_specs=[pl.BlockSpec((1,) + pieces.shape[1:], lambda i: (i, 0, 0, 0))],
        out_specs=pl.BlockSpec((1, PANEL, TILES * LANES), lambda i: (i, 0, 0)),
        out_shape=jax.ShapeDtypeStruct((layers, PANEL, TILES * LANES), pieces.dtype),
        compiler_params=pltpu.CompilerParams(vmem_limit_bytes=16 * MIB),
        name="join_columns",
    )(pieces)


def swap_cores(value):
    return lax.ppermute(value, "c", [(0, 1), (1, 0)])


def shards(iterate):
    pieces = split_columns(iterate.reshape(PANEL, COLS))
    own = lax.all_to_all(pieces, CHIP_AXES, 0, 0, tiled=True).reshape(HALF, WIDTH)
    other = swap_cores(own)
    partial = partial_gram(own, other).reshape(CHIPS, PANEL, ROWS)
    partials = lax.all_to_all(partial, CHIP_AXES, 0, 0, tiled=True)
    gram = jnp.sum(partials.astype(jnp.float32), axis=0).astype(jnp.bfloat16)
    copies = jnp.broadcast_to(gram, (CHIPS, PANEL, ROWS))
    gram_own = lax.all_to_all(copies, CHIP_AXES, 0, 0, tiled=True).reshape(HALF, ROWS)
    gram_other = swap_cores(gram_own)
    sent = update_rows(gram_own, gram_other, own, other)
    sent = sent.reshape(STRIPES * CHIPS, PANEL + PANEL // 2, LANES)
    received = lax.all_to_all(sent, ALL_CHIPS, 0, 0, tiled=True)
    return join_columns(received.reshape(STRIPES, CHIPS, PANEL + PANEL // 2, LANES))


def solution(mesh):
    fine = Mesh(mesh.devices.reshape(4, 2, 4, 2, 2), ("z", "yl", "x", "yh", "c"))
    return jax.shard_map(
        shards,
        mesh=fine,
        in_specs=(P(("z", "yl"), ("x", "yh", "c"), None),),
        out_specs=P(None, ("x", "yh", "c"), ("z", "yl")),
        check_vma=False,
    )
```

```python
import math

import jax
import jax.numpy as jnp
from jax import lax
from jax.experimental import pallas as pl
from jax.experimental.pallas import tpu as pltpu
from jax.sharding import Mesh, PartitionSpec as P

coeff_a = 3.4445
coeff_b = -4.775
coeff_c = 2.0315

ROWS = 1536
COLS = 12288
LANES = 128
CHIPS = 8
STRIPES = 8
PANEL = ROWS // (2 * CHIPS)
HALF = ROWS // 2
WIDTH = COLS // CHIPS
TILES = COLS // STRIPES // LANES
BLOCKS = HALF // LANES
PACKED = LANES * BLOCKS * (BLOCKS + 1)
MIB = 1 << 20

CHIP_AXES = ("x", "yh")
ALL_CHIPS = ("z", "yl", "x", "yh")


def halves(a, b, first):
    a, b = a.astype(jnp.float32), b.astype(jnp.float32)
    low = lax.broadcasted_iota(jnp.int32, a.shape, a.ndim - 1) < LANES // 2
    if first:
        return jnp.where(low, a, pltpu.roll(b, LANES // 2, a.ndim - 1))
    return jnp.where(low, pltpu.roll(a, LANES // 2, a.ndim - 1), b)


def tile(index):
    return pl.ds(index * LANES, LANES)


def split_kernel(x_ref, out_ref):
    for p in range(CHIPS):
        for j in range(STRIPES):
            out_ref[p, :, tile(j)] = x_ref[:, tile(TILES * j + p)]
        for m in range(STRIPES // 2):
            left = x_ref[:, tile(TILES * (2 * m) + CHIPS + p // 2)]
            right = x_ref[:, tile(TILES * (2 * m + 1) + CHIPS + p // 2)]
            out_ref[p, :, tile(STRIPES + m)] = halves(left, right, p % 2 == 0).astype(out_ref.dtype)


def split_columns(x):
    return pl.pallas_call(
        split_kernel,
        out_shape=jax.ShapeDtypeStruct((CHIPS, PANEL, WIDTH), x.dtype),
        compiler_params=pltpu.CompilerParams(vmem_limit_bytes=16 * MIB),
        name="split_columns",
    )(x)


def lower_start(j):
    return LANES * (BLOCKS * j - j * (j - 1) // 2)


def gram_kernel(own_ref, other_ref, out_ref):
    for side, ref in enumerate((own_ref, other_ref)):
        for j in range(0, BLOCKS, 2):
            first = j * LANES
            part = lax.dot_general(
                own_ref[pl.ds(first, HALF - first), :],
                ref[pl.ds(first, 2 * LANES), :],
                (((1,), (1,)), ((), ())),
                preferred_element_type=jnp.float32,
            ).astype(out_ref.dtype)
            for i in range(2):
                start = side * PACKED // 2 + lower_start(j + i)
                rows = HALF - first - i * LANES
                out_ref[pl.ds(start, rows), :] = part[i * LANES :, i * LANES : (i + 1) * LANES]


def partial_gram(own, other):
    return pl.pallas_call(
        gram_kernel,
        out_shape=jax.ShapeDtypeStruct((PACKED, LANES), own.dtype),
        compiler_params=pltpu.CompilerParams(vmem_limit_bytes=24 * MIB),
        cost_estimate=pl.CostEstimate(
            flops=2 * PACKED * LANES * WIDTH, bytes_accessed=6 * HALF * ROWS, transcendentals=0
        ),
        name="partial_gram",
    )(own, other)


def sum_kernel(parts_ref, out_ref):
    total = jnp.sum(parts_ref[...].astype(jnp.float32), axis=0).astype(out_ref.dtype)
    for p in range(CHIPS):
        out_ref[p] = total


def sum_copies(parts):
    return pl.pallas_call(
        sum_kernel,
        out_shape=jax.ShapeDtypeStruct(parts.shape, parts.dtype),
        compiler_params=pltpu.CompilerParams(vmem_limit_bytes=16 * MIB),
        name="sum_copies",
    )(parts)


def unpack(own_ref, other_ref, gram_ref, gram_other_ref):
    half = PACKED // 2
    for j in range(BLOCKS):
        first = j * LANES
        rows = HALF - first
        start = lower_start(j)
        columns = tile(j)
        mine = own_ref[pl.ds(start, rows), :]
        theirs = other_ref[pl.ds(start, rows), :]
        gram_ref[pl.ds(first, rows), columns] = mine
        gram_other_ref[pl.ds(first, rows), columns] = theirs
        gram_ref[pl.ds(first, rows), tile(BLOCKS + j)] = own_ref[pl.ds(half + start, rows), :]
        if j + 1 < BLOCKS:
            below = rows - LANES
            cross = other_ref[pl.ds(half + start + LANES, below), :]
            gram_ref[pl.ds(first, LANES), pl.ds(first + LANES, below)] = mine[LANES:].T
            gram_other_ref[pl.ds(first, LANES), pl.ds(first + LANES, below)] = theirs[LANES:].T
            gram_ref[pl.ds(first, LANES), pl.ds(HALF + first + LANES, below)] = cross.T


def update_kernel(own_ref, other_ref, x_ref, x_other_ref, out_ref, gram_ref, gram_other_ref, mixing_ref):
    scale = math.sqrt(max(ROWS, COLS))
    step = 256
    unpack(own_ref, other_ref, gram_ref, gram_other_ref)
    for n in range(0, ROWS, step):
        left, right = gram_ref[:, pl.ds(0, HALF)], gram_ref[:, pl.ds(HALF, HALF)]
        square = jnp.dot(left, gram_ref[:, pl.ds(n, step)], preferred_element_type=jnp.float32)
        if n < HALF:
            square += lax.dot_general(
                right,
                gram_ref[pl.ds(n, step), pl.ds(HALF, HALF)],
                (((1,), (1,)), ((), ())),
                preferred_element_type=jnp.float32,
            )
        else:
            square += jnp.dot(right, gram_other_ref[:, pl.ds(n - HALF, step)], preferred_element_type=jnp.float32)
        gram = gram_ref[:, pl.ds(n, step)].astype(jnp.float32)
        mixing_ref[:, pl.ds(n, step)] = (coeff_b * gram + coeff_c * square).astype(mixing_ref.dtype)
    for t in range(0, TILES, 2):
        columns = pl.ds(t * LANES, 2 * LANES)
        result = jnp.dot(mixing_ref[:, pl.ds(0, HALF)], x_ref[:, columns], preferred_element_type=jnp.float32)
        result += jnp.dot(mixing_ref[:, pl.ds(HALF, HALF)], x_other_ref[:, columns], preferred_element_type=jnp.float32)
        result = scale * (coeff_a * x_ref[:, columns].astype(jnp.float32) + result)
        for i in range(2):
            block = result[:, i * LANES : (i + 1) * LANES].reshape(CHIPS, PANEL, LANES)
            j = t + i
            if j < STRIPES:
                out_ref[j, :, pl.ds(0, PANEL), :] = block.astype(out_ref.dtype)
            else:
                top, bottom = block[:, : PANEL // 2], block[:, PANEL // 2 :]
                for side in range(2):
                    packed = halves(top, bottom, side == 0).astype(out_ref.dtype)
                    out_ref[2 * (j - STRIPES) + side, :, pl.ds(PANEL, PANEL // 2), :] = packed


def update_rows(own, other, x, x_other):
    return pl.pallas_call(
        update_kernel,
        out_shape=jax.ShapeDtypeStruct((STRIPES, CHIPS, PANEL + PANEL // 2, LANES), x.dtype),
        scratch_shapes=[
            pltpu.VMEM((HALF, ROWS), x.dtype),
            pltpu.VMEM((HALF, HALF), x.dtype),
            pltpu.VMEM((HALF, ROWS), x.dtype),
        ],
        compiler_params=pltpu.CompilerParams(vmem_limit_bytes=32 * MIB),
        cost_estimate=pl.CostEstimate(
            flops=4 * HALF * ROWS * ROWS, bytes_accessed=10 * HALF * ROWS, transcendentals=0
        ),
        name="update_rows",
    )(own, other, x, x_other)


def join_kernel(pieces_ref, out_ref):
    for p in range(CHIPS):
        out_ref[0, :, tile(p)] = pieces_ref[0, p, pl.ds(0, PANEL), :]
    for pair in range(CHIPS // 2):
        left = pieces_ref[0, 2 * pair, pl.ds(PANEL, PANEL // 2), :]
        right = pieces_ref[0, 2 * pair + 1, pl.ds(PANEL, PANEL // 2), :]
        for part in range(2):
            joined = halves(left, right, part == 0).astype(out_ref.dtype)
            out_ref[0, pl.ds(part * PANEL // 2, PANEL // 2), tile(CHIPS + pair)] = joined


def join_columns(pieces):
    layers = pieces.shape[0]
    return pl.pallas_call(
        join_kernel,
        grid=(layers,),
        in_specs=[pl.BlockSpec((1,) + pieces.shape[1:], lambda i: (i, 0, 0, 0))],
        out_specs=pl.BlockSpec((1, PANEL, TILES * LANES), lambda i: (i, 0, 0)),
        out_shape=jax.ShapeDtypeStruct((layers, PANEL, TILES * LANES), pieces.dtype),
        compiler_params=pltpu.CompilerParams(vmem_limit_bytes=16 * MIB),
        name="join_columns",
    )(pieces)


def swap_cores(value):
    return lax.ppermute(value, "c", [(0, 1), (1, 0)])


def shards(iterate):
    pieces = split_columns(iterate.reshape(PANEL, COLS))
    own = lax.all_to_all(pieces, CHIP_AXES, 0, 0, tiled=True).reshape(HALF, WIDTH)
    other = swap_cores(own)
    partial = partial_gram(own, other).reshape(CHIPS, PACKED // CHIPS, LANES)
    partials = lax.all_to_all(partial, CHIP_AXES, 0, 0, tiled=True)
    copies = sum_copies(partials)
    gram_own = lax.all_to_all(copies, CHIP_AXES, 0, 0, tiled=True).reshape(PACKED, LANES)
    gram_other = swap_cores(gram_own)
    sent = update_rows(gram_own, gram_other, own, other)
    sent = sent.reshape(STRIPES * CHIPS, PANEL + PANEL // 2, LANES)
    received = lax.all_to_all(sent, ALL_CHIPS, 0, 0, tiled=True)
    return join_columns(received.reshape(STRIPES, CHIPS, PANEL + PANEL // 2, LANES))


def solution(mesh):
    fine = Mesh(mesh.devices.reshape(4, 2, 4, 2, 2), ("z", "yl", "x", "yh", "c"))
    return jax.shard_map(
        shards,
        mesh=fine,
        in_specs=(P(("z", "yl"), ("x", "yh", "c"), None),),
        out_specs=P(None, ("x", "yh", "c"), ("z", "yl")),
        check_vma=False,
    )
```

```python
import math

import jax
import jax.numpy as jnp
import numpy as np
from jax import lax
from jax.experimental import pallas as pl
from jax.experimental.pallas import tpu as pltpu
from jax.sharding import Mesh, PartitionSpec as P

coeff_a = 3.4445
coeff_b = -4.775
coeff_c = 2.0315

ROWS = 1536
COLS = 12288
LANES = 128
CHIPS = 8
STRIPES = 8
PANEL = ROWS // (2 * CHIPS)
HALF = ROWS // 2
WIDTH = COLS // CHIPS
TILES = COLS // STRIPES // LANES
BLOCKS = HALF // LANES
STREAM = LANES * BLOCKS * (BLOCKS + 1) // 3
PIECE = STREAM // CHIPS
MIB = 1 << 20

CHIP_AXES = ("x", "yh")
ALL_CHIPS = ("z", "yl", "x", "yh")
ORDERS = ("abd", "bda", "dab")


def halves(a, b, first):
    a, b = a.astype(jnp.float32), b.astype(jnp.float32)
    low = lax.broadcasted_iota(jnp.int32, a.shape, a.ndim - 1) < LANES // 2
    if first:
        return jnp.where(low, a, pltpu.roll(b, LANES // 2, a.ndim - 1))
    return jnp.where(low, pltpu.roll(a, LANES // 2, a.ndim - 1), b)


def tile(index):
    return pl.ds(index * LANES, LANES)


def positions():
    table = []
    for x in range(4):
        for d in range(2):
            bit = {"a": (x + 1) // 2 % 2, "b": x // 2, "d": d}
            table.append([4 * bit[i] + 2 * bit[j] + bit[k] for i, j, k in ORDERS])
    return np.array(table, np.int32)


def split_kernel(x_ref, out_ref):
    for p in range(CHIPS):
        for j in range(STRIPES):
            out_ref[p, :, tile(j)] = x_ref[:, tile(TILES * j + p)]
        for m in range(STRIPES // 2):
            left = x_ref[:, tile(TILES * (2 * m) + CHIPS + p // 2)]
            right = x_ref[:, tile(TILES * (2 * m + 1) + CHIPS + p // 2)]
            out_ref[p, :, tile(STRIPES + m)] = halves(left, right, p % 2 == 0).astype(out_ref.dtype)


def split_columns(x):
    return pl.pallas_call(
        split_kernel,
        out_shape=jax.ShapeDtypeStruct((CHIPS, PANEL, WIDTH), x.dtype),
        compiler_params=pltpu.CompilerParams(vmem_limit_bytes=16 * MIB),
        name="split_columns",
    )(x)


STREAMS = (
    ((0, 0), (0, 1), (0, 3)),
    ((0, 2), (0, 4), (0, 5), (1, 2), (1, 4), (1, 5)),
    ((1, 0), (1, 1), (1, 3)),
)


def strip_rows(j):
    return HALF - j * LANES


def strip_starts():
    starts = {}
    for s, strips in enumerate(STREAMS):
        row = 0
        for side, j in strips:
            starts[side, j] = s, row
            row += strip_rows(j)
        assert row == STREAM
    return starts


def fill_strips(own_ref, ref, side, columns, whole_ref, lead):
    first = columns[0] * LANES
    part = lax.dot_general(
        own_ref[pl.ds(first, HALF - first), :],
        ref[pl.ds(first, LANES * len(columns)), :],
        (((1,), (1,)), ((), ())),
        preferred_element_type=jnp.float32,
    )
    for i, j in enumerate(columns):
        s, start = strip_starts()[side, j]
        whole_ref[s - lead, pl.ds(start, strip_rows(j)), :] = part[i * LANES :, i * LANES : (i + 1) * LANES]


def place(whole_ref, stream, index, position):
    piece = lax.bitwise_xor(position, index)
    return whole_ref[stream, pl.ds(pl.multiple_of(piece * PIECE, 32), PIECE), :]


def first_kernel(index_ref, own_ref, keep_ref, send_ref, whole_ref):
    fill_strips(own_ref, own_ref, 0, (0, 1), whole_ref, 0)
    fill_strips(own_ref, own_ref, 0, (3,), whole_ref, 0)
    for k in range(CHIPS // 2):
        keep_ref[k] = place(whole_ref, 0, index_ref[0], k)
        send_ref[k] = place(whole_ref, 0, index_ref[0], k + CHIPS // 2).astype(send_ref.dtype)


def rest_kernel(index_ref, own_ref, other_ref, keep_b_ref, send_b_ref, keep_c_ref, send_c_ref, whole_ref):
    fill_strips(own_ref, own_ref, 0, (2,), whole_ref, 1)
    fill_strips(own_ref, own_ref, 0, (4, 5), whole_ref, 1)
    fill_strips(own_ref, other_ref, 1, (0, 1), whole_ref, 1)
    fill_strips(own_ref, other_ref, 1, (2, 3), whole_ref, 1)
    fill_strips(own_ref, other_ref, 1, (4, 5), whole_ref, 1)
    for s, (keep_ref, send_ref) in enumerate(((keep_b_ref, send_b_ref), (keep_c_ref, send_c_ref))):
        for k in range(CHIPS // 2):
            keep_ref[k] = place(whole_ref, s, index_ref[s + 1], k)
            send_ref[k] = place(whole_ref, s, index_ref[s + 1], k + CHIPS // 2).astype(send_ref.dtype)


def partial_gram(kernel, name, streams, blocks, index, *panels):
    half = (CHIPS // 2, PIECE, LANES)
    return pl.pallas_call(
        kernel,
        in_specs=[pl.BlockSpec(memory_space=pltpu.SMEM)] + [pl.BlockSpec(memory_space=pltpu.VMEM)] * len(panels),
        out_shape=[jax.ShapeDtypeStruct(half, t) for _ in range(streams) for t in (jnp.float32, panels[0].dtype)],
        scratch_shapes=[pltpu.VMEM((streams, STREAM, LANES), jnp.float32)],
        compiler_params=pltpu.CompilerParams(vmem_limit_bytes=12 * MIB),
        cost_estimate=pl.CostEstimate(
            flops=2 * blocks * LANES * LANES * WIDTH, bytes_accessed=6 * streams * STREAM * LANES, transcendentals=0
        ),
        name=name,
    )(index, *panels)


def flip(axis):
    if axis == "d":
        return "yh", [(0, 1), (1, 0)]
    return "x", [(i, i ^ 1 if axis == "a" else 3 - i) for i in range(4)]


def exchange(value, axis):
    return lax.ppermute(value, *flip(axis))


def wide(value):
    return value.astype(jnp.float32)


def sum_over_chips(keep, arrived, order):
    kind = arrived.dtype
    half = keep + wide(arrived)
    quarter = half[:2] + wide(exchange(half[2:].astype(kind), order[1]))
    quarter = quarter.astype(kind)
    total = (wide(quarter) + wide(exchange(quarter, order[2]))[::-1]).astype(kind)
    half = jnp.concatenate([total, exchange(total, order[1])])
    return jnp.concatenate([half, exchange(half, order[0])])


def unpack(index_ref, own_refs, other_refs, own_ref, other_ref, gram_ref, gram_other_ref):
    for s in range(len(STREAMS)):
        for k in range(CHIPS):
            rows = pl.ds(pl.multiple_of(lax.bitwise_xor(k, index_ref[s]) * PIECE, 32), PIECE)
            own_ref[s, rows, :] = own_refs[s][k]
            other_ref[s, rows, :] = other_refs[s][k]
    starts = strip_starts()
    for j in range(BLOCKS):
        first = j * LANES
        rows = strip_rows(j)
        s, start = starts[0, j]
        t, cross_start = starts[1, j]
        mine = own_ref[s, pl.ds(start, rows), :]
        theirs = other_ref[s, pl.ds(start, rows), :]
        gram_ref[pl.ds(first, rows), tile(j)] = mine
        gram_other_ref[pl.ds(first, rows), tile(j)] = theirs
        gram_ref[pl.ds(first, rows), tile(BLOCKS + j)] = own_ref[t, pl.ds(cross_start, rows), :]
        if j + 1 < BLOCKS:
            below = rows - LANES
            cross = other_ref[t, pl.ds(cross_start + LANES, below), :]
            gram_ref[pl.ds(first, LANES), pl.ds(first + LANES, below)] = mine[LANES:].T
            gram_other_ref[pl.ds(first, LANES), pl.ds(first + LANES, below)] = theirs[LANES:].T
            gram_ref[pl.ds(first, LANES), pl.ds(HALF + first + LANES, below)] = cross.T


def update_kernel(index_ref, *refs):
    own_refs, other_refs = refs[:3], refs[3:6]
    x_ref, x_other_ref, out_ref, own_ref, other_ref, gram_ref, gram_other_ref, mixing_ref = refs[6:]
    scale = math.sqrt(max(ROWS, COLS))
    step = 256
    unpack(index_ref, own_refs, other_refs, own_ref, other_ref, gram_ref, gram_other_ref)
    for n in range(0, ROWS, step):
        left, right = gram_ref[:, pl.ds(0, HALF)], gram_ref[:, pl.ds(HALF, HALF)]
        square = jnp.dot(left, gram_ref[:, pl.ds(n, step)], preferred_element_type=jnp.float32)
        if n < HALF:
            square += lax.dot_general(
                right,
                gram_ref[pl.ds(n, step), pl.ds(HALF, HALF)],
                (((1,), (1,)), ((), ())),
                preferred_element_type=jnp.float32,
            )
        else:
            square += jnp.dot(right, gram_other_ref[:, pl.ds(n - HALF, step)], preferred_element_type=jnp.float32)
        gram = gram_ref[:, pl.ds(n, step)].astype(jnp.float32)
        mixing_ref[:, pl.ds(n, step)] = (coeff_b * gram + coeff_c * square).astype(mixing_ref.dtype)
    for t in range(0, TILES, 2):
        columns = pl.ds(t * LANES, 2 * LANES)
        result = jnp.dot(mixing_ref[:, pl.ds(0, HALF)], x_ref[:, columns], preferred_element_type=jnp.float32)
        result += jnp.dot(mixing_ref[:, pl.ds(HALF, HALF)], x_other_ref[:, columns], preferred_element_type=jnp.float32)
        result = scale * (coeff_a * x_ref[:, columns].astype(jnp.float32) + result)
        for i in range(2):
            block = result[:, i * LANES : (i + 1) * LANES].reshape(CHIPS, PANEL, LANES)
            j = t + i
            if j < STRIPES:
                out_ref[j, :, pl.ds(0, PANEL), :] = block.astype(out_ref.dtype)
            else:
                top, bottom = block[:, : PANEL // 2], block[:, PANEL // 2 :]
                for side in range(2):
                    packed = halves(top, bottom, side == 0).astype(out_ref.dtype)
                    out_ref[2 * (j - STRIPES) + side, :, pl.ds(PANEL, PANEL // 2), :] = packed


def update_rows(index, own, other, x, x_other):
    operands = (*own, *other, x, x_other)
    return pl.pallas_call(
        update_kernel,
        in_specs=[pl.BlockSpec(memory_space=pltpu.SMEM)] + [pl.BlockSpec(memory_space=pltpu.VMEM)] * len(operands),
        out_shape=jax.ShapeDtypeStruct((STRIPES, CHIPS, PANEL + PANEL // 2, LANES), x.dtype),
        scratch_shapes=[
            pltpu.VMEM((len(STREAMS), STREAM, LANES), x.dtype),
            pltpu.VMEM((len(STREAMS), STREAM, LANES), x.dtype),
            pltpu.VMEM((HALF, ROWS), x.dtype),
            pltpu.VMEM((HALF, HALF), x.dtype),
            pltpu.VMEM((HALF, ROWS), x.dtype),
        ],
        compiler_params=pltpu.CompilerParams(vmem_limit_bytes=32 * MIB),
        cost_estimate=pl.CostEstimate(
            flops=4 * HALF * ROWS * ROWS, bytes_accessed=10 * HALF * ROWS, transcendentals=0
        ),
        name="update_rows",
    )(index, *operands)


def join_kernel(pieces_ref, out_ref):
    for p in range(CHIPS):
        out_ref[0, :, tile(p)] = pieces_ref[0, p, pl.ds(0, PANEL), :]
    for pair in range(CHIPS // 2):
        left = pieces_ref[0, 2 * pair, pl.ds(PANEL, PANEL // 2), :]
        right = pieces_ref[0, 2 * pair + 1, pl.ds(PANEL, PANEL // 2), :]
        for part in range(2):
            joined = halves(left, right, part == 0).astype(out_ref.dtype)
            out_ref[0, pl.ds(part * PANEL // 2, PANEL // 2), tile(CHIPS + pair)] = joined


def join_columns(pieces):
    layers = pieces.shape[0]
    return pl.pallas_call(
        join_kernel,
        grid=(layers,),
        in_specs=[pl.BlockSpec((1,) + pieces.shape[1:], lambda i: (i, 0, 0, 0))],
        out_specs=pl.BlockSpec((1, PANEL, TILES * LANES), lambda i: (i, 0, 0)),
        out_shape=jax.ShapeDtypeStruct((layers, PANEL, TILES * LANES), pieces.dtype),
        compiler_params=pltpu.CompilerParams(vmem_limit_bytes=16 * MIB),
        name="join_columns",
    )(pieces)


def swap_cores(value):
    return lax.ppermute(value, "c", [(0, 1), (1, 0)])


def shards(iterate):
    pieces = split_columns(iterate.reshape(PANEL, COLS))
    own = lax.all_to_all(pieces, CHIP_AXES, 0, 0, tiled=True).reshape(HALF, WIDTH)
    other = swap_cores(own)
    index = jnp.asarray(positions())[lax.axis_index(CHIP_AXES)]
    keep_a, send_a = partial_gram(first_kernel, "gram_first", 1, 15, index, own)
    arrived_a = exchange(send_a, ORDERS[0][0])
    rest = partial_gram(rest_kernel, "gram_rest", 2, 33, index, own, other)
    arrived_a, (keep_b, send_b, keep_c, send_c) = lax.optimization_barrier((arrived_a, rest))
    arrived = arrived_a, exchange(send_b, ORDERS[1][0]), exchange(send_c, ORDERS[2][0])
    grams = [sum_over_chips(*stream) for stream in zip((keep_a, keep_b, keep_c), arrived, ORDERS)]
    sent = update_rows(index, grams, [swap_cores(gram) for gram in grams], own, other)
    sent = sent.reshape(STRIPES * CHIPS, PANEL + PANEL // 2, LANES)
    received = lax.all_to_all(sent, ALL_CHIPS, 0, 0, tiled=True)
    return join_columns(received.reshape(STRIPES, CHIPS, PANEL + PANEL // 2, LANES))


def solution(mesh):
    fine = Mesh(mesh.devices.reshape(4, 2, 4, 2, 2), ("z", "yl", "x", "yh", "c"))
    return jax.shard_map(
        shards,
        mesh=fine,
        in_specs=(P(("z", "yl"), ("x", "yh", "c"), None),),
        out_specs=P(None, ("x", "yh", "c"), ("z", "yl")),
        check_vma=False,
    )
```

```python
import math

import jax
import jax.numpy as jnp
from jax import lax
from jax.experimental import pallas as pl
from jax.experimental.pallas import tpu as pltpu
from jax.sharding import Mesh, PartitionSpec as P

coeff_a = 3.4445
coeff_b = -4.775
coeff_c = 2.0315

ROWS = 1536
COLS = 12288
LANES = 128
CHIPS = 8
STRIPES = 8
PANEL = ROWS // (2 * CHIPS)
HALF = ROWS // 2
WIDTH = COLS // CHIPS
TILES = COLS // STRIPES // LANES
BLOCKS = HALF // LANES
BELOW = LANES * BLOCKS * (BLOCKS - 1) // 2
EDGE = 2 * BELOW + HALF
PACKED = -(-(EDGE + BLOCKS) // (16 * CHIPS)) * 16 * CHIPS
MIB = 1 << 20

CHIP_AXES = ("x", "yh")
ALL_CHIPS = ("z", "yl", "x", "yh")


def halves(a, b, first):
    a, b = a.astype(jnp.float32), b.astype(jnp.float32)
    low = lax.broadcasted_iota(jnp.int32, a.shape, a.ndim - 1) < LANES // 2
    if first:
        return jnp.where(low, a, pltpu.roll(b, LANES // 2, a.ndim - 1))
    return jnp.where(low, pltpu.roll(a, LANES // 2, a.ndim - 1), b)


def tile(index):
    return pl.ds(index * LANES, LANES)


def split_kernel(x_ref, out_ref):
    for p in range(CHIPS):
        for j in range(STRIPES):
            out_ref[p, :, tile(j)] = x_ref[:, tile(TILES * j + p)]
        for m in range(STRIPES // 2):
            left = x_ref[:, tile(TILES * (2 * m) + CHIPS + p // 2)]
            right = x_ref[:, tile(TILES * (2 * m + 1) + CHIPS + p // 2)]
            out_ref[p, :, tile(STRIPES + m)] = halves(left, right, p % 2 == 0).astype(out_ref.dtype)


def split_columns(x):
    return pl.pallas_call(
        split_kernel,
        out_shape=jax.ShapeDtypeStruct((CHIPS, PANEL, WIDTH), x.dtype),
        compiler_params=pltpu.CompilerParams(vmem_limit_bytes=16 * MIB),
        name="split_columns",
    )(x)


def strip(j):
    below = (BLOCKS - 1 - j) * LANES
    start = LANES * sum(BLOCKS - 1 - i for i in range(j))
    return pl.ds(start, below)


def triangle(own_ref, ref, store_below, store_diagonal):
    for j in range(0, BLOCKS, 2):
        first = j * LANES
        part = lax.dot_general(
            own_ref[pl.ds(first, HALF - first), :],
            ref[pl.ds(first, 2 * LANES), :],
            (((1,), (1,)), ((), ())),
            preferred_element_type=jnp.float32,
        )
        for i in range(2):
            columns = part[i * LANES :, i * LANES : (i + 1) * LANES]
            store_diagonal(j + i, columns[:LANES])
            if j + i + 1 < BLOCKS:
                store_below(strip(j + i), columns[LANES:])


def iotas():
    return [lax.broadcasted_iota(jnp.int32, (LANES, LANES), axis) for axis in range(2)]


def own_gram_kernel(own_ref, below_ref, diagonal_ref):
    def store_below(rows, value):
        below_ref[rows, :] = value.astype(below_ref.dtype)

    def store_diagonal(j, value):
        diagonal_ref[j] = value

    triangle(own_ref, own_ref, store_below, store_diagonal)


def own_gram(own):
    return pl.pallas_call(
        own_gram_kernel,
        out_shape=(
            jax.ShapeDtypeStruct((BELOW, LANES), own.dtype),
            jax.ShapeDtypeStruct((BLOCKS, LANES, LANES), jnp.float32),
        ),
        compiler_params=pltpu.CompilerParams(vmem_limit_bytes=8 * MIB),
        cost_estimate=pl.CostEstimate(
            flops=2 * (BELOW + 3 * HALF) * LANES * WIDTH, bytes_accessed=2 * HALF * WIDTH, transcendentals=0
        ),
        name="own_gram",
    )(own)


def cross_gram_kernel(below_ref, diagonal_ref, own_ref, other_ref, out_ref):
    row, column = iotas()
    edges = []

    def store_below(rows, value):
        out_ref[pl.ds(BELOW + rows.start, rows.size), :] = value.astype(out_ref.dtype)

    def store_diagonal(j, value):
        block = jnp.where(row >= column, diagonal_ref[j], value)
        out_ref[pl.ds(2 * BELOW + j * LANES, LANES), :] = block.astype(out_ref.dtype)
        edges.append(jnp.sum(jnp.where(row == column, value, 0.0), axis=0, keepdims=True))

    out_ref[pl.ds(0, BELOW), :] = below_ref[...]
    triangle(own_ref, other_ref, store_below, store_diagonal)
    rest = PACKED - EDGE
    edges.append(jnp.zeros((rest - BLOCKS, LANES), jnp.float32))
    out_ref[pl.ds(EDGE, rest), :] = jnp.concatenate(edges).astype(out_ref.dtype)


def cross_gram(below, diagonal, own, other):
    return pl.pallas_call(
        cross_gram_kernel,
        out_shape=jax.ShapeDtypeStruct((PACKED, LANES), own.dtype),
        compiler_params=pltpu.CompilerParams(vmem_limit_bytes=12 * MIB),
        cost_estimate=pl.CostEstimate(
            flops=2 * (BELOW + 3 * HALF) * LANES * WIDTH, bytes_accessed=4 * HALF * WIDTH, transcendentals=0
        ),
        name="cross_gram",
    )(below, diagonal, own, other)


def sum_kernel(parts_ref, out_ref):
    total = jnp.sum(parts_ref[...].astype(jnp.float32), axis=0).astype(out_ref.dtype)
    for p in range(CHIPS):
        out_ref[p] = total


def sum_copies(parts):
    return pl.pallas_call(
        sum_kernel,
        out_shape=jax.ShapeDtypeStruct(parts.shape, parts.dtype),
        compiler_params=pltpu.CompilerParams(vmem_limit_bytes=16 * MIB),
        name="sum_copies",
    )(parts)


def mirror(packed_ref, out_ref, lower):
    for j in range(BLOCKS):
        first = j * LANES
        block = packed_ref[pl.ds(2 * BELOW + first, LANES), :]
        out_ref[pl.ds(first, LANES), tile(j)] = jnp.where(lower, block, block.T)
        if j + 1 < BLOCKS:
            below = packed_ref[strip(j), :]
            out_ref[pl.ds(first + LANES, below.shape[0]), tile(j)] = below
            out_ref[pl.ds(first, LANES), pl.ds(first + LANES, below.shape[0])] = below.T


def own_square_kernel(packed_ref, gram_ref, square_ref):
    row, column = iotas()
    mirror(packed_ref, gram_ref, row >= column)
    for n in range(0, HALF, 256):
        columns = pl.ds(n, 256)
        square_ref[:, columns] = jnp.dot(gram_ref[...], gram_ref[:, columns], preferred_element_type=jnp.float32)


def own_square(packed):
    return pl.pallas_call(
        own_square_kernel,
        out_shape=(
            jax.ShapeDtypeStruct((HALF, HALF), packed.dtype),
            jax.ShapeDtypeStruct((HALF, HALF), jnp.float32),
        ),
        compiler_params=pltpu.CompilerParams(vmem_limit_bytes=12 * MIB),
        cost_estimate=pl.CostEstimate(
            flops=2 * HALF * HALF * HALF, bytes_accessed=8 * HALF * HALF, transcendentals=0
        ),
        name="own_square",
    )(packed)


def unpack_cross(own_ref, other_ref, cross_ref):
    row, column = iotas()
    for j in range(BLOCKS):
        first = j * LANES
        upper, theirs = (ref[pl.ds(2 * BELOW + first, LANES), :] for ref in (own_ref, other_ref))
        edge = jnp.broadcast_to(own_ref[pl.ds(EDGE, 16), :].astype(jnp.float32)[j : j + 1], (LANES, LANES))
        block = jnp.where(row < column, upper.astype(jnp.float32), theirs.T.astype(jnp.float32))
        cross_ref[pl.ds(first, LANES), tile(j)] = jnp.where(row == column, edge, block).astype(cross_ref.dtype)
        if j + 1 < BLOCKS:
            rows = pl.ds(BELOW + strip(j).start, strip(j).size)
            cross_ref[pl.ds(first + LANES, rows.size), tile(j)] = own_ref[rows, :]
            cross_ref[pl.ds(first, LANES), pl.ds(first + LANES, rows.size)] = other_ref[rows, :].T


def update_kernel(
    own_ref, other_ref, gram_ref, square_ref, x_ref, x_other_ref, out_ref, cross_ref, gram_other_ref, mixing_ref
):
    scale = math.sqrt(max(ROWS, COLS))
    step = 256
    row, column = iotas()
    unpack_cross(own_ref, other_ref, cross_ref)
    mirror(other_ref, gram_other_ref, row >= column)
    for n in range(0, HALF, step):
        columns = pl.ds(n, step)
        square = square_ref[:, columns] + lax.dot_general(
            cross_ref[...], cross_ref[columns, :], (((1,), (1,)), ((), ())), preferred_element_type=jnp.float32
        )
        gram = gram_ref[:, columns].astype(jnp.float32)
        mixing_ref[:, columns] = (coeff_b * gram + coeff_c * square).astype(mixing_ref.dtype)
    for n in range(0, HALF, step):
        columns = pl.ds(n, step)
        square = jnp.dot(gram_ref[...], cross_ref[:, columns], preferred_element_type=jnp.float32)
        square += jnp.dot(cross_ref[...], gram_other_ref[:, columns], preferred_element_type=jnp.float32)
        gram = cross_ref[:, columns].astype(jnp.float32)
        mixing_ref[:, pl.ds(HALF + n, step)] = (coeff_b * gram + coeff_c * square).astype(mixing_ref.dtype)
    for t in range(0, TILES, 2):
        columns = pl.ds(t * LANES, 2 * LANES)
        result = jnp.dot(mixing_ref[:, pl.ds(0, HALF)], x_ref[:, columns], preferred_element_type=jnp.float32)
        result += jnp.dot(mixing_ref[:, pl.ds(HALF, HALF)], x_other_ref[:, columns], preferred_element_type=jnp.float32)
        result = scale * (coeff_a * x_ref[:, columns].astype(jnp.float32) + result)
        for i in range(2):
            block = result[:, i * LANES : (i + 1) * LANES].reshape(CHIPS, PANEL, LANES)
            j = t + i
            if j < STRIPES:
                out_ref[j, :, pl.ds(0, PANEL), :] = block.astype(out_ref.dtype)
            else:
                top, bottom = block[:, : PANEL // 2], block[:, PANEL // 2 :]
                for side in range(2):
                    packed = halves(top, bottom, side == 0).astype(out_ref.dtype)
                    out_ref[2 * (j - STRIPES) + side, :, pl.ds(PANEL, PANEL // 2), :] = packed


def update_rows(packed, packed_other, gram, square, x, x_other):
    return pl.pallas_call(
        update_kernel,
        out_shape=jax.ShapeDtypeStruct((STRIPES, CHIPS, PANEL + PANEL // 2, LANES), x.dtype),
        scratch_shapes=[
            pltpu.VMEM((HALF, HALF), x.dtype),
            pltpu.VMEM((HALF, HALF), x.dtype),
            pltpu.VMEM((HALF, ROWS), x.dtype),
        ],
        compiler_params=pltpu.CompilerParams(vmem_limit_bytes=24 * MIB),
        cost_estimate=pl.CostEstimate(
            flops=4 * HALF * ROWS * ROWS - 2 * HALF * HALF * HALF, bytes_accessed=10 * HALF * ROWS, transcendentals=0
        ),
        name="update_rows",
    )(packed, packed_other, gram, square, x, x_other)


def join_kernel(pieces_ref, out_ref, whole_ref, sems):
    copies = []
    for layer in range(STRIPES):
        for p in range(CHIPS):
            whole_ref[layer, :, tile(p)] = pieces_ref[layer, p, pl.ds(0, PANEL), :]
        for pair in range(CHIPS // 2):
            left = pieces_ref[layer, 2 * pair, pl.ds(PANEL, PANEL // 2), :]
            right = pieces_ref[layer, 2 * pair + 1, pl.ds(PANEL, PANEL // 2), :]
            for part in range(2):
                joined = halves(left, right, part == 0).astype(whole_ref.dtype)
                whole_ref[layer, pl.ds(part * PANEL // 2, PANEL // 2), tile(CHIPS + pair)] = joined
        copies.append(pltpu.make_async_copy(whole_ref.at[layer], out_ref.at[layer], sems.at[layer]))
        copies[-1].start()
    for copy in copies:
        copy.wait()


def join_columns(pieces):
    shape = (pieces.shape[0], PANEL, TILES * LANES)
    return pl.pallas_call(
        join_kernel,
        in_specs=[pl.BlockSpec(memory_space=pltpu.VMEM)],
        out_specs=pl.BlockSpec(memory_space=pl.ANY),
        out_shape=jax.ShapeDtypeStruct(shape, pieces.dtype),
        scratch_shapes=[pltpu.VMEM(shape, pieces.dtype), pltpu.SemaphoreType.DMA((pieces.shape[0],))],
        compiler_params=pltpu.CompilerParams(vmem_limit_bytes=12 * MIB),
        name="join_columns",
    )(pieces)


def swap_cores(value):
    return lax.ppermute(value, "c", [(0, 1), (1, 0)])


def shards(iterate):
    pieces = split_columns(iterate.reshape(PANEL, COLS))
    own = lax.all_to_all(pieces, CHIP_AXES, 0, 0, tiled=True).reshape(HALF, WIDTH)
    other = swap_cores(own)
    partial = cross_gram(*own_gram(own), own, other).reshape(CHIPS, PACKED // CHIPS, LANES)
    partials = lax.all_to_all(partial, CHIP_AXES, 0, 0, tiled=True)
    copies = sum_copies(partials)
    packed = lax.all_to_all(copies, CHIP_AXES, 0, 0, tiled=True).reshape(PACKED, LANES)
    packed_other = swap_cores(packed)
    sent = update_rows(packed, packed_other, *own_square(packed), own, other)
    sent = sent.reshape(STRIPES * CHIPS, PANEL + PANEL // 2, LANES)
    received = lax.all_to_all(sent, ALL_CHIPS, 0, 0, tiled=True)
    return join_columns(received.reshape(STRIPES, CHIPS, PANEL + PANEL // 2, LANES))


def solution(mesh):
    fine = Mesh(mesh.devices.reshape(4, 2, 4, 2, 2), ("z", "yl", "x", "yh", "c"))
    return jax.shard_map(
        shards,
        mesh=fine,
        in_specs=(P(("z", "yl"), ("x", "yh", "c"), None),),
        out_specs=P(None, ("x", "yh", "c"), ("z", "yl")),
        check_vma=False,
    )
```

```python
import math

import jax
import jax.numpy as jnp
import numpy as np
from jax import lax
from jax.experimental import pallas as pl
from jax.experimental.pallas import tpu as pltpu
from jax.sharding import Mesh, PartitionSpec as P

coeff_a = 3.4445
coeff_b = -4.775
coeff_c = 2.0315

ROWS = 1536
COLS = 12288
LANES = 128
CHIPS = 8
STRIPES = 8
PANEL = ROWS // (2 * CHIPS)
HALF = ROWS // 2
WIDTH = COLS // CHIPS
TILES = COLS // STRIPES // LANES
BLOCKS = HALF // LANES
BELOW = LANES * BLOCKS * (BLOCKS - 1) // 2
EDGE = 2 * BELOW + HALF
PACKED = -(-(EDGE + BLOCKS) // (16 * CHIPS)) * 16 * CHIPS
PIECES = (BELOW // CHIPS,) + ((PACKED - BELOW) // (2 * CHIPS),) * 2
BASES = (0, BELOW, BELOW + CHIPS * PIECES[1])
MIB = 1 << 20

CHIP_AXES = ("x", "yh")
ALL_CHIPS = ("z", "yl", "x", "yh")
ORDERS = ("abd", "bda", "dab")


def halves(a, b, first):
    a, b = a.astype(jnp.float32), b.astype(jnp.float32)
    low = lax.broadcasted_iota(jnp.int32, a.shape, a.ndim - 1) < LANES // 2
    if first:
        return jnp.where(low, a, pltpu.roll(b, LANES // 2, a.ndim - 1))
    return jnp.where(low, pltpu.roll(a, LANES // 2, a.ndim - 1), b)


def tile(index):
    return pl.ds(index * LANES, LANES)


def positions():
    table = []
    for x in range(4):
        for d in range(2):
            bit = {"a": (x + 1) // 2 % 2, "b": x // 2, "d": d}
            table.append([4 * bit[i] + 2 * bit[j] + bit[k] for i, j, k in ORDERS])
    return np.array(table, np.int32)


def piece_rows(index_ref, stream, position, base=0):
    piece = lax.bitwise_xor(index_ref[stream], position)
    return pl.ds(base + pl.multiple_of(piece * PIECES[stream], 16), PIECES[stream])


def split_pieces(index_ref, stream, whole_ref, base, keep_ref, send_ref):
    half = CHIPS // 2
    for k in range(half):
        keep_ref[k] = whole_ref[piece_rows(index_ref, stream, k, base), :]
        send_ref[k] = whole_ref[piece_rows(index_ref, stream, k + half, base), :].astype(send_ref.dtype)


def half_shapes(stream, kind):
    shape = (CHIPS // 2, PIECES[stream], LANES)
    return [jax.ShapeDtypeStruct(shape, jnp.float32), jax.ShapeDtypeStruct(shape, kind)]


def specs(vmem):
    return [pl.BlockSpec(memory_space=pltpu.SMEM)] + [pl.BlockSpec(memory_space=pltpu.VMEM)] * vmem


def split_kernel(x_ref, out_ref):
    for p in range(CHIPS):
        for j in range(STRIPES):
            out_ref[p, :, tile(j)] = x_ref[:, tile(TILES * j + p)]
        for m in range(STRIPES // 2):
            left = x_ref[:, tile(TILES * (2 * m) + CHIPS + p // 2)]
            right = x_ref[:, tile(TILES * (2 * m + 1) + CHIPS + p // 2)]
            out_ref[p, :, tile(STRIPES + m)] = halves(left, right, p % 2 == 0).astype(out_ref.dtype)


def split_columns(x):
    return pl.pallas_call(
        split_kernel,
        out_shape=jax.ShapeDtypeStruct((CHIPS, PANEL, WIDTH), x.dtype),
        compiler_params=pltpu.CompilerParams(vmem_limit_bytes=16 * MIB),
        name="split_columns",
    )(x)


def strip(j):
    below = (BLOCKS - 1 - j) * LANES
    start = LANES * sum(BLOCKS - 1 - i for i in range(j))
    return pl.ds(start, below)


def triangle(own_ref, ref, store_below, store_diagonal):
    for j in range(0, BLOCKS, 2):
        first = j * LANES
        part = lax.dot_general(
            own_ref[pl.ds(first, HALF - first), :],
            ref[pl.ds(first, 2 * LANES), :],
            (((1,), (1,)), ((), ())),
            preferred_element_type=jnp.float32,
        )
        for i in range(2):
            columns = part[i * LANES :, i * LANES : (i + 1) * LANES]
            store_diagonal(j + i, columns[:LANES])
            if j + i + 1 < BLOCKS:
                store_below(strip(j + i), columns[LANES:])


def iotas():
    return [lax.broadcasted_iota(jnp.int32, (LANES, LANES), axis) for axis in range(2)]


def own_gram_kernel(index_ref, own_ref, keep_ref, send_ref, diagonal_ref, whole_ref):
    def store_below(rows, value):
        whole_ref[rows, :] = value

    def store_diagonal(j, value):
        diagonal_ref[j] = value

    triangle(own_ref, own_ref, store_below, store_diagonal)
    split_pieces(index_ref, 0, whole_ref, 0, keep_ref, send_ref)


def own_gram(index, own):
    return pl.pallas_call(
        own_gram_kernel,
        in_specs=specs(1),
        out_shape=half_shapes(0, own.dtype) + [jax.ShapeDtypeStruct((BLOCKS, LANES, LANES), jnp.float32)],
        scratch_shapes=[pltpu.VMEM((BELOW, LANES), jnp.float32)],
        compiler_params=pltpu.CompilerParams(vmem_limit_bytes=8 * MIB),
        cost_estimate=pl.CostEstimate(
            flops=2 * (BELOW + 3 * HALF) * LANES * WIDTH, bytes_accessed=2 * HALF * WIDTH, transcendentals=0
        ),
        name="own_gram",
    )(index, own)


def cross_gram_kernel(
    index_ref, diagonal_ref, own_ref, other_ref, keep_b_ref, send_b_ref, keep_c_ref, send_c_ref, whole_ref
):
    row, column = iotas()
    edges = []

    def store_below(rows, value):
        whole_ref[rows, :] = value

    def store_diagonal(j, value):
        whole_ref[pl.ds(BELOW + j * LANES, LANES), :] = jnp.where(row >= column, diagonal_ref[j], value)
        edges.append(jnp.sum(jnp.where(row == column, value, 0.0), axis=0, keepdims=True))

    triangle(own_ref, other_ref, store_below, store_diagonal)
    rest = PACKED - EDGE
    edges.append(jnp.zeros((rest - BLOCKS, LANES), jnp.float32))
    whole_ref[pl.ds(EDGE - BELOW, rest), :] = jnp.concatenate(edges)
    split_pieces(index_ref, 1, whole_ref, BASES[1] - BELOW, keep_b_ref, send_b_ref)
    split_pieces(index_ref, 2, whole_ref, BASES[2] - BELOW, keep_c_ref, send_c_ref)


def cross_gram(index, diagonal, own, other):
    return pl.pallas_call(
        cross_gram_kernel,
        in_specs=specs(3),
        out_shape=half_shapes(1, own.dtype) + half_shapes(2, own.dtype),
        scratch_shapes=[pltpu.VMEM((PACKED - BELOW, LANES), jnp.float32)],
        compiler_params=pltpu.CompilerParams(vmem_limit_bytes=12 * MIB),
        cost_estimate=pl.CostEstimate(
            flops=2 * (BELOW + 3 * HALF) * LANES * WIDTH, bytes_accessed=4 * HALF * WIDTH, transcendentals=0
        ),
        name="cross_gram",
    )(index, diagonal, own, other)


def exchange(value, axis):
    if axis == "d":
        return lax.ppermute(value, "yh", [(0, 1), (1, 0)])
    return lax.ppermute(value, "x", [(i, i ^ 1 if axis == "a" else 3 - i) for i in range(4)])


def wide(value):
    return value.astype(jnp.float32)


def sum_over_chips(keep, arrived, order):
    kind = arrived.dtype
    half = keep + wide(arrived)
    quarter = half[:2] + wide(exchange(half[2:].astype(kind), order[1]))
    quarter = quarter.astype(kind)
    total = (wide(quarter) + wide(exchange(quarter, order[2]))[::-1]).astype(kind)
    half = jnp.concatenate([total, exchange(total, order[1])])
    return jnp.concatenate([half, exchange(half, order[0])])


def unpermute(index_ref, pieces_ref, packed_ref):
    first = 0
    for s, rows in enumerate(PIECES):
        for k in range(CHIPS):
            packed_ref[piece_rows(index_ref, s, k, BASES[s]), :] = pieces_ref[k, pl.ds(first, rows), :]
        first += rows


def mirror(packed_ref, out_ref, lower):
    for j in range(BLOCKS):
        first = j * LANES
        block = packed_ref[pl.ds(2 * BELOW + first, LANES), :]
        out_ref[pl.ds(first, LANES), tile(j)] = jnp.where(lower, block, block.T)
        if j + 1 < BLOCKS:
            below = packed_ref[strip(j), :]
            out_ref[pl.ds(first + LANES, below.shape[0]), tile(j)] = below
            out_ref[pl.ds(first, LANES), pl.ds(first + LANES, below.shape[0])] = below.T


def own_square_kernel(index_ref, pieces_ref, packed_ref, gram_ref, square_ref):
    row, column = iotas()
    unpermute(index_ref, pieces_ref, packed_ref)
    mirror(packed_ref, gram_ref, row >= column)
    for n in range(0, HALF, 256):
        columns = pl.ds(n, 256)
        square_ref[:, columns] = jnp.dot(gram_ref[...], gram_ref[:, columns], preferred_element_type=jnp.float32)


def own_square(index, pieces):
    return pl.pallas_call(
        own_square_kernel,
        in_specs=specs(1),
        out_shape=(
            jax.ShapeDtypeStruct((PACKED, LANES), pieces.dtype),
            jax.ShapeDtypeStruct((HALF, HALF), pieces.dtype),
            jax.ShapeDtypeStruct((HALF, HALF), jnp.float32),
        ),
        compiler_params=pltpu.CompilerParams(vmem_limit_bytes=12 * MIB),
        cost_estimate=pl.CostEstimate(
            flops=2 * HALF * HALF * HALF, bytes_accessed=8 * HALF * HALF, transcendentals=0
        ),
        name="own_square",
    )(index, pieces)


def unpack_cross(own_ref, other_ref, cross_ref):
    row, column = iotas()
    for j in range(BLOCKS):
        first = j * LANES
        upper, theirs = (ref[pl.ds(2 * BELOW + first, LANES), :] for ref in (own_ref, other_ref))
        edge = jnp.broadcast_to(own_ref[pl.ds(EDGE, 16), :].astype(jnp.float32)[j : j + 1], (LANES, LANES))
        block = jnp.where(row < column, upper.astype(jnp.float32), theirs.T.astype(jnp.float32))
        cross_ref[pl.ds(first, LANES), tile(j)] = jnp.where(row == column, edge, block).astype(cross_ref.dtype)
        if j + 1 < BLOCKS:
            rows = pl.ds(BELOW + strip(j).start, strip(j).size)
            cross_ref[pl.ds(first + LANES, rows.size), tile(j)] = own_ref[rows, :]
            cross_ref[pl.ds(first, LANES), pl.ds(first + LANES, rows.size)] = other_ref[rows, :].T


def update_kernel(
    index_ref, own_ref, pieces_ref, gram_ref, square_ref, x_ref, x_other_ref, out_ref,
    other_ref, cross_ref, gram_other_ref, mixing_ref,
):
    scale = math.sqrt(max(ROWS, COLS))
    step = 256
    row, column = iotas()
    unpermute(index_ref, pieces_ref, other_ref)
    unpack_cross(own_ref, other_ref, cross_ref)
    mirror(other_ref, gram_other_ref, row >= column)
    for n in range(0, HALF, step):
        columns = pl.ds(n, step)
        square = square_ref[:, columns] + lax.dot_general(
            cross_ref[...], cross_ref[columns, :], (((1,), (1,)), ((), ())), preferred_element_type=jnp.float32
        )
        gram = gram_ref[:, columns].astype(jnp.float32)
        mixing_ref[:, columns] = (coeff_b * gram + coeff_c * square).astype(mixing_ref.dtype)
    for n in range(0, HALF, step):
        columns = pl.ds(n, step)
        square = jnp.dot(gram_ref[...], cross_ref[:, columns], preferred_element_type=jnp.float32)
        square += jnp.dot(cross_ref[...], gram_other_ref[:, columns], preferred_element_type=jnp.float32)
        gram = cross_ref[:, columns].astype(jnp.float32)
        mixing_ref[:, pl.ds(HALF + n, step)] = (coeff_b * gram + coeff_c * square).astype(mixing_ref.dtype)
    for t in range(0, TILES, 2):
        columns = pl.ds(t * LANES, 2 * LANES)
        result = jnp.dot(mixing_ref[:, pl.ds(0, HALF)], x_ref[:, columns], preferred_element_type=jnp.float32)
        result += jnp.dot(mixing_ref[:, pl.ds(HALF, HALF)], x_other_ref[:, columns], preferred_element_type=jnp.float32)
        result = scale * (coeff_a * x_ref[:, columns].astype(jnp.float32) + result)
        for i in range(2):
            block = result[:, i * LANES : (i + 1) * LANES].reshape(CHIPS, PANEL, LANES)
            j = t + i
            if j < STRIPES:
                out_ref[j, :, pl.ds(0, PANEL), :] = block.astype(out_ref.dtype)
            else:
                top, bottom = block[:, : PANEL // 2], block[:, PANEL // 2 :]
                for side in range(2):
                    packed = halves(top, bottom, side == 0).astype(out_ref.dtype)
                    out_ref[2 * (j - STRIPES) + side, :, pl.ds(PANEL, PANEL // 2), :] = packed


def update_rows(index, *operands):
    kind = operands[0].dtype
    return pl.pallas_call(
        update_kernel,
        in_specs=specs(len(operands)),
        out_shape=jax.ShapeDtypeStruct((STRIPES, CHIPS, PANEL + PANEL // 2, LANES), kind),
        scratch_shapes=[
            pltpu.VMEM((PACKED, LANES), kind),
            pltpu.VMEM((HALF, HALF), kind),
            pltpu.VMEM((HALF, HALF), kind),
            pltpu.VMEM((HALF, ROWS), kind),
        ],
        compiler_params=pltpu.CompilerParams(vmem_limit_bytes=24 * MIB),
        cost_estimate=pl.CostEstimate(
            flops=4 * HALF * ROWS * ROWS - 2 * HALF * HALF * HALF, bytes_accessed=10 * HALF * ROWS, transcendentals=0
        ),
        name="update_rows",
    )(index, *operands)


def join_kernel(pieces_ref, out_ref, whole_ref, sems):
    copies = []
    for layer in range(STRIPES):
        for p in range(CHIPS):
            whole_ref[layer, :, tile(p)] = pieces_ref[layer, p, pl.ds(0, PANEL), :]
        for pair in range(CHIPS // 2):
            left = pieces_ref[layer, 2 * pair, pl.ds(PANEL, PANEL // 2), :]
            right = pieces_ref[layer, 2 * pair + 1, pl.ds(PANEL, PANEL // 2), :]
            for part in range(2):
                joined = halves(left, right, part == 0).astype(whole_ref.dtype)
                whole_ref[layer, pl.ds(part * PANEL // 2, PANEL // 2), tile(CHIPS + pair)] = joined
        copies.append(pltpu.make_async_copy(whole_ref.at[layer], out_ref.at[layer], sems.at[layer]))
        copies[-1].start()
    for copy in copies:
        copy.wait()


def join_columns(pieces):
    shape = (pieces.shape[0], PANEL, TILES * LANES)
    return pl.pallas_call(
        join_kernel,
        in_specs=[pl.BlockSpec(memory_space=pltpu.VMEM)],
        out_specs=pl.BlockSpec(memory_space=pl.ANY),
        out_shape=jax.ShapeDtypeStruct(shape, pieces.dtype),
        scratch_shapes=[pltpu.VMEM(shape, pieces.dtype), pltpu.SemaphoreType.DMA((pieces.shape[0],))],
        compiler_params=pltpu.CompilerParams(vmem_limit_bytes=12 * MIB),
        name="join_columns",
    )(pieces)


def swap_cores(value):
    return lax.ppermute(value, "c", [(0, 1), (1, 0)])


def shards(iterate):
    pieces = split_columns(iterate.reshape(PANEL, COLS))
    own = lax.all_to_all(pieces, CHIP_AXES, 0, 0, tiled=True).reshape(HALF, WIDTH)
    other = swap_cores(own)
    index = jnp.asarray(positions())[lax.axis_index(CHIP_AXES)]
    keep_a, send_a, diagonal = own_gram(index, own)
    arrived_a = exchange(send_a, ORDERS[0][0])
    keep_b, send_b, keep_c, send_c = cross_gram(index, diagonal, own, other)
    arrived = arrived_a, exchange(send_b, ORDERS[1][0]), exchange(send_c, ORDERS[2][0])
    arrived = lax.optimization_barrier(arrived)
    streams = [sum_over_chips(*stream) for stream in zip((keep_a, keep_b, keep_c), arrived, ORDERS)]
    pieces = jnp.concatenate(streams, axis=1)
    pieces_other = swap_cores(pieces)
    packed, gram, square = own_square(index, pieces)
    sent = update_rows(index, packed, pieces_other, gram, square, own, other)
    sent = sent.reshape(STRIPES * CHIPS, PANEL + PANEL // 2, LANES)
    received = lax.all_to_all(sent, ALL_CHIPS, 0, 0, tiled=True)
    return join_columns(received.reshape(STRIPES, CHIPS, PANEL + PANEL // 2, LANES))


def solution(mesh):
    fine = Mesh(mesh.devices.reshape(4, 2, 4, 2, 2), ("z", "yl", "x", "yh", "c"))
    return jax.shard_map(
        shards,
        mesh=fine,
        in_specs=(P(("z", "yl"), ("x", "yh", "c"), None),),
        out_specs=P(None, ("x", "yh", "c"), ("z", "yl")),
        check_vma=False,
    )
```

```python
import math

import jax
import jax.numpy as jnp
from jax import lax
from jax.experimental import pallas as pl
from jax.experimental.pallas import tpu as pltpu
from jax.sharding import Mesh, PartitionSpec as P

coeff_a = 3.4445
coeff_b = -4.775
coeff_c = 2.0315

ROWS = 1536
COLS = 12288
LANES = 128
CHIPS = 8
STRIPES = 8
PANEL = ROWS // (2 * CHIPS)
HALF = ROWS // 2
WIDTH = COLS // CHIPS
TILES = COLS // STRIPES // LANES
BLOCKS = HALF // LANES
BELOW = LANES * BLOCKS * (BLOCKS - 1) // 2
EDGE = 2 * BELOW + HALF
PACKED = -(-(EDGE + BLOCKS) // (16 * CHIPS)) * 16 * CHIPS
PIECES = (BELOW // CHIPS,) + ((PACKED - BELOW) // (2 * CHIPS),) * 2
BASES = (0, BELOW, BELOW + CHIPS * PIECES[1])
MIB = 1 << 20

CHIP_AXES = ("x", "yh")
ALL_CHIPS = ("z", "yl", "x", "yh")
ORDERS = ("abd", "bda", "dab")


def halves(a, b, first):
    a, b = a.astype(jnp.float32), b.astype(jnp.float32)
    low = lax.broadcasted_iota(jnp.int32, a.shape, a.ndim - 1) < LANES // 2
    if first:
        return jnp.where(low, a, pltpu.roll(b, LANES // 2, a.ndim - 1))
    return jnp.where(low, pltpu.roll(a, LANES // 2, a.ndim - 1), b)


def tile(index):
    return pl.ds(index * LANES, LANES)


def place(stream):
    x, d = lax.axis_index("x"), lax.axis_index("yh")
    bit = {"a": lax.rem((x + 1) // 2, 2), "b": x // 2, "d": d}
    first, second, third = (bit[axis] for axis in ORDERS[stream])
    return 4 * first + 2 * second + third


def piece_rows(stream, position, base=0):
    piece = lax.bitwise_xor(place(stream), position)
    return pl.ds(base + pl.multiple_of(piece * PIECES[stream], 16), PIECES[stream])


def split_pieces(stream, whole_ref, base, keep_ref, send_ref):
    half = CHIPS // 2
    for k in range(half):
        keep_ref[k] = whole_ref[piece_rows(stream, k, base), :]
        send_ref[k] = whole_ref[piece_rows(stream, k + half, base), :].astype(send_ref.dtype)


def half_shapes(stream, kind):
    shape = (CHIPS // 2, PIECES[stream], LANES)
    return [jax.ShapeDtypeStruct(shape, jnp.float32), jax.ShapeDtypeStruct(shape, kind)]


def split_kernel(x_ref, out_ref):
    for p in range(CHIPS):
        for j in range(STRIPES):
            out_ref[p, :, tile(j)] = x_ref[:, tile(TILES * j + p)]
        for m in range(STRIPES // 2):
            left = x_ref[:, tile(TILES * (2 * m) + CHIPS + p // 2)]
            right = x_ref[:, tile(TILES * (2 * m + 1) + CHIPS + p // 2)]
            out_ref[p, :, tile(STRIPES + m)] = halves(left, right, p % 2 == 0).astype(out_ref.dtype)


def split_columns(x):
    return pl.pallas_call(
        split_kernel,
        out_shape=jax.ShapeDtypeStruct((CHIPS, PANEL, WIDTH), x.dtype),
        compiler_params=pltpu.CompilerParams(vmem_limit_bytes=16 * MIB),
        name="split_columns",
    )(x)


def strip(j):
    below = (BLOCKS - 1 - j) * LANES
    start = LANES * sum(BLOCKS - 1 - i for i in range(j))
    return pl.ds(start, below)


def triangle(own_ref, ref, store_below, store_diagonal):
    for j in range(0, BLOCKS, 2):
        first = j * LANES
        part = lax.dot_general(
            own_ref[pl.ds(first, HALF - first), :],
            ref[pl.ds(first, 2 * LANES), :],
            (((1,), (1,)), ((), ())),
            preferred_element_type=jnp.float32,
        )
        for i in range(2):
            columns = part[i * LANES :, i * LANES : (i + 1) * LANES]
            store_diagonal(j + i, columns[:LANES])
            if j + i + 1 < BLOCKS:
                store_below(strip(j + i), columns[LANES:])


def iotas():
    return [lax.broadcasted_iota(jnp.int32, (LANES, LANES), axis) for axis in range(2)]


def own_gram_kernel(own_ref, keep_ref, send_ref, diagonal_ref, whole_ref):
    def store_below(rows, value):
        whole_ref[rows, :] = value

    def store_diagonal(j, value):
        diagonal_ref[j] = value

    triangle(own_ref, own_ref, store_below, store_diagonal)
    split_pieces(0, whole_ref, 0, keep_ref, send_ref)


def own_gram(own):
    return pl.pallas_call(
        own_gram_kernel,
        out_shape=half_shapes(0, own.dtype) + [jax.ShapeDtypeStruct((BLOCKS, LANES, LANES), jnp.float32)],
        scratch_shapes=[pltpu.VMEM((BELOW, LANES), jnp.float32)],
        compiler_params=pltpu.CompilerParams(vmem_limit_bytes=8 * MIB),
        cost_estimate=pl.CostEstimate(
            flops=2 * (BELOW + 3 * HALF) * LANES * WIDTH, bytes_accessed=2 * HALF * WIDTH, transcendentals=0
        ),
        name="own_gram",
    )(own)


def cross_gram_kernel(
    diagonal_ref, own_ref, other_ref, keep_b_ref, send_b_ref, keep_c_ref, send_c_ref, whole_ref
):
    row, column = iotas()
    edges = []

    def store_below(rows, value):
        whole_ref[rows, :] = value

    def store_diagonal(j, value):
        whole_ref[pl.ds(BELOW + j * LANES, LANES), :] = jnp.where(row >= column, diagonal_ref[j], value)
        edges.append(jnp.sum(jnp.where(row == column, value, 0.0), axis=0, keepdims=True))

    triangle(own_ref, other_ref, store_below, store_diagonal)
    rest = PACKED - EDGE
    edges.append(jnp.zeros((rest - BLOCKS, LANES), jnp.float32))
    whole_ref[pl.ds(EDGE - BELOW, rest), :] = jnp.concatenate(edges)
    split_pieces(1, whole_ref, BASES[1] - BELOW, keep_b_ref, send_b_ref)
    split_pieces(2, whole_ref, BASES[2] - BELOW, keep_c_ref, send_c_ref)


def cross_gram(diagonal, own, other):
    return pl.pallas_call(
        cross_gram_kernel,
        out_shape=half_shapes(1, own.dtype) + half_shapes(2, own.dtype),
        scratch_shapes=[pltpu.VMEM((PACKED - BELOW, LANES), jnp.float32)],
        compiler_params=pltpu.CompilerParams(vmem_limit_bytes=12 * MIB),
        cost_estimate=pl.CostEstimate(
            flops=2 * (BELOW + 3 * HALF) * LANES * WIDTH, bytes_accessed=4 * HALF * WIDTH, transcendentals=0
        ),
        name="cross_gram",
    )(diagonal, own, other)


def exchange(value, axis):
    if axis == "d":
        return lax.ppermute(value, "yh", [(0, 1), (1, 0)])
    return lax.ppermute(value, "x", [(i, i ^ 1 if axis == "a" else 3 - i) for i in range(4)])


def wide(value):
    return value.astype(jnp.float32)


def sum_over_chips(keep, arrived, order):
    kind = arrived.dtype
    half = (keep + wide(arrived)).astype(kind).reshape(2, 2, *keep.shape[1:])
    half = (wide(half) + wide(exchange(half, order[1]))[::-1]).astype(kind)
    half = (wide(half) + wide(exchange(half, order[2]))[:, ::-1]).astype(kind).reshape(arrived.shape)
    return jnp.concatenate([half, exchange(half, order[0])])


def unpermute(pieces_ref, packed_ref):
    first = 0
    for s, rows in enumerate(PIECES):
        for k in range(CHIPS):
            packed_ref[piece_rows(s, k, BASES[s]), :] = pieces_ref[k, pl.ds(first, rows), :]
        first += rows


def mirror(packed_ref, out_ref, lower):
    for j in range(BLOCKS):
        first = j * LANES
        block = packed_ref[pl.ds(2 * BELOW + first, LANES), :]
        out_ref[pl.ds(first, LANES), tile(j)] = jnp.where(lower, block, block.T)
        if j + 1 < BLOCKS:
            below = packed_ref[strip(j), :]
            out_ref[pl.ds(first + LANES, below.shape[0]), tile(j)] = below
            out_ref[pl.ds(first, LANES), pl.ds(first + LANES, below.shape[0])] = below.T


def own_square_kernel(pieces_ref, packed_ref, gram_ref, square_ref):
    row, column = iotas()
    unpermute(pieces_ref, packed_ref)
    mirror(packed_ref, gram_ref, row >= column)
    for n in range(0, HALF, 256):
        columns = pl.ds(n, 256)
        square_ref[:, columns] = jnp.dot(gram_ref[...], gram_ref[:, columns], preferred_element_type=jnp.float32)


def own_square(pieces):
    return pl.pallas_call(
        own_square_kernel,
        out_shape=(
            jax.ShapeDtypeStruct((PACKED, LANES), pieces.dtype),
            jax.ShapeDtypeStruct((HALF, HALF), pieces.dtype),
            jax.ShapeDtypeStruct((HALF, HALF), jnp.float32),
        ),
        compiler_params=pltpu.CompilerParams(vmem_limit_bytes=12 * MIB),
        cost_estimate=pl.CostEstimate(
            flops=2 * HALF * HALF * HALF, bytes_accessed=8 * HALF * HALF, transcendentals=0
        ),
        name="own_square",
    )(pieces)


def unpack_cross(own_ref, other_ref, cross_ref):
    row, column = iotas()
    for j in range(BLOCKS):
        first = j * LANES
        upper, theirs = (ref[pl.ds(2 * BELOW + first, LANES), :] for ref in (own_ref, other_ref))
        edge = jnp.broadcast_to(own_ref[pl.ds(EDGE, 16), :].astype(jnp.float32)[j : j + 1], (LANES, LANES))
        block = jnp.where(row < column, upper.astype(jnp.float32), theirs.T.astype(jnp.float32))
        cross_ref[pl.ds(first, LANES), tile(j)] = jnp.where(row == column, edge, block).astype(cross_ref.dtype)
        if j + 1 < BLOCKS:
            rows = pl.ds(BELOW + strip(j).start, strip(j).size)
            cross_ref[pl.ds(first + LANES, rows.size), tile(j)] = own_ref[rows, :]
            cross_ref[pl.ds(first, LANES), pl.ds(first + LANES, rows.size)] = other_ref[rows, :].T


def update_kernel(
    own_ref, pieces_ref, gram_ref, square_ref, x_ref, x_other_ref, out_ref,
    other_ref, cross_ref, gram_other_ref, mixing_ref,
):
    scale = math.sqrt(max(ROWS, COLS))
    step = 256
    row, column = iotas()
    unpermute(pieces_ref, other_ref)
    unpack_cross(own_ref, other_ref, cross_ref)
    mirror(other_ref, gram_other_ref, row >= column)
    for n in range(0, HALF, step):
        columns = pl.ds(n, step)
        square = square_ref[:, columns] + lax.dot_general(
            cross_ref[...], cross_ref[columns, :], (((1,), (1,)), ((), ())), preferred_element_type=jnp.float32
        )
        gram = gram_ref[:, columns].astype(jnp.float32)
        mixing_ref[:, columns] = (coeff_b * gram + coeff_c * square).astype(mixing_ref.dtype)
    for n in range(0, HALF, step):
        columns = pl.ds(n, step)
        square = jnp.dot(gram_ref[...], cross_ref[:, columns], preferred_element_type=jnp.float32)
        square += jnp.dot(cross_ref[...], gram_other_ref[:, columns], preferred_element_type=jnp.float32)
        gram = cross_ref[:, columns].astype(jnp.float32)
        mixing_ref[:, pl.ds(HALF + n, step)] = (coeff_b * gram + coeff_c * square).astype(mixing_ref.dtype)
    for t in range(0, TILES, 2):
        columns = pl.ds(t * LANES, 2 * LANES)
        result = jnp.dot(mixing_ref[:, pl.ds(0, HALF)], x_ref[:, columns], preferred_element_type=jnp.float32)
        result += jnp.dot(mixing_ref[:, pl.ds(HALF, HALF)], x_other_ref[:, columns], preferred_element_type=jnp.float32)
        result = scale * (coeff_a * x_ref[:, columns].astype(jnp.float32) + result)
        for i in range(2):
            block = result[:, i * LANES : (i + 1) * LANES].reshape(CHIPS, PANEL, LANES)
            j = t + i
            if j < STRIPES:
                out_ref[j, :, pl.ds(0, PANEL), :] = block.astype(out_ref.dtype)
            else:
                top, bottom = block[:, : PANEL // 2], block[:, PANEL // 2 :]
                for side in range(2):
                    packed = halves(top, bottom, side == 0).astype(out_ref.dtype)
                    out_ref[2 * (j - STRIPES) + side, :, pl.ds(PANEL, PANEL // 2), :] = packed


def update_rows(*operands):
    kind = operands[0].dtype
    return pl.pallas_call(
        update_kernel,
        out_shape=jax.ShapeDtypeStruct((STRIPES, CHIPS, PANEL + PANEL // 2, LANES), kind),
        scratch_shapes=[
            pltpu.VMEM((PACKED, LANES), kind),
            pltpu.VMEM((HALF, HALF), kind),
            pltpu.VMEM((HALF, HALF), kind),
            pltpu.VMEM((HALF, ROWS), kind),
        ],
        compiler_params=pltpu.CompilerParams(vmem_limit_bytes=24 * MIB),
        cost_estimate=pl.CostEstimate(
            flops=4 * HALF * ROWS * ROWS - 2 * HALF * HALF * HALF, bytes_accessed=10 * HALF * ROWS, transcendentals=0
        ),
        name="update_rows",
    )(*operands)


def join_kernel(pieces_ref, out_ref, whole_ref, sems):
    copies = []
    for layer in range(STRIPES):
        for p in range(CHIPS):
            whole_ref[layer, :, tile(p)] = pieces_ref[layer, p, pl.ds(0, PANEL), :]
        for pair in range(CHIPS // 2):
            left = pieces_ref[layer, 2 * pair, pl.ds(PANEL, PANEL // 2), :]
            right = pieces_ref[layer, 2 * pair + 1, pl.ds(PANEL, PANEL // 2), :]
            for part in range(2):
                joined = halves(left, right, part == 0).astype(whole_ref.dtype)
                whole_ref[layer, pl.ds(part * PANEL // 2, PANEL // 2), tile(CHIPS + pair)] = joined
        copies.append(pltpu.make_async_copy(whole_ref.at[layer], out_ref.at[layer], sems.at[layer]))
        copies[-1].start()
    for copy in copies:
        copy.wait()


def join_columns(pieces):
    shape = (pieces.shape[0], PANEL, TILES * LANES)
    return pl.pallas_call(
        join_kernel,
        in_specs=[pl.BlockSpec(memory_space=pltpu.VMEM)],
        out_specs=pl.BlockSpec(memory_space=pl.ANY),
        out_shape=jax.ShapeDtypeStruct(shape, pieces.dtype),
        scratch_shapes=[pltpu.VMEM(shape, pieces.dtype), pltpu.SemaphoreType.DMA((pieces.shape[0],))],
        compiler_params=pltpu.CompilerParams(vmem_limit_bytes=12 * MIB),
        name="join_columns",
    )(pieces)


def swap_cores(value):
    return lax.ppermute(value, "c", [(0, 1), (1, 0)])


def shards(iterate):
    pieces = split_columns(iterate.reshape(PANEL, COLS))
    own = lax.all_to_all(pieces, CHIP_AXES, 0, 0, tiled=True).reshape(HALF, WIDTH)
    other = swap_cores(own)
    keep_a, send_a, diagonal = own_gram(own)
    arrived_a = exchange(send_a, ORDERS[0][0])
    keep_b, send_b, keep_c, send_c = cross_gram(diagonal, own, other)
    arrived = arrived_a, exchange(send_b, ORDERS[1][0]), exchange(send_c, ORDERS[2][0])
    arrived = lax.optimization_barrier(arrived)
    streams = [sum_over_chips(*stream) for stream in zip((keep_a, keep_b, keep_c), arrived, ORDERS)]
    pieces = jnp.concatenate(streams, axis=1)
    pieces_other = swap_cores(pieces)
    packed, gram, square = own_square(pieces)
    sent = update_rows(packed, pieces_other, gram, square, own, other)
    sent = sent.reshape(STRIPES * CHIPS, PANEL + PANEL // 2, LANES)
    received = lax.all_to_all(sent, ALL_CHIPS, 0, 0, tiled=True)
    return join_columns(received.reshape(STRIPES, CHIPS, PANEL + PANEL // 2, LANES))


def solution(mesh):
    fine = Mesh(mesh.devices.reshape(4, 2, 4, 2, 2), ("z", "yl", "x", "yh", "c"))
    return jax.shard_map(
        shards,
        mesh=fine,
        in_specs=(P(("z", "yl"), ("x", "yh", "c"), None),),
        out_specs=P(None, ("x", "yh", "c"), ("z", "yl")),
        check_vma=False,
    )
```

```python
import math

import jax
import jax.numpy as jnp
from jax import lax
from jax.experimental import pallas as pl
from jax.experimental.pallas import tpu as pltpu
from jax.sharding import Mesh, PartitionSpec as P

coeff_a = 3.4445
coeff_b = -4.775
coeff_c = 2.0315

ROWS = 1536
COLS = 12288
LANES = 128
CHIPS = 8
STRIPES = 8
PANEL = ROWS // (2 * CHIPS)
HALF = ROWS // 2
WIDTH = COLS // CHIPS
TILES = COLS // STRIPES // LANES
BLOCKS = HALF // LANES
BELOW = LANES * BLOCKS * (BLOCKS - 1) // 2
EDGE = 2 * BELOW + HALF
PACKED = -(-(EDGE + BLOCKS) // (16 * CHIPS)) * 16 * CHIPS
PIECES = (208, 192, 192)
BASES = (0, CHIPS * PIECES[0], CHIPS * (PIECES[0] + PIECES[1]))
MIB = 1 << 20

CHIP_AXES = ("x", "yh")
ALL_CHIPS = ("z", "yl", "x", "yh")
ORDERS = ("abd", "bda", "dab")


def halves(a, b, first):
    a, b = a.astype(jnp.float32), b.astype(jnp.float32)
    low = lax.broadcasted_iota(jnp.int32, a.shape, a.ndim - 1) < LANES // 2
    if first:
        return jnp.where(low, a, pltpu.roll(b, LANES // 2, a.ndim - 1))
    return jnp.where(low, pltpu.roll(a, LANES // 2, a.ndim - 1), b)


def tile(index):
    return pl.ds(index * LANES, LANES)


def place(stream):
    x, d = lax.axis_index("x"), lax.axis_index("yh")
    bit = {"a": lax.rem((x + 1) // 2, 2), "b": x // 2, "d": d}
    first, second, third = (bit[axis] for axis in ORDERS[stream])
    return 4 * first + 2 * second + third


def piece_rows(stream, position, base=0):
    piece = lax.bitwise_xor(place(stream), position)
    return pl.ds(base + pl.multiple_of(piece * PIECES[stream], 16), PIECES[stream])


def split_pieces(stream, whole_ref, base, keep_ref, send_ref):
    half = CHIPS // 2
    for k in range(half):
        keep_ref[k] = whole_ref[piece_rows(stream, k, base), :]
        send_ref[k] = whole_ref[piece_rows(stream, k + half, base), :].astype(send_ref.dtype)


def half_shapes(stream, kind):
    shape = (CHIPS // 2, PIECES[stream], LANES)
    return [jax.ShapeDtypeStruct(shape, jnp.float32), jax.ShapeDtypeStruct(shape, kind)]


def split_kernel(x_ref, out_ref, whole_ref, sems):
    copies = [
        pltpu.make_async_copy(x_ref.at[pl.ds(r, 16)], whole_ref.at[pl.ds(r, 16)], sems.at[r // 16])
        for r in range(0, PANEL, 16)
    ]
    for copy in copies:
        copy.start()
    for r, copy in zip(range(0, PANEL, 16), copies):
        copy.wait()
        rows = pl.ds(r, 16)
        for p in range(CHIPS):
            for j in range(STRIPES):
                out_ref[p, rows, tile(j)] = whole_ref[rows, tile(TILES * j + p)]
            for m in range(STRIPES // 2):
                left = whole_ref[rows, tile(TILES * (2 * m) + CHIPS + p // 2)]
                right = whole_ref[rows, tile(TILES * (2 * m + 1) + CHIPS + p // 2)]
                out_ref[p, rows, tile(STRIPES + m)] = halves(left, right, p % 2 == 0).astype(out_ref.dtype)


def split_columns(x):
    return pl.pallas_call(
        split_kernel,
        in_specs=[pl.BlockSpec(memory_space=pltpu.HBM)],
        out_shape=jax.ShapeDtypeStruct((CHIPS, PANEL, WIDTH), x.dtype),
        scratch_shapes=[pltpu.VMEM(x.shape, x.dtype), pltpu.SemaphoreType.DMA((PANEL // 16,))],
        compiler_params=pltpu.CompilerParams(vmem_limit_bytes=57 * MIB),
        name="split_columns",
    )(x)


def strip(j):
    below = (BLOCKS - 1 - j) * LANES
    start = LANES * sum(BLOCKS - 1 - i for i in range(j))
    return pl.ds(start, below)


def triangle(own_ref, ref, store_below, store_diagonal):
    for j in range(0, BLOCKS, 2):
        first = j * LANES
        part = lax.dot_general(
            own_ref[pl.ds(first, HALF - first), :],
            ref[pl.ds(first, 2 * LANES), :],
            (((1,), (1,)), ((), ())),
            preferred_element_type=jnp.float32,
        )
        for i in range(2):
            columns = part[i * LANES :, i * LANES : (i + 1) * LANES]
            store_diagonal(j + i, columns[:LANES])
            if j + i + 1 < BLOCKS:
                store_below(strip(j + i), columns[LANES:])


def iotas():
    return [lax.broadcasted_iota(jnp.int32, (LANES, LANES), axis) for axis in range(2)]


def own_gram_kernel(own_ref, keep_ref, send_ref, rest_ref, diagonal_ref, whole_ref):
    def store_below(rows, value):
        whole_ref[rows, :] = value

    def store_diagonal(j, value):
        diagonal_ref[j] = value

    triangle(own_ref, own_ref, store_below, store_diagonal)
    split_pieces(0, whole_ref, 0, keep_ref, send_ref)
    rest_ref[...] = whole_ref[pl.ds(BASES[1], BELOW - BASES[1]), :]


def own_gram(own):
    return pl.pallas_call(
        own_gram_kernel,
        out_shape=half_shapes(0, own.dtype)
        + [
            jax.ShapeDtypeStruct((BELOW - BASES[1], LANES), jnp.float32),
            jax.ShapeDtypeStruct((BLOCKS, LANES, LANES), jnp.float32),
        ],
        scratch_shapes=[pltpu.VMEM((BELOW, LANES), jnp.float32)],
        compiler_params=pltpu.CompilerParams(vmem_limit_bytes=8 * MIB),
        cost_estimate=pl.CostEstimate(
            flops=2 * (BELOW + 3 * HALF) * LANES * WIDTH, bytes_accessed=2 * HALF * WIDTH, transcendentals=0
        ),
        name="own_gram",
    )(own)


def cross_gram_kernel(
    rest_ref, diagonal_ref, own_ref, other_ref, keep_b_ref, send_b_ref, keep_c_ref, send_c_ref, whole_ref
):
    start = BELOW - BASES[1]
    whole_ref[pl.ds(0, start), :] = rest_ref[...]
    row, column = iotas()
    edges = []

    def store_below(rows, value):
        whole_ref[pl.ds(start + rows.start, rows.size), :] = value

    def store_diagonal(j, value):
        whole_ref[pl.ds(start + BELOW + j * LANES, LANES), :] = jnp.where(row >= column, diagonal_ref[j], value)
        edges.append(jnp.sum(jnp.where(row == column, value, 0.0), axis=0, keepdims=True))

    triangle(own_ref, other_ref, store_below, store_diagonal)
    edges.append(jnp.zeros((PACKED - EDGE - BLOCKS, LANES), jnp.float32))
    whole_ref[pl.ds(EDGE - BASES[1], PACKED - EDGE), :] = jnp.concatenate(edges)
    split_pieces(1, whole_ref, 0, keep_b_ref, send_b_ref)
    split_pieces(2, whole_ref, BASES[2] - BASES[1], keep_c_ref, send_c_ref)


def cross_gram(rest, diagonal, own, other):
    return pl.pallas_call(
        cross_gram_kernel,
        out_shape=half_shapes(1, own.dtype) + half_shapes(2, own.dtype),
        scratch_shapes=[pltpu.VMEM((PACKED - BASES[1], LANES), jnp.float32)],
        compiler_params=pltpu.CompilerParams(vmem_limit_bytes=12 * MIB),
        cost_estimate=pl.CostEstimate(
            flops=2 * (BELOW + 3 * HALF) * LANES * WIDTH, bytes_accessed=4 * HALF * WIDTH, transcendentals=0
        ),
        name="cross_gram",
    )(rest, diagonal, own, other)


def exchange(value, axis):
    if axis == "d":
        return lax.ppermute(value, "yh", [(0, 1), (1, 0)])
    return lax.ppermute(value, "x", [(i, i ^ 1 if axis == "a" else 3 - i) for i in range(4)])


def wide(value):
    return value.astype(jnp.float32)


def sum_over_chips(keep, arrived, order):
    kind = arrived.dtype
    half = (keep + wide(arrived)).astype(kind).reshape(2, 2, *keep.shape[1:])
    half = (wide(half) + wide(exchange(half, order[1]))[::-1]).astype(kind)
    half = (wide(half) + wide(exchange(half, order[2]))[:, ::-1]).astype(kind).reshape(arrived.shape)
    return jnp.concatenate([half, exchange(half, order[0])])


def unpermute(pieces_ref, packed_ref):
    first = 0
    for s, rows in enumerate(PIECES):
        for k in range(CHIPS):
            packed_ref[piece_rows(s, k, BASES[s]), :] = pieces_ref[k, pl.ds(first, rows), :]
        first += rows


def mirror(packed_ref, out_ref, lower):
    for j in range(BLOCKS):
        first = j * LANES
        block = packed_ref[pl.ds(2 * BELOW + first, LANES), :]
        out_ref[pl.ds(first, LANES), tile(j)] = jnp.where(lower, block, block.T)
        if j + 1 < BLOCKS:
            below = packed_ref[strip(j), :]
            out_ref[pl.ds(first + LANES, below.shape[0]), tile(j)] = below
            out_ref[pl.ds(first, LANES), pl.ds(first + LANES, below.shape[0])] = below.T


def own_square_kernel(pieces_ref, packed_ref, gram_ref, square_ref):
    row, column = iotas()
    unpermute(pieces_ref, packed_ref)
    mirror(packed_ref, gram_ref, row >= column)
    for n in range(0, HALF, 256):
        columns = pl.ds(n, 256)
        square_ref[:, columns] = jnp.dot(gram_ref[...], gram_ref[:, columns], preferred_element_type=jnp.float32)


def own_square(pieces):
    return pl.pallas_call(
        own_square_kernel,
        out_shape=(
            jax.ShapeDtypeStruct((PACKED, LANES), pieces.dtype),
            jax.ShapeDtypeStruct((HALF, HALF), pieces.dtype),
            jax.ShapeDtypeStruct((HALF, HALF), jnp.float32),
        ),
        compiler_params=pltpu.CompilerParams(vmem_limit_bytes=12 * MIB),
        cost_estimate=pl.CostEstimate(
            flops=2 * HALF * HALF * HALF, bytes_accessed=8 * HALF * HALF, transcendentals=0
        ),
        name="own_square",
    )(pieces)


def unpack_cross(own_ref, other_ref, cross_ref):
    row, column = iotas()
    for j in range(BLOCKS):
        first = j * LANES
        upper, theirs = (ref[pl.ds(2 * BELOW + first, LANES), :] for ref in (own_ref, other_ref))
        edge = jnp.broadcast_to(own_ref[pl.ds(EDGE, 16), :].astype(jnp.float32)[j : j + 1], (LANES, LANES))
        block = jnp.where(row < column, upper.astype(jnp.float32), theirs.T.astype(jnp.float32))
        cross_ref[pl.ds(first, LANES), tile(j)] = jnp.where(row == column, edge, block).astype(cross_ref.dtype)
        if j + 1 < BLOCKS:
            rows = pl.ds(BELOW + strip(j).start, strip(j).size)
            cross_ref[pl.ds(first + LANES, rows.size), tile(j)] = own_ref[rows, :]
            cross_ref[pl.ds(first, LANES), pl.ds(first + LANES, rows.size)] = other_ref[rows, :].T


def update_kernel(
    own_ref, pieces_ref, gram_ref, square_ref, x_ref, x_other_ref, out_ref,
    other_ref, cross_ref, gram_other_ref, mixing_ref,
):
    scale = math.sqrt(max(ROWS, COLS))
    step = 256
    row, column = iotas()
    unpermute(pieces_ref, other_ref)
    unpack_cross(own_ref, other_ref, cross_ref)
    mirror(other_ref, gram_other_ref, row >= column)
    for n in range(0, HALF, step):
        columns = pl.ds(n, step)
        square = square_ref[:, columns] + lax.dot_general(
            cross_ref[...], cross_ref[columns, :], (((1,), (1,)), ((), ())), preferred_element_type=jnp.float32
        )
        gram = gram_ref[:, columns].astype(jnp.float32)
        mixing_ref[:, columns] = (coeff_b * gram + coeff_c * square).astype(mixing_ref.dtype)
    for n in range(0, HALF, step):
        columns = pl.ds(n, step)
        square = jnp.dot(gram_ref[...], cross_ref[:, columns], preferred_element_type=jnp.float32)
        square += jnp.dot(cross_ref[...], gram_other_ref[:, columns], preferred_element_type=jnp.float32)
        gram = cross_ref[:, columns].astype(jnp.float32)
        mixing_ref[:, pl.ds(HALF + n, step)] = (coeff_b * gram + coeff_c * square).astype(mixing_ref.dtype)
    for t in range(0, TILES, 2):
        columns = pl.ds(t * LANES, 2 * LANES)
        result = jnp.dot(mixing_ref[:, pl.ds(0, HALF)], x_ref[:, columns], preferred_element_type=jnp.float32)
        result += jnp.dot(mixing_ref[:, pl.ds(HALF, HALF)], x_other_ref[:, columns], preferred_element_type=jnp.float32)
        result = scale * (coeff_a * x_ref[:, columns].astype(jnp.float32) + result)
        for i in range(2):
            block = result[:, i * LANES : (i + 1) * LANES].reshape(CHIPS, PANEL, LANES)
            j = t + i
            if j < STRIPES:
                out_ref[j, :, pl.ds(0, PANEL), :] = block.astype(out_ref.dtype)
            else:
                top, bottom = block[:, : PANEL // 2], block[:, PANEL // 2 :]
                for side in range(2):
                    packed = halves(top, bottom, side == 0).astype(out_ref.dtype)
                    out_ref[2 * (j - STRIPES) + side, :, pl.ds(PANEL, PANEL // 2), :] = packed


def update_rows(*operands):
    kind = operands[0].dtype
    return pl.pallas_call(
        update_kernel,
        out_shape=jax.ShapeDtypeStruct((STRIPES, CHIPS, PANEL + PANEL // 2, LANES), kind),
        scratch_shapes=[
            pltpu.VMEM((PACKED, LANES), kind),
            pltpu.VMEM((HALF, HALF), kind),
            pltpu.VMEM((HALF, HALF), kind),
            pltpu.VMEM((HALF, ROWS), kind),
        ],
        compiler_params=pltpu.CompilerParams(vmem_limit_bytes=24 * MIB),
        cost_estimate=pl.CostEstimate(
            flops=4 * HALF * ROWS * ROWS - 2 * HALF * HALF * HALF, bytes_accessed=10 * HALF * ROWS, transcendentals=0
        ),
        name="update_rows",
    )(*operands)


def join_kernel(pieces_ref, out_ref, whole_ref, sems):
    copies = []
    for layer in range(STRIPES):
        for p in range(CHIPS):
            whole_ref[layer, :, tile(p)] = pieces_ref[layer, p, pl.ds(0, PANEL), :]
        for pair in range(CHIPS // 2):
            left = pieces_ref[layer, 2 * pair, pl.ds(PANEL, PANEL // 2), :]
            right = pieces_ref[layer, 2 * pair + 1, pl.ds(PANEL, PANEL // 2), :]
            for part in range(2):
                joined = halves(left, right, part == 0).astype(whole_ref.dtype)
                whole_ref[layer, pl.ds(part * PANEL // 2, PANEL // 2), tile(CHIPS + pair)] = joined
        copies.append(pltpu.make_async_copy(whole_ref.at[layer], out_ref.at[layer], sems.at[layer]))
        copies[-1].start()
    for copy in copies:
        copy.wait()


def join_columns(pieces):
    shape = (pieces.shape[0], PANEL, TILES * LANES)
    return pl.pallas_call(
        join_kernel,
        in_specs=[pl.BlockSpec(memory_space=pltpu.VMEM)],
        out_specs=pl.BlockSpec(memory_space=pl.ANY),
        out_shape=jax.ShapeDtypeStruct(shape, pieces.dtype),
        scratch_shapes=[pltpu.VMEM(shape, pieces.dtype), pltpu.SemaphoreType.DMA((pieces.shape[0],))],
        compiler_params=pltpu.CompilerParams(vmem_limit_bytes=12 * MIB),
        name="join_columns",
    )(pieces)


def swap_cores(value):
    return lax.ppermute(value, "c", [(0, 1), (1, 0)])


def shards(iterate):
    pieces = split_columns(iterate.reshape(PANEL, COLS))
    own = lax.all_to_all(pieces, CHIP_AXES, 0, 0, tiled=True).reshape(HALF, WIDTH)
    other = swap_cores(own)
    keep_a, send_a, *rest = own_gram(own)
    arrived_a = exchange(send_a, ORDERS[0][0])
    keep_b, send_b, keep_c, send_c = cross_gram(*rest, own, other)
    arrived = arrived_a, exchange(send_b, ORDERS[1][0]), exchange(send_c, ORDERS[2][0])
    arrived = lax.optimization_barrier(arrived)
    streams = [sum_over_chips(*stream) for stream in zip((keep_a, keep_b, keep_c), arrived, ORDERS)]
    pieces = jnp.concatenate(streams, axis=1)
    pieces_other = swap_cores(pieces)
    packed, gram, square = own_square(pieces)
    sent = update_rows(packed, pieces_other, gram, square, own, other)
    sent = sent.reshape(STRIPES * CHIPS, PANEL + PANEL // 2, LANES)
    received = lax.all_to_all(sent, ALL_CHIPS, 0, 0, tiled=True)
    return join_columns(received.reshape(STRIPES, CHIPS, PANEL + PANEL // 2, LANES))


def solution(mesh):
    fine = Mesh(mesh.devices.reshape(4, 2, 4, 2, 2), ("z", "yl", "x", "yh", "c"))
    return jax.shard_map(
        shards,
        mesh=fine,
        in_specs=(P(("z", "yl"), ("x", "yh", "c"), None),),
        out_specs=P(None, ("x", "yh", "c"), ("z", "yl")),
        check_vma=False,
    )
```

```python
import math

import jax
import jax.numpy as jnp
from jax import lax
from jax.experimental import pallas as pl
from jax.experimental.pallas import tpu as pltpu
from jax.sharding import Mesh, PartitionSpec as P

coeff_a = 3.4445
coeff_b = -4.775
coeff_c = 2.0315

ROWS = 1536
COLS = 12288
LANES = 128
CHIPS = 8
STRIPES = 8
PANEL = ROWS // (2 * CHIPS)
HALF = ROWS // 2
WIDTH = COLS // CHIPS
TILES = COLS // STRIPES // LANES
BLOCKS = HALF // LANES
BELOW = LANES * BLOCKS * (BLOCKS - 1) // 2
EDGE = 2 * BELOW + HALF
PACKED = -(-(EDGE + BLOCKS) // (16 * CHIPS)) * 16 * CHIPS
PIECES = (208, 192, 192)
BASES = (0, CHIPS * PIECES[0], CHIPS * (PIECES[0] + PIECES[1]))
MIB = 1 << 20

CHIP_AXES = ("x", "yh")
ALL_CHIPS = ("z", "yl", "x", "yh")
ORDERS = (("abd", "bda", "dab"), ("bda", "dab", "abd"))


def halves(a, b, first):
    a, b = a.astype(jnp.float32), b.astype(jnp.float32)
    low = lax.broadcasted_iota(jnp.int32, a.shape, a.ndim - 1) < LANES // 2
    if first:
        return jnp.where(low, a, pltpu.roll(b, LANES // 2, a.ndim - 1))
    return jnp.where(low, pltpu.roll(a, LANES // 2, a.ndim - 1), b)


def tile(index):
    return pl.ds(index * LANES, LANES)


def place(stream, core):
    x, d = lax.axis_index("x"), lax.axis_index("yh")
    bit = {"a": lax.rem((x + 1) // 2, 2), "b": x // 2, "d": d}
    places = [4 * bit[i] + 2 * bit[j] + bit[k] for i, j, k in (orders[stream] for orders in ORDERS)]
    return places[0] + core * (places[1] - places[0])


def piece_rows(stream, position, base, core):
    piece = lax.bitwise_xor(place(stream, core), position)
    return pl.ds(base + pl.multiple_of(piece * PIECES[stream], 16), PIECES[stream])


def split_pieces(stream, whole_ref, base, keep_ref, send_ref):
    half, core = CHIPS // 2, lax.axis_index("c")
    for k in range(half):
        keep_ref[k] = whole_ref[piece_rows(stream, k, base, core), :]
        send_ref[k] = whole_ref[piece_rows(stream, k + half, base, core), :].astype(send_ref.dtype)


def half_shapes(stream, kind):
    shape = (CHIPS // 2, PIECES[stream], LANES)
    return [jax.ShapeDtypeStruct(shape, jnp.float32), jax.ShapeDtypeStruct(shape, kind)]


def split_kernel(x_ref, out_ref):
    for p in range(CHIPS):
        for j in range(STRIPES):
            out_ref[p, :, tile(j)] = x_ref[:, tile(TILES * j + p)]
        for m in range(STRIPES // 2):
            left = x_ref[:, tile(TILES * (2 * m) + CHIPS + p // 2)]
            right = x_ref[:, tile(TILES * (2 * m + 1) + CHIPS + p // 2)]
            out_ref[p, :, tile(STRIPES + m)] = halves(left, right, p % 2 == 0).astype(out_ref.dtype)


def split_columns(x):
    return pl.pallas_call(
        split_kernel,
        out_shape=jax.ShapeDtypeStruct((CHIPS, PANEL, WIDTH), x.dtype),
        compiler_params=pltpu.CompilerParams(vmem_limit_bytes=16 * MIB),
        name="split_columns",
    )(x)


def strip(j):
    below = (BLOCKS - 1 - j) * LANES
    start = LANES * sum(BLOCKS - 1 - i for i in range(j))
    return pl.ds(start, below)


def triangle(own_ref, ref, store_below, store_diagonal):
    for j in range(0, BLOCKS, 2):
        first = j * LANES
        part = lax.dot_general(
            own_ref[pl.ds(first, HALF - first), :],
            ref[pl.ds(first, 2 * LANES), :],
            (((1,), (1,)), ((), ())),
            preferred_element_type=jnp.float32,
        )
        for i in range(2):
            columns = part[i * LANES :, i * LANES : (i + 1) * LANES]
            store_diagonal(j + i, columns[:LANES])
            if j + i + 1 < BLOCKS:
                store_below(strip(j + i), columns[LANES:])


def iotas():
    return [lax.broadcasted_iota(jnp.int32, (LANES, LANES), axis) for axis in range(2)]


def own_gram_kernel(own_ref, keep_ref, send_ref, rest_ref, diagonal_ref, whole_ref):
    def store_below(rows, value):
        whole_ref[rows, :] = value

    def store_diagonal(j, value):
        diagonal_ref[j] = value

    triangle(own_ref, own_ref, store_below, store_diagonal)
    split_pieces(0, whole_ref, 0, keep_ref, send_ref)
    rest_ref[...] = whole_ref[pl.ds(BASES[1], BELOW - BASES[1]), :]


def own_gram(own):
    return pl.pallas_call(
        own_gram_kernel,
        out_shape=half_shapes(0, own.dtype)
        + [
            jax.ShapeDtypeStruct((BELOW - BASES[1], LANES), jnp.float32),
            jax.ShapeDtypeStruct((BLOCKS, LANES, LANES), jnp.float32),
        ],
        scratch_shapes=[pltpu.VMEM((BELOW, LANES), jnp.float32)],
        compiler_params=pltpu.CompilerParams(vmem_limit_bytes=8 * MIB),
        cost_estimate=pl.CostEstimate(
            flops=2 * (BELOW + 3 * HALF) * LANES * WIDTH, bytes_accessed=2 * HALF * WIDTH, transcendentals=0
        ),
        name="own_gram",
    )(own)


def cross_gram_kernel(
    rest_ref, diagonal_ref, own_ref, other_ref, keep_b_ref, send_b_ref, keep_c_ref, send_c_ref, whole_ref
):
    start = BELOW - BASES[1]
    whole_ref[pl.ds(0, start), :] = rest_ref[...]
    row, column = iotas()
    edges = []

    def store_below(rows, value):
        whole_ref[pl.ds(start + rows.start, rows.size), :] = value

    def store_diagonal(j, value):
        whole_ref[pl.ds(start + BELOW + j * LANES, LANES), :] = jnp.where(row >= column, diagonal_ref[j], value)
        edges.append(jnp.sum(jnp.where(row == column, value, 0.0), axis=0, keepdims=True))

    triangle(own_ref, other_ref, store_below, store_diagonal)
    edges.append(jnp.zeros((PACKED - EDGE - BLOCKS, LANES), jnp.float32))
    whole_ref[pl.ds(EDGE - BASES[1], PACKED - EDGE), :] = jnp.concatenate(edges)
    split_pieces(1, whole_ref, 0, keep_b_ref, send_b_ref)
    split_pieces(2, whole_ref, BASES[2] - BASES[1], keep_c_ref, send_c_ref)


def cross_gram(rest, diagonal, own, other):
    return pl.pallas_call(
        cross_gram_kernel,
        out_shape=half_shapes(1, own.dtype) + half_shapes(2, own.dtype),
        scratch_shapes=[pltpu.VMEM((PACKED - BASES[1], LANES), jnp.float32)],
        compiler_params=pltpu.CompilerParams(vmem_limit_bytes=12 * MIB),
        cost_estimate=pl.CostEstimate(
            flops=2 * (BELOW + 3 * HALF) * LANES * WIDTH, bytes_accessed=4 * HALF * WIDTH, transcendentals=0
        ),
        name="cross_gram",
    )(rest, diagonal, own, other)


def exchange(value, stream, hop):
    pairs = []
    for x in range(4):
        for d in range(2):
            for core in range(2):
                axis = ORDERS[core][stream][hop]
                to = {"a": (x ^ 1, d), "b": (3 - x, d), "d": (x, 1 - d)}[axis]
                pairs.append((4 * x + 2 * d + core, 4 * to[0] + 2 * to[1] + core))
    return lax.ppermute(value, ("x", "yh", "c"), pairs)


def wide(value):
    return value.astype(jnp.float32)


def sum_over_chips(stream, keep, arrived):
    kind = arrived.dtype
    half = (keep + wide(arrived)).astype(kind).reshape(2, 2, *keep.shape[1:])
    half = (wide(half) + wide(exchange(half, stream, 1))[::-1]).astype(kind)
    half = (wide(half) + wide(exchange(half, stream, 2))[:, ::-1]).astype(kind).reshape(arrived.shape)
    return jnp.concatenate([half, exchange(half, stream, 0)])


def unpermute(pieces_ref, packed_ref, core):
    first = 0
    for s, rows in enumerate(PIECES):
        for k in range(CHIPS):
            packed_ref[piece_rows(s, k, BASES[s], core), :] = pieces_ref[k, pl.ds(first, rows), :]
        first += rows


def mirror(packed_ref, out_ref, lower):
    for j in range(BLOCKS):
        first = j * LANES
        block = packed_ref[pl.ds(2 * BELOW + first, LANES), :]
        out_ref[pl.ds(first, LANES), tile(j)] = jnp.where(lower, block, block.T)
        if j + 1 < BLOCKS:
            below = packed_ref[strip(j), :]
            out_ref[pl.ds(first + LANES, below.shape[0]), tile(j)] = below
            out_ref[pl.ds(first, LANES), pl.ds(first + LANES, below.shape[0])] = below.T


def own_square_kernel(pieces_ref, packed_ref, gram_ref, square_ref):
    row, column = iotas()
    unpermute(pieces_ref, packed_ref, lax.axis_index("c"))
    mirror(packed_ref, gram_ref, row >= column)
    for n in range(0, HALF, 256):
        columns = pl.ds(n, 256)
        square_ref[:, columns] = jnp.dot(gram_ref[...], gram_ref[:, columns], preferred_element_type=jnp.float32)


def own_square(pieces):
    return pl.pallas_call(
        own_square_kernel,
        out_shape=(
            jax.ShapeDtypeStruct((PACKED, LANES), pieces.dtype),
            jax.ShapeDtypeStruct((HALF, HALF), pieces.dtype),
            jax.ShapeDtypeStruct((HALF, HALF), jnp.float32),
        ),
        compiler_params=pltpu.CompilerParams(vmem_limit_bytes=12 * MIB),
        cost_estimate=pl.CostEstimate(
            flops=2 * HALF * HALF * HALF, bytes_accessed=8 * HALF * HALF, transcendentals=0
        ),
        name="own_square",
    )(pieces)


def unpack_cross(own_ref, other_ref, cross_ref):
    row, column = iotas()
    for j in range(BLOCKS):
        first = j * LANES
        upper, theirs = (ref[pl.ds(2 * BELOW + first, LANES), :] for ref in (own_ref, other_ref))
        edge = jnp.broadcast_to(own_ref[pl.ds(EDGE, 16), :].astype(jnp.float32)[j : j + 1], (LANES, LANES))
        block = jnp.where(row < column, upper.astype(jnp.float32), theirs.T.astype(jnp.float32))
        cross_ref[pl.ds(first, LANES), tile(j)] = jnp.where(row == column, edge, block).astype(cross_ref.dtype)
        if j + 1 < BLOCKS:
            rows = pl.ds(BELOW + strip(j).start, strip(j).size)
            cross_ref[pl.ds(first + LANES, rows.size), tile(j)] = own_ref[rows, :]
            cross_ref[pl.ds(first, LANES), pl.ds(first + LANES, rows.size)] = other_ref[rows, :].T


def update_kernel(
    own_ref, pieces_ref, gram_ref, square_ref, x_ref, x_other_ref, out_ref,
    other_ref, cross_ref, gram_other_ref, mixing_ref,
):
    scale = math.sqrt(max(ROWS, COLS))
    step = 256
    row, column = iotas()
    unpermute(pieces_ref, other_ref, 1 - lax.axis_index("c"))
    unpack_cross(own_ref, other_ref, cross_ref)
    mirror(other_ref, gram_other_ref, row >= column)
    for n in range(0, HALF, step):
        columns = pl.ds(n, step)
        square = square_ref[:, columns] + lax.dot_general(
            cross_ref[...], cross_ref[columns, :], (((1,), (1,)), ((), ())), preferred_element_type=jnp.float32
        )
        gram = gram_ref[:, columns].astype(jnp.float32)
        mixing_ref[:, columns] = (coeff_b * gram + coeff_c * square).astype(mixing_ref.dtype)
    for n in range(0, HALF, step):
        columns = pl.ds(n, step)
        square = jnp.dot(gram_ref[...], cross_ref[:, columns], preferred_element_type=jnp.float32)
        square += jnp.dot(cross_ref[...], gram_other_ref[:, columns], preferred_element_type=jnp.float32)
        gram = cross_ref[:, columns].astype(jnp.float32)
        mixing_ref[:, pl.ds(HALF + n, step)] = (coeff_b * gram + coeff_c * square).astype(mixing_ref.dtype)
    for t in range(0, TILES, 2):
        columns = pl.ds(t * LANES, 2 * LANES)
        result = jnp.dot(mixing_ref[:, pl.ds(0, HALF)], x_ref[:, columns], preferred_element_type=jnp.float32)
        result += jnp.dot(mixing_ref[:, pl.ds(HALF, HALF)], x_other_ref[:, columns], preferred_element_type=jnp.float32)
        result = scale * (coeff_a * x_ref[:, columns].astype(jnp.float32) + result)
        for i in range(2):
            block = result[:, i * LANES : (i + 1) * LANES].reshape(CHIPS, PANEL, LANES)
            j = t + i
            if j < STRIPES:
                out_ref[j, :, pl.ds(0, PANEL), :] = block.astype(out_ref.dtype)
            else:
                top, bottom = block[:, : PANEL // 2], block[:, PANEL // 2 :]
                for side in range(2):
                    packed = halves(top, bottom, side == 0).astype(out_ref.dtype)
                    out_ref[2 * (j - STRIPES) + side, :, pl.ds(PANEL, PANEL // 2), :] = packed


def update_rows(*operands):
    kind = operands[0].dtype
    return pl.pallas_call(
        update_kernel,
        out_shape=jax.ShapeDtypeStruct((STRIPES, CHIPS, PANEL + PANEL // 2, LANES), kind),
        scratch_shapes=[
            pltpu.VMEM((PACKED, LANES), kind),
            pltpu.VMEM((HALF, HALF), kind),
            pltpu.VMEM((HALF, HALF), kind),
            pltpu.VMEM((HALF, ROWS), kind),
        ],
        compiler_params=pltpu.CompilerParams(vmem_limit_bytes=24 * MIB),
        cost_estimate=pl.CostEstimate(
            flops=4 * HALF * ROWS * ROWS - 2 * HALF * HALF * HALF, bytes_accessed=10 * HALF * ROWS, transcendentals=0
        ),
        name="update_rows",
    )(*operands)


def join_kernel(pieces_ref, out_ref, whole_ref, sems):
    copies = []
    for layer in range(STRIPES):
        for p in range(CHIPS):
            whole_ref[layer, :, tile(p)] = pieces_ref[layer, p, pl.ds(0, PANEL), :]
        for pair in range(CHIPS // 2):
            left = pieces_ref[layer, 2 * pair, pl.ds(PANEL, PANEL // 2), :]
            right = pieces_ref[layer, 2 * pair + 1, pl.ds(PANEL, PANEL // 2), :]
            for part in range(2):
                joined = halves(left, right, part == 0).astype(whole_ref.dtype)
                whole_ref[layer, pl.ds(part * PANEL // 2, PANEL // 2), tile(CHIPS + pair)] = joined
        copies.append(pltpu.make_async_copy(whole_ref.at[layer], out_ref.at[layer], sems.at[layer]))
        copies[-1].start()
    for copy in copies:
        copy.wait()


def join_columns(pieces):
    shape = (pieces.shape[0], PANEL, TILES * LANES)
    return pl.pallas_call(
        join_kernel,
        in_specs=[pl.BlockSpec(memory_space=pltpu.VMEM)],
        out_specs=pl.BlockSpec(memory_space=pl.ANY),
        out_shape=jax.ShapeDtypeStruct(shape, pieces.dtype),
        scratch_shapes=[pltpu.VMEM(shape, pieces.dtype), pltpu.SemaphoreType.DMA((pieces.shape[0],))],
        compiler_params=pltpu.CompilerParams(vmem_limit_bytes=12 * MIB),
        name="join_columns",
    )(pieces)


def swap_cores(value):
    return lax.ppermute(value, "c", [(0, 1), (1, 0)])


def shards(iterate):
    pieces = split_columns(iterate.reshape(PANEL, COLS))
    own = lax.all_to_all(pieces, CHIP_AXES, 0, 0, tiled=True).reshape(HALF, WIDTH)
    other = swap_cores(own)
    keep_a, send_a, *rest = own_gram(own)
    arrived_a = exchange(send_a, 0, 0)
    keep_b, send_b, keep_c, send_c = cross_gram(*rest, own, other)
    arrived_b, arrived_c = exchange(send_b, 1, 0), exchange(send_c, 2, 0)
    arrived_a, arrived_b = lax.optimization_barrier((arrived_a, arrived_b))
    first_hops = (keep_a, arrived_a), (keep_b, arrived_b), (keep_c, arrived_c)
    streams = [sum_over_chips(s, *pair) for s, pair in enumerate(first_hops)]
    pieces = jnp.concatenate(streams, axis=1)
    pieces_other = swap_cores(pieces)
    packed, gram, square = own_square(pieces)
    sent = update_rows(packed, pieces_other, gram, square, own, other)
    sent = sent.reshape(STRIPES * CHIPS, PANEL + PANEL // 2, LANES)
    received = lax.all_to_all(sent, ALL_CHIPS, 0, 0, tiled=True)
    return join_columns(received.reshape(STRIPES, CHIPS, PANEL + PANEL // 2, LANES))


def solution(mesh):
    fine = Mesh(mesh.devices.reshape(4, 2, 4, 2, 2), ("z", "yl", "x", "yh", "c"))
    return jax.shard_map(
        shards,
        mesh=fine,
        in_specs=(P(("z", "yl"), ("x", "yh", "c"), None),),
        out_specs=P(None, ("x", "yh", "c"), ("z", "yl")),
        check_vma=False,
    )
```

```python
import math

import jax
import jax.numpy as jnp
from jax import lax
from jax.experimental import pallas as pl
from jax.experimental.pallas import tpu as pltpu
from jax.sharding import Mesh, PartitionSpec as P

coeff_a = 3.4445
coeff_b = -4.775
coeff_c = 2.0315

ROWS = 1536
COLS = 12288
LANES = 128
CHIPS = 8
STRIPES = 8
PANEL = ROWS // (2 * CHIPS)
HALF = ROWS // 2
WIDTH = COLS // CHIPS
TILES = COLS // STRIPES // LANES
BLOCKS = HALF // LANES
BELOW = LANES * BLOCKS * (BLOCKS - 1) // 2
EDGE = 2 * BELOW + HALF
PACKED = -(-(EDGE + BLOCKS) // (16 * CHIPS)) * 16 * CHIPS
PIECES = (208, 192, 192)
BASES = (0, CHIPS * PIECES[0], CHIPS * (PIECES[0] + PIECES[1]))
TAILS = TILES - CHIPS
MIB = 1 << 20

CHIP_AXES = ("x", "yh")
ALL_CHIPS = ("z", "yl", "x", "yh")
ORDERS = (("abd", "bda", "dab"), ("bda", "dab", "abd"))


def halves(a, b, first):
    a, b = a.astype(jnp.float32), b.astype(jnp.float32)
    low = lax.broadcasted_iota(jnp.int32, a.shape, a.ndim - 1) < LANES // 2
    if first:
        return jnp.where(low, a, pltpu.roll(b, LANES // 2, a.ndim - 1))
    return jnp.where(low, pltpu.roll(a, LANES // 2, a.ndim - 1), b)


def tile(index):
    return pl.ds(index * LANES, LANES)


def place(stream, core):
    x, d = lax.axis_index("x"), lax.axis_index("yh")
    bit = {"a": lax.rem((x + 1) // 2, 2), "b": x // 2, "d": d}
    places = [4 * bit[i] + 2 * bit[j] + bit[k] for i, j, k in (orders[stream] for orders in ORDERS)]
    return places[0] + core * (places[1] - places[0])


def piece_rows(stream, position, base, core):
    piece = lax.bitwise_xor(place(stream, core), position)
    return pl.ds(base + pl.multiple_of(piece * PIECES[stream], 16), PIECES[stream])


def split_pieces(stream, whole_ref, base, keep_ref, send_ref):
    half, core = CHIPS // 2, lax.axis_index("c")
    for k in range(half):
        keep_ref[k] = whole_ref[piece_rows(stream, k, base, core), :]
        send_ref[k] = whole_ref[piece_rows(stream, k + half, base, core), :].astype(send_ref.dtype)


def half_shapes(stream, kind):
    shape = (CHIPS // 2, PIECES[stream], LANES)
    return [jax.ShapeDtypeStruct(shape, jnp.float32), jax.ShapeDtypeStruct(shape, kind)]


def split_kernel(x_ref, out_ref, tails_ref, sems, tail_sems):
    tails = [
        pltpu.make_async_copy(
            x_ref.at[:, pl.ds((TILES * j + CHIPS) * LANES, TAILS * LANES)],
            tails_ref.at[:, pl.ds(TAILS * j * LANES, TAILS * LANES)],
            tail_sems.at[j],
        )
        for j in range(STRIPES)
    ]
    mains = [
        pltpu.make_async_copy(x_ref.at[:, tile(TILES * j + p)], out_ref.at[p, :, tile(j)], sems.at[p, j])
        for j in range(STRIPES)
        for p in range(CHIPS)
    ]
    for copy in tails + mains:
        copy.start()
    for copy in tails:
        copy.wait()
    for p in range(CHIPS):
        for m in range(STRIPES // 2):
            left, right = (tails_ref[:, tile(TAILS * (2 * m + i) + p // 2)] for i in range(2))
            out_ref[p, :, tile(STRIPES + m)] = halves(left, right, p % 2 == 0).astype(out_ref.dtype)
    for copy in mains:
        copy.wait()


def split_columns(x):
    return pl.pallas_call(
        split_kernel,
        in_specs=[pl.BlockSpec(memory_space=pltpu.HBM)],
        out_shape=jax.ShapeDtypeStruct((CHIPS, PANEL, WIDTH), x.dtype),
        scratch_shapes=[
            pltpu.VMEM((PANEL, STRIPES * TAILS * LANES), x.dtype),
            pltpu.SemaphoreType.DMA((CHIPS, STRIPES)),
            pltpu.SemaphoreType.DMA((STRIPES,)),
        ],
        compiler_params=pltpu.CompilerParams(vmem_limit_bytes=16 * MIB),
        name="split_columns",
    )(pltpu.with_memory_space_constraint(x, pltpu.HBM))


def strip(j):
    below = (BLOCKS - 1 - j) * LANES
    start = LANES * sum(BLOCKS - 1 - i for i in range(j))
    return pl.ds(start, below)


def triangle(own_ref, ref, store_below, store_diagonal):
    for j in range(0, BLOCKS, 2):
        first = j * LANES
        part = lax.dot_general(
            own_ref[pl.ds(first, HALF - first), :],
            ref[pl.ds(first, 2 * LANES), :],
            (((1,), (1,)), ((), ())),
            preferred_element_type=jnp.float32,
        )
        for i in range(2):
            columns = part[i * LANES :, i * LANES : (i + 1) * LANES]
            store_diagonal(j + i, columns[:LANES])
            if j + i + 1 < BLOCKS:
                store_below(strip(j + i), columns[LANES:])


def iotas():
    return [lax.broadcasted_iota(jnp.int32, (LANES, LANES), axis) for axis in range(2)]


def own_gram_kernel(own_ref, keep_ref, send_ref, rest_ref, diagonal_ref, whole_ref):
    def store_below(rows, value):
        whole_ref[rows, :] = value

    def store_diagonal(j, value):
        diagonal_ref[j] = value

    triangle(own_ref, own_ref, store_below, store_diagonal)
    split_pieces(0, whole_ref, 0, keep_ref, send_ref)
    rest_ref[...] = whole_ref[pl.ds(BASES[1], BELOW - BASES[1]), :]


def own_gram(own):
    return pl.pallas_call(
        own_gram_kernel,
        out_shape=half_shapes(0, own.dtype)
        + [
            jax.ShapeDtypeStruct((BELOW - BASES[1], LANES), jnp.float32),
            jax.ShapeDtypeStruct((BLOCKS, LANES, LANES), jnp.float32),
        ],
        scratch_shapes=[pltpu.VMEM((BELOW, LANES), jnp.float32)],
        compiler_params=pltpu.CompilerParams(vmem_limit_bytes=8 * MIB),
        cost_estimate=pl.CostEstimate(
            flops=2 * (BELOW + 3 * HALF) * LANES * WIDTH, bytes_accessed=2 * HALF * WIDTH, transcendentals=0
        ),
        name="own_gram",
    )(own)


def cross_gram_kernel(
    rest_ref, diagonal_ref, own_ref, other_ref, keep_b_ref, send_b_ref, keep_c_ref, send_c_ref, whole_ref
):
    start = BELOW - BASES[1]
    whole_ref[pl.ds(0, start), :] = rest_ref[...]
    row, column = iotas()
    edges = []

    def store_below(rows, value):
        whole_ref[pl.ds(start + rows.start, rows.size), :] = value

    def store_diagonal(j, value):
        whole_ref[pl.ds(start + BELOW + j * LANES, LANES), :] = jnp.where(row >= column, diagonal_ref[j], value)
        edges.append(jnp.sum(jnp.where(row == column, value, 0.0), axis=0, keepdims=True))

    triangle(own_ref, other_ref, store_below, store_diagonal)
    edges.append(jnp.zeros((PACKED - EDGE - BLOCKS, LANES), jnp.float32))
    whole_ref[pl.ds(EDGE - BASES[1], PACKED - EDGE), :] = jnp.concatenate(edges)
    split_pieces(1, whole_ref, 0, keep_b_ref, send_b_ref)
    split_pieces(2, whole_ref, BASES[2] - BASES[1], keep_c_ref, send_c_ref)


def cross_gram(rest, diagonal, own, other):
    return pl.pallas_call(
        cross_gram_kernel,
        out_shape=half_shapes(1, own.dtype) + half_shapes(2, own.dtype),
        scratch_shapes=[pltpu.VMEM((PACKED - BASES[1], LANES), jnp.float32)],
        compiler_params=pltpu.CompilerParams(vmem_limit_bytes=12 * MIB),
        cost_estimate=pl.CostEstimate(
            flops=2 * (BELOW + 3 * HALF) * LANES * WIDTH, bytes_accessed=4 * HALF * WIDTH, transcendentals=0
        ),
        name="cross_gram",
    )(rest, diagonal, own, other)


def exchange(value, stream, hop):
    pairs = []
    for x in range(4):
        for d in range(2):
            for core in range(2):
                axis = ORDERS[core][stream][hop]
                to = {"a": (x ^ 1, d), "b": (3 - x, d), "d": (x, 1 - d)}[axis]
                pairs.append((4 * x + 2 * d + core, 4 * to[0] + 2 * to[1] + core))
    return lax.ppermute(value, ("x", "yh", "c"), pairs)


def wide(value):
    return value.astype(jnp.float32)


def sum_over_chips(stream, keep, arrived):
    kind = arrived.dtype
    half = (keep + wide(arrived)).astype(kind).reshape(2, 2, *keep.shape[1:])
    half = (wide(half) + wide(exchange(half, stream, 1))[::-1]).astype(kind)
    half = (wide(half) + wide(exchange(half, stream, 2))[:, ::-1]).astype(kind).reshape(arrived.shape)
    return jnp.concatenate([half, exchange(half, stream, 0)])


def unpermute(pieces_ref, packed_ref, core):
    first = 0
    for s, rows in enumerate(PIECES):
        for k in range(CHIPS):
            packed_ref[piece_rows(s, k, BASES[s], core), :] = pieces_ref[k, pl.ds(first, rows), :]
        first += rows


def mirror(packed_ref, out_ref, lower):
    for j in range(BLOCKS):
        first = j * LANES
        block = packed_ref[pl.ds(2 * BELOW + first, LANES), :]
        out_ref[pl.ds(first, LANES), tile(j)] = jnp.where(lower, block, block.T)
        if j + 1 < BLOCKS:
            below = packed_ref[strip(j), :]
            out_ref[pl.ds(first + LANES, below.shape[0]), tile(j)] = below
            out_ref[pl.ds(first, LANES), pl.ds(first + LANES, below.shape[0])] = below.T


def own_square_kernel(pieces_ref, packed_ref, gram_ref, square_ref):
    row, column = iotas()
    unpermute(pieces_ref, packed_ref, lax.axis_index("c"))
    mirror(packed_ref, gram_ref, row >= column)
    for n in range(0, HALF, 256):
        columns = pl.ds(n, 256)
        square_ref[:, columns] = jnp.dot(gram_ref[...], gram_ref[:, columns], preferred_element_type=jnp.float32)


def own_square(pieces):
    return pl.pallas_call(
        own_square_kernel,
        out_shape=(
            jax.ShapeDtypeStruct((PACKED, LANES), pieces.dtype),
            jax.ShapeDtypeStruct((HALF, HALF), pieces.dtype),
            jax.ShapeDtypeStruct((HALF, HALF), jnp.float32),
        ),
        compiler_params=pltpu.CompilerParams(vmem_limit_bytes=12 * MIB),
        cost_estimate=pl.CostEstimate(
            flops=2 * HALF * HALF * HALF, bytes_accessed=8 * HALF * HALF, transcendentals=0
        ),
        name="own_square",
    )(pieces)


def unpack_cross(own_ref, other_ref, cross_ref):
    row, column = iotas()
    for j in range(BLOCKS):
        first = j * LANES
        upper, theirs = (ref[pl.ds(2 * BELOW + first, LANES), :] for ref in (own_ref, other_ref))
        edge = jnp.broadcast_to(own_ref[pl.ds(EDGE, 16), :].astype(jnp.float32)[j : j + 1], (LANES, LANES))
        block = jnp.where(row < column, upper.astype(jnp.float32), theirs.T.astype(jnp.float32))
        cross_ref[pl.ds(first, LANES), tile(j)] = jnp.where(row == column, edge, block).astype(cross_ref.dtype)
        if j + 1 < BLOCKS:
            rows = pl.ds(BELOW + strip(j).start, strip(j).size)
            cross_ref[pl.ds(first + LANES, rows.size), tile(j)] = own_ref[rows, :]
            cross_ref[pl.ds(first, LANES), pl.ds(first + LANES, rows.size)] = other_ref[rows, :].T


def update_kernel(
    own_ref, pieces_ref, gram_ref, square_ref, x_ref, x_other_ref, out_ref,
    other_ref, cross_ref, gram_other_ref, mixing_ref,
):
    scale = math.sqrt(max(ROWS, COLS))
    step = 256
    row, column = iotas()
    unpermute(pieces_ref, other_ref, 1 - lax.axis_index("c"))
    unpack_cross(own_ref, other_ref, cross_ref)
    mirror(other_ref, gram_other_ref, row >= column)
    for n in range(0, HALF, step):
        columns = pl.ds(n, step)
        square = square_ref[:, columns] + lax.dot_general(
            cross_ref[...], cross_ref[columns, :], (((1,), (1,)), ((), ())), preferred_element_type=jnp.float32
        )
        gram = gram_ref[:, columns].astype(jnp.float32)
        mixing_ref[:, columns] = (coeff_b * gram + coeff_c * square).astype(mixing_ref.dtype)
    for n in range(0, HALF, step):
        columns = pl.ds(n, step)
        square = jnp.dot(gram_ref[...], cross_ref[:, columns], preferred_element_type=jnp.float32)
        square += jnp.dot(cross_ref[...], gram_other_ref[:, columns], preferred_element_type=jnp.float32)
        gram = cross_ref[:, columns].astype(jnp.float32)
        mixing_ref[:, pl.ds(HALF + n, step)] = (coeff_b * gram + coeff_c * square).astype(mixing_ref.dtype)
    for t in range(0, TILES, 2):
        columns = pl.ds(t * LANES, 2 * LANES)
        result = jnp.dot(mixing_ref[:, pl.ds(0, HALF)], x_ref[:, columns], preferred_element_type=jnp.float32)
        result += jnp.dot(mixing_ref[:, pl.ds(HALF, HALF)], x_other_ref[:, columns], preferred_element_type=jnp.float32)
        result = scale * (coeff_a * x_ref[:, columns].astype(jnp.float32) + result)
        for i in range(2):
            block = result[:, i * LANES : (i + 1) * LANES].reshape(CHIPS, PANEL, LANES)
            j = t + i
            if j < STRIPES:
                out_ref[j, :, pl.ds(0, PANEL), :] = block.astype(out_ref.dtype)
            else:
                top, bottom = block[:, : PANEL // 2], block[:, PANEL // 2 :]
                for side in range(2):
                    packed = halves(top, bottom, side == 0).astype(out_ref.dtype)
                    out_ref[2 * (j - STRIPES) + side, :, pl.ds(PANEL, PANEL // 2), :] = packed


def update_rows(*operands):
    kind = operands[0].dtype
    return pl.pallas_call(
        update_kernel,
        out_shape=jax.ShapeDtypeStruct((STRIPES, CHIPS, PANEL + PANEL // 2, LANES), kind),
        scratch_shapes=[
            pltpu.VMEM((PACKED, LANES), kind),
            pltpu.VMEM((HALF, HALF), kind),
            pltpu.VMEM((HALF, HALF), kind),
            pltpu.VMEM((HALF, ROWS), kind),
        ],
        compiler_params=pltpu.CompilerParams(vmem_limit_bytes=24 * MIB),
        cost_estimate=pl.CostEstimate(
            flops=4 * HALF * ROWS * ROWS - 2 * HALF * HALF * HALF, bytes_accessed=10 * HALF * ROWS, transcendentals=0
        ),
        name="update_rows",
    )(*operands)


def join_kernel(pieces_ref, out_ref, whole_ref, sems):
    copies = []
    for layer in range(STRIPES):
        for p in range(CHIPS):
            whole_ref[layer, :, tile(p)] = pieces_ref[layer, p, pl.ds(0, PANEL), :]
        for pair in range(CHIPS // 2):
            left = pieces_ref[layer, 2 * pair, pl.ds(PANEL, PANEL // 2), :]
            right = pieces_ref[layer, 2 * pair + 1, pl.ds(PANEL, PANEL // 2), :]
            for part in range(2):
                joined = halves(left, right, part == 0).astype(whole_ref.dtype)
                whole_ref[layer, pl.ds(part * PANEL // 2, PANEL // 2), tile(CHIPS + pair)] = joined
        copies.append(pltpu.make_async_copy(whole_ref.at[layer], out_ref.at[layer], sems.at[layer]))
        copies[-1].start()
    for copy in copies:
        copy.wait()


def join_columns(pieces):
    shape = (pieces.shape[0], PANEL, TILES * LANES)
    return pl.pallas_call(
        join_kernel,
        in_specs=[pl.BlockSpec(memory_space=pltpu.VMEM)],
        out_specs=pl.BlockSpec(memory_space=pl.ANY),
        out_shape=jax.ShapeDtypeStruct(shape, pieces.dtype),
        scratch_shapes=[pltpu.VMEM(shape, pieces.dtype), pltpu.SemaphoreType.DMA((pieces.shape[0],))],
        compiler_params=pltpu.CompilerParams(vmem_limit_bytes=12 * MIB),
        name="join_columns",
    )(pieces)


def swap_cores(value):
    return lax.ppermute(value, "c", [(0, 1), (1, 0)])


def shards(iterate):
    pieces = split_columns(iterate.reshape(PANEL, COLS))
    own = lax.all_to_all(pieces, CHIP_AXES, 0, 0, tiled=True).reshape(HALF, WIDTH)
    other = swap_cores(own)
    keep_a, send_a, *rest = own_gram(own)
    arrived_a = exchange(send_a, 0, 0)
    keep_b, send_b, keep_c, send_c = cross_gram(*rest, own, other)
    arrived_b, arrived_c = exchange(send_b, 1, 0), exchange(send_c, 2, 0)
    arrived_a, arrived_b = lax.optimization_barrier((arrived_a, arrived_b))
    first_hops = (keep_a, arrived_a), (keep_b, arrived_b), (keep_c, arrived_c)
    streams = [sum_over_chips(s, *pair) for s, pair in enumerate(first_hops)]
    pieces = jnp.concatenate(streams, axis=1)
    pieces_other = swap_cores(pieces)
    packed, gram, square = own_square(pieces)
    sent = update_rows(packed, pieces_other, gram, square, own, other)
    sent = sent.reshape(STRIPES * CHIPS, PANEL + PANEL // 2, LANES)
    received = lax.all_to_all(sent, ALL_CHIPS, 0, 0, tiled=True)
    return join_columns(received.reshape(STRIPES, CHIPS, PANEL + PANEL // 2, LANES))


def solution(mesh):
    fine = Mesh(mesh.devices.reshape(4, 2, 4, 2, 2), ("z", "yl", "x", "yh", "c"))
    return jax.shard_map(
        shards,
        mesh=fine,
        in_specs=(P(("z", "yl"), ("x", "yh", "c"), None),),
        out_specs=P(None, ("x", "yh", "c"), ("z", "yl")),
        check_vma=False,
    )
```

```python
import math

import jax
import jax.numpy as jnp
from jax import lax
from jax.experimental import pallas as pl
from jax.experimental.pallas import tpu as pltpu
from jax.sharding import Mesh, PartitionSpec as P

coeff_a = 3.4445
coeff_b = -4.775
coeff_c = 2.0315

ROWS = 1536
COLS = 12288
LANES = 128
CHIPS = 8
STRIPES = 8
PANEL = ROWS // (2 * CHIPS)
HALF = ROWS // 2
WIDTH = COLS // CHIPS
TILES = COLS // STRIPES // LANES
BLOCKS = HALF // LANES
BELOW = LANES * BLOCKS * (BLOCKS - 1) // 2
EDGE = 2 * BELOW + HALF
PACKED = -(-(EDGE + BLOCKS) // (16 * CHIPS)) * 16 * CHIPS
PIECES = (240, 176, 176)
BASES = (0, CHIPS * PIECES[0], CHIPS * (PIECES[0] + PIECES[1]))
MIB = 1 << 20

CHIP_AXES = ("x", "yh")
ALL_CHIPS = ("z", "yl", "x", "yh")
ORDERS = (("abd", "bda", "dab"), ("bda", "dab", "abd"))


def halves(a, b, first):
    a, b = a.astype(jnp.float32), b.astype(jnp.float32)
    low = lax.broadcasted_iota(jnp.int32, a.shape, a.ndim - 1) < LANES // 2
    if first:
        return jnp.where(low, a, pltpu.roll(b, LANES // 2, a.ndim - 1))
    return jnp.where(low, pltpu.roll(a, LANES // 2, a.ndim - 1), b)


def tile(index):
    return pl.ds(index * LANES, LANES)


def place(stream, core):
    x, d = lax.axis_index("x"), lax.axis_index("yh")
    bit = {"a": lax.rem((x + 1) // 2, 2), "b": x // 2, "d": d}
    places = [4 * bit[i] + 2 * bit[j] + bit[k] for i, j, k in (orders[stream] for orders in ORDERS)]
    return places[0] + core * (places[1] - places[0])


def piece_rows(stream, position, base, core):
    if stream > 0:
        piece = lax.bitwise_xor(place(stream, core), position)
        return pl.ds(base + pl.multiple_of(piece * PIECES[stream], 16), PIECES[stream])
    return pl.ds(base + position * PIECES[stream], PIECES[stream])


def split_pieces(stream, whole_ref, base, keep_ref, send_ref):
    half, core = CHIPS // 2, lax.axis_index("c")
    for k in range(half):
        keep_ref[k] = whole_ref[piece_rows(stream, k, base, core), :]
        send_ref[k] = whole_ref[piece_rows(stream, k + half, base, core), :].astype(send_ref.dtype)


def half_shapes(stream, kind):
    shape = (CHIPS // 2, PIECES[stream], LANES)
    return [jax.ShapeDtypeStruct(shape, jnp.float32), jax.ShapeDtypeStruct(shape, kind)]


def split_kernel(x_ref, out_ref):
    for p in range(CHIPS):
        for j in range(STRIPES):
            out_ref[p, :, tile(j)] = x_ref[:, tile(TILES * j + p)]
        for m in range(STRIPES // 2):
            left = x_ref[:, tile(TILES * (2 * m) + CHIPS + p // 2)]
            right = x_ref[:, tile(TILES * (2 * m + 1) + CHIPS + p // 2)]
            out_ref[p, :, tile(STRIPES + m)] = halves(left, right, p % 2 == 0).astype(out_ref.dtype)


def split_columns(x):
    return pl.pallas_call(
        split_kernel,
        out_shape=jax.ShapeDtypeStruct((CHIPS, PANEL, WIDTH), x.dtype),
        compiler_params=pltpu.CompilerParams(vmem_limit_bytes=16 * MIB),
        name="split_columns",
    )(x)


def strip(j):
    below = (BLOCKS - 1 - j) * LANES
    start = LANES * sum(BLOCKS - 1 - i for i in range(j))
    return pl.ds(start, below)


def triangle(own_ref, ref, store_below, store_diagonal):
    for j in range(0, BLOCKS, 2):
        first = j * LANES
        part = lax.dot_general(
            own_ref[pl.ds(first, HALF - first), :],
            ref[pl.ds(first, 2 * LANES), :],
            (((1,), (1,)), ((), ())),
            preferred_element_type=jnp.float32,
        )
        for i in range(2):
            columns = part[i * LANES :, i * LANES : (i + 1) * LANES]
            store_diagonal(j + i, columns[:LANES])
            if j + i + 1 < BLOCKS:
                store_below(strip(j + i), columns[LANES:])


def iotas():
    return [lax.broadcasted_iota(jnp.int32, (LANES, LANES), axis) for axis in range(2)]


def own_gram_kernel(own_ref, below_ref, diagonal_ref):
    def store_below(rows, value):
        below_ref[rows, :] = value.astype(below_ref.dtype)

    def store_diagonal(j, value):
        diagonal_ref[j] = value

    triangle(own_ref, own_ref, store_below, store_diagonal)


def own_gram(own):
    return pl.pallas_call(
        own_gram_kernel,
        out_shape=(
            jax.ShapeDtypeStruct((BELOW, LANES), own.dtype),
            jax.ShapeDtypeStruct((BLOCKS, LANES, LANES), jnp.float32),
        ),
        compiler_params=pltpu.CompilerParams(vmem_limit_bytes=8 * MIB),
        cost_estimate=pl.CostEstimate(
            flops=2 * (BELOW + 3 * HALF) * LANES * WIDTH, bytes_accessed=2 * HALF * WIDTH, transcendentals=0
        ),
        name="own_gram",
    )(own)


def sum_kernel(parts_ref, out_ref):
    total = jnp.sum(parts_ref[...].astype(jnp.float32), axis=0).astype(out_ref.dtype)
    for p in range(CHIPS):
        out_ref[p] = total


def sum_copies(parts):
    return pl.pallas_call(
        sum_kernel,
        out_shape=jax.ShapeDtypeStruct(parts.shape, parts.dtype),
        compiler_params=pltpu.CompilerParams(vmem_limit_bytes=4 * MIB),
        name="sum_copies",
    )(parts)


def cross_gram_kernel(
    diagonal_ref, own_ref, other_ref, keep_b_ref, send_b_ref, keep_c_ref, send_c_ref, whole_ref
):
    row, column = iotas()
    edges = []

    def store_below(rows, value):
        whole_ref[rows, :] = value

    def store_diagonal(j, value):
        whole_ref[pl.ds(BELOW + j * LANES, LANES), :] = jnp.where(row >= column, diagonal_ref[j], value)
        edges.append(jnp.sum(jnp.where(row == column, value, 0.0), axis=0, keepdims=True))

    triangle(own_ref, other_ref, store_below, store_diagonal)
    edges.append(jnp.zeros((PACKED - EDGE - BLOCKS, LANES), jnp.float32))
    whole_ref[pl.ds(EDGE - BASES[1], PACKED - EDGE), :] = jnp.concatenate(edges)
    split_pieces(1, whole_ref, 0, keep_b_ref, send_b_ref)
    split_pieces(2, whole_ref, BASES[2] - BASES[1], keep_c_ref, send_c_ref)


def cross_gram(diagonal, own, other):
    return pl.pallas_call(
        cross_gram_kernel,
        out_shape=half_shapes(1, own.dtype) + half_shapes(2, own.dtype),
        scratch_shapes=[pltpu.VMEM((PACKED - BASES[1], LANES), jnp.float32)],
        compiler_params=pltpu.CompilerParams(vmem_limit_bytes=12 * MIB),
        cost_estimate=pl.CostEstimate(
            flops=2 * (BELOW + 3 * HALF) * LANES * WIDTH, bytes_accessed=4 * HALF * WIDTH, transcendentals=0
        ),
        name="cross_gram",
    )(diagonal, own, other)


def exchange(value, stream, hop):
    pairs = []
    for x in range(4):
        for d in range(2):
            for core in range(2):
                axis = ORDERS[core][stream][hop]
                to = {"a": (x ^ 1, d), "b": (3 - x, d), "d": (x, 1 - d)}[axis]
                pairs.append((4 * x + 2 * d + core, 4 * to[0] + 2 * to[1] + core))
    return lax.ppermute(value, ("x", "yh", "c"), pairs)


def wide(value):
    return value.astype(jnp.float32)


def sum_over_chips(stream, keep, arrived):
    kind = arrived.dtype
    half = (keep + wide(arrived)).astype(kind).reshape(2, 2, *keep.shape[1:])
    half = (wide(half) + wide(exchange(half, stream, 1))[::-1]).astype(kind)
    half = (wide(half) + wide(exchange(half, stream, 2))[:, ::-1]).astype(kind).reshape(arrived.shape)
    return jnp.concatenate([half, exchange(half, stream, 0)])


def unpermute(pieces_ref, packed_ref, core):
    first = 0
    for s, rows in enumerate(PIECES):
        for k in range(CHIPS):
            packed_ref[piece_rows(s, k, BASES[s], core), :] = pieces_ref[k, pl.ds(first, rows), :]
        first += rows


def mirror(packed_ref, out_ref, lower):
    for j in range(BLOCKS):
        first = j * LANES
        block = packed_ref[pl.ds(2 * BELOW + first, LANES), :]
        out_ref[pl.ds(first, LANES), tile(j)] = jnp.where(lower, block, block.T)
        if j + 1 < BLOCKS:
            below = packed_ref[strip(j), :]
            out_ref[pl.ds(first + LANES, below.shape[0]), tile(j)] = below
            out_ref[pl.ds(first, LANES), pl.ds(first + LANES, below.shape[0])] = below.T


def own_square_kernel(pieces_ref, packed_ref, gram_ref, square_ref):
    row, column = iotas()
    unpermute(pieces_ref, packed_ref, lax.axis_index("c"))
    mirror(packed_ref, gram_ref, row >= column)
    for n in range(0, HALF, 256):
        columns = pl.ds(n, 256)
        square_ref[:, columns] = jnp.dot(gram_ref[...], gram_ref[:, columns], preferred_element_type=jnp.float32)


def own_square(pieces):
    return pl.pallas_call(
        own_square_kernel,
        out_shape=(
            jax.ShapeDtypeStruct((PACKED, LANES), pieces.dtype),
            jax.ShapeDtypeStruct((HALF, HALF), pieces.dtype),
            jax.ShapeDtypeStruct((HALF, HALF), jnp.float32),
        ),
        compiler_params=pltpu.CompilerParams(vmem_limit_bytes=12 * MIB),
        cost_estimate=pl.CostEstimate(
            flops=2 * HALF * HALF * HALF, bytes_accessed=8 * HALF * HALF, transcendentals=0
        ),
        name="own_square",
    )(pieces)


def unpack_cross(own_ref, other_ref, cross_ref):
    row, column = iotas()
    for j in range(BLOCKS):
        first = j * LANES
        upper, theirs = (ref[pl.ds(2 * BELOW + first, LANES), :] for ref in (own_ref, other_ref))
        edge = jnp.broadcast_to(own_ref[pl.ds(EDGE, 16), :].astype(jnp.float32)[j : j + 1], (LANES, LANES))
        block = jnp.where(row < column, upper.astype(jnp.float32), theirs.T.astype(jnp.float32))
        cross_ref[pl.ds(first, LANES), tile(j)] = jnp.where(row == column, edge, block).astype(cross_ref.dtype)
        if j + 1 < BLOCKS:
            rows = pl.ds(BELOW + strip(j).start, strip(j).size)
            cross_ref[pl.ds(first + LANES, rows.size), tile(j)] = own_ref[rows, :]
            cross_ref[pl.ds(first, LANES), pl.ds(first + LANES, rows.size)] = other_ref[rows, :].T


def update_kernel(
    own_ref, pieces_ref, gram_ref, square_ref, x_ref, x_other_ref, out_ref,
    other_ref, cross_ref, gram_other_ref, mixing_ref,
):
    scale = math.sqrt(max(ROWS, COLS))
    step = 256
    row, column = iotas()
    unpermute(pieces_ref, other_ref, 1 - lax.axis_index("c"))
    unpack_cross(own_ref, other_ref, cross_ref)
    mirror(other_ref, gram_other_ref, row >= column)
    for n in range(0, HALF, step):
        columns = pl.ds(n, step)
        square = square_ref[:, columns] + lax.dot_general(
            cross_ref[...], cross_ref[columns, :], (((1,), (1,)), ((), ())), preferred_element_type=jnp.float32
        )
        gram = gram_ref[:, columns].astype(jnp.float32)
        mixing_ref[:, columns] = (coeff_b * gram + coeff_c * square).astype(mixing_ref.dtype)
    for n in range(0, HALF, step):
        columns = pl.ds(n, step)
        square = jnp.dot(gram_ref[...], cross_ref[:, columns], preferred_element_type=jnp.float32)
        square += jnp.dot(cross_ref[...], gram_other_ref[:, columns], preferred_element_type=jnp.float32)
        gram = cross_ref[:, columns].astype(jnp.float32)
        mixing_ref[:, pl.ds(HALF + n, step)] = (coeff_b * gram + coeff_c * square).astype(mixing_ref.dtype)
    for t in range(0, TILES, 2):
        columns = pl.ds(t * LANES, 2 * LANES)
        result = jnp.dot(mixing_ref[:, pl.ds(0, HALF)], x_ref[:, columns], preferred_element_type=jnp.float32)
        result += jnp.dot(mixing_ref[:, pl.ds(HALF, HALF)], x_other_ref[:, columns], preferred_element_type=jnp.float32)
        result = scale * (coeff_a * x_ref[:, columns].astype(jnp.float32) + result)
        for i in range(2):
            block = result[:, i * LANES : (i + 1) * LANES].reshape(CHIPS, PANEL, LANES)
            j = t + i
            if j < STRIPES:
                out_ref[j, :, pl.ds(0, PANEL), :] = block.astype(out_ref.dtype)
            else:
                top, bottom = block[:, : PANEL // 2], block[:, PANEL // 2 :]
                for side in range(2):
                    packed = halves(top, bottom, side == 0).astype(out_ref.dtype)
                    out_ref[2 * (j - STRIPES) + side, :, pl.ds(PANEL, PANEL // 2), :] = packed


def update_rows(*operands):
    kind = operands[0].dtype
    return pl.pallas_call(
        update_kernel,
        out_shape=jax.ShapeDtypeStruct((STRIPES, CHIPS, PANEL + PANEL // 2, LANES), kind),
        scratch_shapes=[
            pltpu.VMEM((PACKED, LANES), kind),
            pltpu.VMEM((HALF, HALF), kind),
            pltpu.VMEM((HALF, HALF), kind),
            pltpu.VMEM((HALF, ROWS), kind),
        ],
        compiler_params=pltpu.CompilerParams(vmem_limit_bytes=24 * MIB),
        cost_estimate=pl.CostEstimate(
            flops=4 * HALF * ROWS * ROWS - 2 * HALF * HALF * HALF, bytes_accessed=10 * HALF * ROWS, transcendentals=0
        ),
        name="update_rows",
    )(*operands)


def join_kernel(pieces_ref, out_ref, whole_ref, sems):
    copies = []
    for layer in range(STRIPES):
        for p in range(CHIPS):
            whole_ref[layer, :, tile(p)] = pieces_ref[layer, p, pl.ds(0, PANEL), :]
        for pair in range(CHIPS // 2):
            left = pieces_ref[layer, 2 * pair, pl.ds(PANEL, PANEL // 2), :]
            right = pieces_ref[layer, 2 * pair + 1, pl.ds(PANEL, PANEL // 2), :]
            for part in range(2):
                joined = halves(left, right, part == 0).astype(whole_ref.dtype)
                whole_ref[layer, pl.ds(part * PANEL // 2, PANEL // 2), tile(CHIPS + pair)] = joined
        copies.append(pltpu.make_async_copy(whole_ref.at[layer], out_ref.at[layer], sems.at[layer]))
        copies[-1].start()
    for copy in copies:
        copy.wait()


def join_columns(pieces):
    shape = (pieces.shape[0], PANEL, TILES * LANES)
    return pl.pallas_call(
        join_kernel,
        in_specs=[pl.BlockSpec(memory_space=pltpu.VMEM)],
        out_specs=pl.BlockSpec(memory_space=pl.ANY),
        out_shape=jax.ShapeDtypeStruct(shape, pieces.dtype),
        scratch_shapes=[pltpu.VMEM(shape, pieces.dtype), pltpu.SemaphoreType.DMA((pieces.shape[0],))],
        compiler_params=pltpu.CompilerParams(vmem_limit_bytes=12 * MIB),
        name="join_columns",
    )(pieces)


def swap_cores(value):
    return lax.ppermute(value, "c", [(0, 1), (1, 0)])


def shards(iterate):
    pieces = split_columns(iterate.reshape(PANEL, COLS))
    own = lax.all_to_all(pieces, CHIP_AXES, 0, 0, tiled=True).reshape(HALF, WIDTH)
    other = pltpu.with_memory_space_constraint(swap_cores(own), pltpu.VMEM)
    below, diagonal = own_gram(own)
    below = lax.all_to_all(below.reshape(CHIPS, PIECES[0], LANES), CHIP_AXES, 0, 0, tiled=True)
    keep_b, send_b, keep_c, send_c = cross_gram(diagonal, own, other)
    below, arrived_b, arrived_c = lax.optimization_barrier((below, exchange(send_b, 1, 0), exchange(send_c, 2, 0)))
    first_hops = (keep_b, arrived_b), (keep_c, arrived_c)
    streams = [sum_over_chips(s + 1, *pair) for s, pair in enumerate(first_hops)]
    below = lax.all_to_all(sum_copies(below), CHIP_AXES, 0, 0, tiled=True)
    streams = [below, *streams]
    pieces = jnp.concatenate(streams, axis=1)
    pieces_other = swap_cores(pieces)
    packed, gram, square = own_square(pieces)
    sent = update_rows(packed, pieces_other, gram, square, own, other)
    sent = sent.reshape(STRIPES * CHIPS, PANEL + PANEL // 2, LANES)
    received = lax.all_to_all(sent, ALL_CHIPS, 0, 0, tiled=True)
    return join_columns(received.reshape(STRIPES, CHIPS, PANEL + PANEL // 2, LANES))


def solution(mesh):
    fine = Mesh(mesh.devices.reshape(4, 2, 4, 2, 2), ("z", "yl", "x", "yh", "c"))
    return jax.shard_map(
        shards,
        mesh=fine,
        in_specs=(P(("z", "yl"), ("x", "yh", "c"), None),),
        out_specs=P(None, ("x", "yh", "c"), ("z", "yl")),
        check_vma=False,
    )
```

```python
import math

import jax
import jax.numpy as jnp
from jax import lax
from jax.experimental import pallas as pl
from jax.experimental.pallas import tpu as pltpu
from jax.sharding import Mesh, PartitionSpec as P

coeff_a = 3.4445
coeff_b = -4.775
coeff_c = 2.0315

ROWS = 1536
COLS = 12288
LANES = 128
CHIPS = 8
STRIPES = 8
PANEL = ROWS // (2 * CHIPS)
HALF = ROWS // 2
WIDTH = COLS // CHIPS
TILES = COLS // STRIPES // LANES
BLOCKS = HALF // LANES
BELOW = LANES * BLOCKS * (BLOCKS - 1) // 2
EDGE = 2 * BELOW + HALF
PACKED = -(-(EDGE + BLOCKS) // (16 * CHIPS)) * 16 * CHIPS
PIECES = (208, 192, 192)
BASES = (0, CHIPS * PIECES[0], CHIPS * (PIECES[0] + PIECES[1]))
MIB = 1 << 20

CHIP_AXES = ("x", "yh")
ALL_CHIPS = ("z", "yl", "x", "yh")
ORDERS = (("abd", "bda", "dab"), ("bda", "dab", "abd"))


def halves(a, b, first):
    a, b = a.astype(jnp.float32), b.astype(jnp.float32)
    low = lax.broadcasted_iota(jnp.int32, a.shape, a.ndim - 1) < LANES // 2
    if first:
        return jnp.where(low, a, pltpu.roll(b, LANES // 2, a.ndim - 1))
    return jnp.where(low, pltpu.roll(a, LANES // 2, a.ndim - 1), b)


def tile(index):
    return pl.ds(index * LANES, LANES)


def place(stream, core):
    x, d = lax.axis_index("x"), lax.axis_index("yh")
    bit = {"a": lax.rem((x + 1) // 2, 2), "b": x // 2, "d": d}
    places = [4 * bit[i] + 2 * bit[j] + bit[k] for i, j, k in (orders[stream] for orders in ORDERS)]
    return places[0] + core * (places[1] - places[0])


def piece_rows(stream, position, base, core):
    piece = lax.bitwise_xor(place(stream, core), position)
    return pl.ds(base + pl.multiple_of(piece * PIECES[stream], 16), PIECES[stream])


def split_pieces(stream, whole_ref, base, keep_ref, send_ref):
    half, core = CHIPS // 2, lax.axis_index("c")
    for k in range(half):
        keep_ref[k] = whole_ref[piece_rows(stream, k, base, core), :]
        send_ref[k] = whole_ref[piece_rows(stream, k + half, base, core), :].astype(send_ref.dtype)


def half_shapes(stream, kind):
    shape = (CHIPS // 2, PIECES[stream], LANES)
    return [jax.ShapeDtypeStruct(shape, jnp.float32), jax.ShapeDtypeStruct(shape, kind)]


def split_kernel(x_ref, out_ref):
    for p in range(CHIPS):
        for j in range(STRIPES):
            out_ref[p, :, tile(j)] = x_ref[:, tile(TILES * j + p)]
        for m in range(STRIPES // 2):
            left = x_ref[:, tile(TILES * (2 * m) + CHIPS + p // 2)]
            right = x_ref[:, tile(TILES * (2 * m + 1) + CHIPS + p // 2)]
            out_ref[p, :, tile(STRIPES + m)] = halves(left, right, p % 2 == 0).astype(out_ref.dtype)


def split_columns(x):
    return pl.pallas_call(
        split_kernel,
        out_shape=jax.ShapeDtypeStruct((CHIPS, PANEL, WIDTH), x.dtype),
        compiler_params=pltpu.CompilerParams(vmem_limit_bytes=16 * MIB),
        name="split_columns",
    )(x)


def strip(j):
    below = (BLOCKS - 1 - j) * LANES
    start = LANES * sum(BLOCKS - 1 - i for i in range(j))
    return pl.ds(start, below)


def triangle(own_ref, ref, store_below, store_diagonal):
    for j in range(0, BLOCKS, 2):
        first = j * LANES
        part = lax.dot_general(
            own_ref[pl.ds(first, HALF - first), :],
            ref[pl.ds(first, 2 * LANES), :],
            (((1,), (1,)), ((), ())),
            preferred_element_type=jnp.float32,
        )
        for i in range(2):
            columns = part[i * LANES :, i * LANES : (i + 1) * LANES]
            store_diagonal(j + i, columns[:LANES])
            if j + i + 1 < BLOCKS:
                store_below(strip(j + i), columns[LANES:])


def iotas():
    return [lax.broadcasted_iota(jnp.int32, (LANES, LANES), axis) for axis in range(2)]


def own_gram_kernel(own_ref, keep_ref, send_ref, rest_ref, diagonal_ref, whole_ref):
    def store_below(rows, value):
        whole_ref[rows, :] = value

    def store_diagonal(j, value):
        diagonal_ref[j] = value

    triangle(own_ref, own_ref, store_below, store_diagonal)
    split_pieces(0, whole_ref, 0, keep_ref, send_ref)
    rest_ref[...] = whole_ref[pl.ds(BASES[1], BELOW - BASES[1]), :]


def own_gram(own):
    return pl.pallas_call(
        own_gram_kernel,
        out_shape=half_shapes(0, own.dtype)
        + [
            jax.ShapeDtypeStruct((BELOW - BASES[1], LANES), jnp.float32),
            jax.ShapeDtypeStruct((BLOCKS, LANES, LANES), jnp.float32),
        ],
        scratch_shapes=[pltpu.VMEM((BELOW, LANES), jnp.float32)],
        compiler_params=pltpu.CompilerParams(vmem_limit_bytes=8 * MIB),
        cost_estimate=pl.CostEstimate(
            flops=2 * (BELOW + 3 * HALF) * LANES * WIDTH, bytes_accessed=2 * HALF * WIDTH, transcendentals=0
        ),
        name="own_gram",
    )(own)


def cross_gram_kernel(
    rest_ref, diagonal_ref, own_ref, other_ref, keep_b_ref, send_b_ref, keep_c_ref, send_c_ref, whole_ref
):
    start = BELOW - BASES[1]
    whole_ref[pl.ds(0, start), :] = rest_ref[...]
    row, column = iotas()
    edges = []

    def store_below(rows, value):
        whole_ref[pl.ds(start + rows.start, rows.size), :] = value

    def store_diagonal(j, value):
        whole_ref[pl.ds(start + BELOW + j * LANES, LANES), :] = jnp.where(row >= column, diagonal_ref[j], value)
        edges.append(jnp.sum(jnp.where(row == column, value, 0.0), axis=0, keepdims=True))

    triangle(own_ref, other_ref, store_below, store_diagonal)
    edges.append(jnp.zeros((PACKED - EDGE - BLOCKS, LANES), jnp.float32))
    whole_ref[pl.ds(EDGE - BASES[1], PACKED - EDGE), :] = jnp.concatenate(edges)
    split_pieces(1, whole_ref, 0, keep_b_ref, send_b_ref)
    split_pieces(2, whole_ref, BASES[2] - BASES[1], keep_c_ref, send_c_ref)


def cross_gram(rest, diagonal, own, other):
    return pl.pallas_call(
        cross_gram_kernel,
        out_shape=half_shapes(1, own.dtype) + half_shapes(2, own.dtype),
        scratch_shapes=[pltpu.VMEM((PACKED - BASES[1], LANES), jnp.float32)],
        compiler_params=pltpu.CompilerParams(vmem_limit_bytes=12 * MIB),
        cost_estimate=pl.CostEstimate(
            flops=2 * (BELOW + 3 * HALF) * LANES * WIDTH, bytes_accessed=4 * HALF * WIDTH, transcendentals=0
        ),
        name="cross_gram",
    )(rest, diagonal, own, other)


def exchange(value, stream, hop):
    pairs = []
    for x in range(4):
        for d in range(2):
            for core in range(2):
                axis = ORDERS[core][stream][hop]
                to = {"a": (x ^ 1, d), "b": (3 - x, d), "d": (x, 1 - d)}[axis]
                pairs.append((4 * x + 2 * d + core, 4 * to[0] + 2 * to[1] + core))
    return lax.ppermute(value, ("x", "yh", "c"), pairs)


def wide(value):
    return value.astype(jnp.float32)


def after(value, *others):
    return lax.optimization_barrier((value, *others))[0]


def sum_over_chips(stream, keep, arrived, *others):
    kind = arrived.dtype
    half = (keep + wide(arrived)).astype(kind).reshape(2, 2, *keep.shape[1:])
    half = (wide(half) + wide(after(exchange(half, stream, 1), *others))[::-1]).astype(kind)
    half = (wide(half) + wide(exchange(half, stream, 2))[:, ::-1]).astype(kind).reshape(arrived.shape)
    return jnp.concatenate([half, exchange(half, stream, 0)])


def unpermute(pieces_ref, packed_ref, core):
    first = 0
    for s, rows in enumerate(PIECES):
        for k in range(CHIPS):
            packed_ref[piece_rows(s, k, BASES[s], core), :] = pieces_ref[k, pl.ds(first, rows), :]
        first += rows


def mirror(packed_ref, out_ref, lower):
    for j in range(BLOCKS):
        first = j * LANES
        block = packed_ref[pl.ds(2 * BELOW + first, LANES), :]
        out_ref[pl.ds(first, LANES), tile(j)] = jnp.where(lower, block, block.T)
        if j + 1 < BLOCKS:
            below = packed_ref[strip(j), :]
            out_ref[pl.ds(first + LANES, below.shape[0]), tile(j)] = below
            out_ref[pl.ds(first, LANES), pl.ds(first + LANES, below.shape[0])] = below.T


def own_square_kernel(pieces_ref, packed_ref, gram_ref, square_ref):
    row, column = iotas()
    unpermute(pieces_ref, packed_ref, lax.axis_index("c"))
    mirror(packed_ref, gram_ref, row >= column)
    for n in range(0, HALF, 256):
        columns = pl.ds(n, 256)
        square_ref[:, columns] = jnp.dot(gram_ref[...], gram_ref[:, columns], preferred_element_type=jnp.float32)


def own_square(pieces):
    return pl.pallas_call(
        own_square_kernel,
        out_shape=(
            jax.ShapeDtypeStruct((PACKED, LANES), pieces.dtype),
            jax.ShapeDtypeStruct((HALF, HALF), pieces.dtype),
            jax.ShapeDtypeStruct((HALF, HALF), jnp.float32),
        ),
        compiler_params=pltpu.CompilerParams(vmem_limit_bytes=12 * MIB),
        cost_estimate=pl.CostEstimate(
            flops=2 * HALF * HALF * HALF, bytes_accessed=8 * HALF * HALF, transcendentals=0
        ),
        name="own_square",
    )(pieces)


def unpack_cross(own_ref, other_ref, cross_ref):
    row, column = iotas()
    for j in range(BLOCKS):
        first = j * LANES
        upper, theirs = (ref[pl.ds(2 * BELOW + first, LANES), :] for ref in (own_ref, other_ref))
        edge = jnp.broadcast_to(own_ref[pl.ds(EDGE, 16), :].astype(jnp.float32)[j : j + 1], (LANES, LANES))
        block = jnp.where(row < column, upper.astype(jnp.float32), theirs.T.astype(jnp.float32))
        cross_ref[pl.ds(first, LANES), tile(j)] = jnp.where(row == column, edge, block).astype(cross_ref.dtype)
        if j + 1 < BLOCKS:
            rows = pl.ds(BELOW + strip(j).start, strip(j).size)
            cross_ref[pl.ds(first + LANES, rows.size), tile(j)] = own_ref[rows, :]
            cross_ref[pl.ds(first, LANES), pl.ds(first + LANES, rows.size)] = other_ref[rows, :].T


def update_kernel(
    own_ref, pieces_ref, gram_ref, square_ref, x_ref, x_other_ref, out_ref,
    other_ref, cross_ref, gram_other_ref, mixing_ref,
):
    scale = math.sqrt(max(ROWS, COLS))
    step = 256
    row, column = iotas()
    unpermute(pieces_ref, other_ref, 1 - lax.axis_index("c"))
    unpack_cross(own_ref, other_ref, cross_ref)
    mirror(other_ref, gram_other_ref, row >= column)
    for n in range(0, HALF, step):
        columns = pl.ds(n, step)
        square = square_ref[:, columns] + lax.dot_general(
            cross_ref[...], cross_ref[columns, :], (((1,), (1,)), ((), ())), preferred_element_type=jnp.float32
        )
        gram = gram_ref[:, columns].astype(jnp.float32)
        mixing_ref[:, columns] = (coeff_b * gram + coeff_c * square).astype(mixing_ref.dtype)
    for n in range(0, HALF, step):
        columns = pl.ds(n, step)
        square = jnp.dot(gram_ref[...], cross_ref[:, columns], preferred_element_type=jnp.float32)
        square += jnp.dot(cross_ref[...], gram_other_ref[:, columns], preferred_element_type=jnp.float32)
        gram = cross_ref[:, columns].astype(jnp.float32)
        mixing_ref[:, pl.ds(HALF + n, step)] = (coeff_b * gram + coeff_c * square).astype(mixing_ref.dtype)
    for t in range(0, TILES, 2):
        columns = pl.ds(t * LANES, 2 * LANES)
        result = jnp.dot(mixing_ref[:, pl.ds(0, HALF)], x_ref[:, columns], preferred_element_type=jnp.float32)
        result += jnp.dot(mixing_ref[:, pl.ds(HALF, HALF)], x_other_ref[:, columns], preferred_element_type=jnp.float32)
        result = scale * (coeff_a * x_ref[:, columns].astype(jnp.float32) + result)
        for i in range(2):
            block = result[:, i * LANES : (i + 1) * LANES].reshape(CHIPS, PANEL, LANES)
            j = t + i
            if j < STRIPES:
                out_ref[j, :, pl.ds(0, PANEL), :] = block.astype(out_ref.dtype)
            else:
                top, bottom = block[:, : PANEL // 2], block[:, PANEL // 2 :]
                for side in range(2):
                    packed = halves(top, bottom, side == 0).astype(out_ref.dtype)
                    out_ref[2 * (j - STRIPES) + side, :, pl.ds(PANEL, PANEL // 2), :] = packed


def update_rows(*operands):
    kind = operands[0].dtype
    return pl.pallas_call(
        update_kernel,
        out_shape=jax.ShapeDtypeStruct((STRIPES, CHIPS, PANEL + PANEL // 2, LANES), kind),
        scratch_shapes=[
            pltpu.VMEM((PACKED, LANES), kind),
            pltpu.VMEM((HALF, HALF), kind),
            pltpu.VMEM((HALF, HALF), kind),
            pltpu.VMEM((HALF, ROWS), kind),
        ],
        compiler_params=pltpu.CompilerParams(vmem_limit_bytes=24 * MIB),
        cost_estimate=pl.CostEstimate(
            flops=4 * HALF * ROWS * ROWS - 2 * HALF * HALF * HALF, bytes_accessed=10 * HALF * ROWS, transcendentals=0
        ),
        name="update_rows",
    )(*operands)


def join_kernel(pieces_ref, out_ref, whole_ref, sems):
    copies = []
    for layer in range(STRIPES):
        for p in range(CHIPS):
            whole_ref[layer, :, tile(p)] = pieces_ref[layer, p, pl.ds(0, PANEL), :]
        for pair in range(CHIPS // 2):
            left = pieces_ref[layer, 2 * pair, pl.ds(PANEL, PANEL // 2), :]
            right = pieces_ref[layer, 2 * pair + 1, pl.ds(PANEL, PANEL // 2), :]
            for part in range(2):
                joined = halves(left, right, part == 0).astype(whole_ref.dtype)
                whole_ref[layer, pl.ds(part * PANEL // 2, PANEL // 2), tile(CHIPS + pair)] = joined
        copies.append(pltpu.make_async_copy(whole_ref.at[layer], out_ref.at[layer], sems.at[layer]))
        copies[-1].start()
    for copy in copies:
        copy.wait()


def join_columns(pieces):
    shape = (pieces.shape[0], PANEL, TILES * LANES)
    return pl.pallas_call(
        join_kernel,
        in_specs=[pl.BlockSpec(memory_space=pltpu.VMEM)],
        out_specs=pl.BlockSpec(memory_space=pl.ANY),
        out_shape=jax.ShapeDtypeStruct(shape, pieces.dtype),
        scratch_shapes=[pltpu.VMEM(shape, pieces.dtype), pltpu.SemaphoreType.DMA((pieces.shape[0],))],
        compiler_params=pltpu.CompilerParams(vmem_limit_bytes=12 * MIB),
        name="join_columns",
    )(pieces)


def swap_cores(value):
    return lax.ppermute(value, "c", [(0, 1), (1, 0)])


def shards(iterate):
    pieces = split_columns(iterate.reshape(PANEL, COLS))
    own = lax.all_to_all(pieces, CHIP_AXES, 0, 0, tiled=True).reshape(HALF, WIDTH)
    other = swap_cores(own)
    keep_a, send_a, *rest = own_gram(own)
    arrived_a = exchange(send_a, 0, 0)
    keep_b, send_b, keep_c, send_c = cross_gram(*rest, own, other)
    arrived_b, arrived_c = exchange(send_b, 1, 0), exchange(send_c, 2, 0)
    streams = [
        sum_over_chips(0, keep_a, after(arrived_a, send_b, send_c), arrived_b),
        sum_over_chips(1, keep_b, arrived_b),
        sum_over_chips(2, keep_c, arrived_c),
    ]
    pieces = jnp.concatenate(streams, axis=1)
    pieces_other = swap_cores(pieces)
    packed, gram, square = own_square(pieces)
    sent = update_rows(packed, pieces_other, gram, square, own, other)
    sent = sent.reshape(STRIPES * CHIPS, PANEL + PANEL // 2, LANES)
    received = lax.all_to_all(sent, ALL_CHIPS, 0, 0, tiled=True)
    return join_columns(received.reshape(STRIPES, CHIPS, PANEL + PANEL // 2, LANES))


def solution(mesh):
    fine = Mesh(mesh.devices.reshape(4, 2, 4, 2, 2), ("z", "yl", "x", "yh", "c"))
    return jax.shard_map(
        shards,
        mesh=fine,
        in_specs=(P(("z", "yl"), ("x", "yh", "c"), None),),
        out_specs=P(None, ("x", "yh", "c"), ("z", "yl")),
        check_vma=False,
    )
```

```python
import math

import jax
import jax.numpy as jnp
from jax import lax
from jax.experimental import pallas as pl
from jax.experimental.pallas import tpu as pltpu
from jax.sharding import Mesh, PartitionSpec as P

coeff_a = 3.4445
coeff_b = -4.775
coeff_c = 2.0315

ROWS = 1536
COLS = 12288
LANES = 128
CHIPS = 8
STRIPES = 8
PANEL = ROWS // (2 * CHIPS)
HALF = ROWS // 2
WIDTH = COLS // CHIPS
TILES = COLS // STRIPES // LANES
BLOCKS = HALF // LANES
BELOW = LANES * BLOCKS * (BLOCKS - 1) // 2
EDGE = 2 * BELOW + HALF
PACKED = -(-(EDGE + BLOCKS) // (16 * CHIPS)) * 16 * CHIPS
PIECES = (240, 176, 176)
BASES = (0, CHIPS * PIECES[0], CHIPS * (PIECES[0] + PIECES[1]))
MIB = 1 << 20

CHIP_AXES = ("x", "yh")
ALL_CHIPS = ("z", "yl", "x", "yh")
ORDERS = (("abd", "bda", "dab"), ("bda", "dab", "abd"))


def halves(a, b, first):
    a, b = a.astype(jnp.float32), b.astype(jnp.float32)
    low = lax.broadcasted_iota(jnp.int32, a.shape, a.ndim - 1) < LANES // 2
    if first:
        return jnp.where(low, a, pltpu.roll(b, LANES // 2, a.ndim - 1))
    return jnp.where(low, pltpu.roll(a, LANES // 2, a.ndim - 1), b)


def tile(index):
    return pl.ds(index * LANES, LANES)


def place(stream, core):
    x, d = lax.axis_index("x"), lax.axis_index("yh")
    bit = {"a": lax.rem((x + 1) // 2, 2), "b": x // 2, "d": d}
    places = [4 * bit[i] + 2 * bit[j] + bit[k] for i, j, k in (orders[stream] for orders in ORDERS)]
    return places[0] + core * (places[1] - places[0])


def piece_rows(stream, position, base, core):
    piece = lax.bitwise_xor(place(stream, core), position)
    return pl.ds(base + pl.multiple_of(piece * PIECES[stream], 16), PIECES[stream])


def split_pieces(stream, whole_ref, base, keep_ref, send_ref):
    half, core = CHIPS // 2, lax.axis_index("c")
    for k in range(half):
        keep_ref[k] = whole_ref[piece_rows(stream, k, base, core), :]
        send_ref[k] = whole_ref[piece_rows(stream, k + half, base, core), :].astype(send_ref.dtype)


def half_shapes(stream, kind):
    shape = (CHIPS // 2, PIECES[stream], LANES)
    return [jax.ShapeDtypeStruct(shape, jnp.float32), jax.ShapeDtypeStruct(shape, kind)]


def split_kernel(x_ref, out_ref):
    for p in range(CHIPS):
        for j in range(STRIPES):
            out_ref[p, :, tile(j)] = x_ref[:, tile(TILES * j + p)]
        for m in range(STRIPES // 2):
            left = x_ref[:, tile(TILES * (2 * m) + CHIPS + p // 2)]
            right = x_ref[:, tile(TILES * (2 * m + 1) + CHIPS + p // 2)]
            out_ref[p, :, tile(STRIPES + m)] = halves(left, right, p % 2 == 0).astype(out_ref.dtype)


def split_columns(x):
    return pl.pallas_call(
        split_kernel,
        out_shape=jax.ShapeDtypeStruct((CHIPS, PANEL, WIDTH), x.dtype),
        compiler_params=pltpu.CompilerParams(vmem_limit_bytes=16 * MIB),
        name="split_columns",
    )(x)


def strip(j):
    below = (BLOCKS - 1 - j) * LANES
    start = LANES * sum(BLOCKS - 1 - i for i in range(j))
    return pl.ds(start, below)


def triangle(own_ref, ref, store_below, store_diagonal):
    for j in range(0, BLOCKS, 2):
        first = j * LANES
        part = lax.dot_general(
            own_ref[pl.ds(first, HALF - first), :],
            ref[pl.ds(first, 2 * LANES), :],
            (((1,), (1,)), ((), ())),
            preferred_element_type=jnp.float32,
        )
        for i in range(2):
            columns = part[i * LANES :, i * LANES : (i + 1) * LANES]
            store_diagonal(j + i, columns[:LANES])
            if j + i + 1 < BLOCKS:
                store_below(strip(j + i), columns[LANES:])


def iotas():
    return [lax.broadcasted_iota(jnp.int32, (LANES, LANES), axis) for axis in range(2)]


def own_gram_kernel(own_ref, keep_ref, send_ref, diagonal_ref, whole_ref):
    def store_below(rows, value):
        whole_ref[rows, :] = value

    def store_diagonal(j, value):
        diagonal_ref[j] = value

    triangle(own_ref, own_ref, store_below, store_diagonal)
    split_pieces(0, whole_ref, 0, keep_ref, send_ref)


def own_gram(own):
    return pl.pallas_call(
        own_gram_kernel,
        out_shape=half_shapes(0, own.dtype) + [jax.ShapeDtypeStruct((BLOCKS, LANES, LANES), jnp.float32)],
        scratch_shapes=[pltpu.VMEM((BELOW, LANES), jnp.float32)],
        compiler_params=pltpu.CompilerParams(vmem_limit_bytes=8 * MIB),
        cost_estimate=pl.CostEstimate(
            flops=2 * (BELOW + 3 * HALF) * LANES * WIDTH, bytes_accessed=2 * HALF * WIDTH, transcendentals=0
        ),
        name="own_gram",
    )(own)


def cross_gram_kernel(
    diagonal_ref, own_ref, other_ref, keep_b_ref, send_b_ref, keep_c_ref, send_c_ref, whole_ref
):
    row, column = iotas()
    edges = []

    def store_below(rows, value):
        whole_ref[rows, :] = value

    def store_diagonal(j, value):
        whole_ref[pl.ds(BELOW + j * LANES, LANES), :] = jnp.where(row >= column, diagonal_ref[j], value)
        edges.append(jnp.sum(jnp.where(row == column, value, 0.0), axis=0, keepdims=True))

    triangle(own_ref, other_ref, store_below, store_diagonal)
    edges.append(jnp.zeros((PACKED - EDGE - BLOCKS, LANES), jnp.float32))
    whole_ref[pl.ds(EDGE - BASES[1], PACKED - EDGE), :] = jnp.concatenate(edges)
    split_pieces(1, whole_ref, 0, keep_b_ref, send_b_ref)
    split_pieces(2, whole_ref, BASES[2] - BASES[1], keep_c_ref, send_c_ref)


def cross_gram(diagonal, own, other):
    return pl.pallas_call(
        cross_gram_kernel,
        out_shape=half_shapes(1, own.dtype) + half_shapes(2, own.dtype),
        scratch_shapes=[pltpu.VMEM((PACKED - BASES[1], LANES), jnp.float32)],
        compiler_params=pltpu.CompilerParams(vmem_limit_bytes=12 * MIB),
        cost_estimate=pl.CostEstimate(
            flops=2 * (BELOW + 3 * HALF) * LANES * WIDTH, bytes_accessed=4 * HALF * WIDTH, transcendentals=0
        ),
        name="cross_gram",
    )(diagonal, own, other)


def exchange(value, stream, hop):
    pairs = []
    for x in range(4):
        for d in range(2):
            for core in range(2):
                axis = ORDERS[core][stream][hop]
                to = {"a": (x ^ 1, d), "b": (3 - x, d), "d": (x, 1 - d)}[axis]
                pairs.append((4 * x + 2 * d + core, 4 * to[0] + 2 * to[1] + core))
    return lax.ppermute(value, ("x", "yh", "c"), pairs)


def wide(value):
    return value.astype(jnp.float32)


def after(value, *others):
    return lax.optimization_barrier((value, *others))[0]


def sum_over_chips(stream, keep, arrived, *others):
    kind = arrived.dtype
    half = (keep + wide(arrived)).astype(kind).reshape(2, 2, *keep.shape[1:])
    half = (wide(half) + wide(after(exchange(half, stream, 1), *others))[::-1]).astype(kind)
    half = (wide(half) + wide(exchange(half, stream, 2))[:, ::-1]).astype(kind).reshape(arrived.shape)
    return jnp.concatenate([half, exchange(half, stream, 0)])


def unpermute(first_ref, rest_ref, packed_ref, core):
    places = ((first_ref, 0), (rest_ref, 0), (rest_ref, PIECES[1]))
    for s, (pieces_ref, start) in enumerate(places):
        for k in range(CHIPS):
            packed_ref[piece_rows(s, k, BASES[s], core), :] = pieces_ref[k, pl.ds(start, PIECES[s]), :]


def mirror(packed_ref, out_ref, lower):
    for j in range(BLOCKS):
        first = j * LANES
        block = packed_ref[pl.ds(2 * BELOW + first, LANES), :]
        out_ref[pl.ds(first, LANES), tile(j)] = jnp.where(lower, block, block.T)
        if j + 1 < BLOCKS:
            below = packed_ref[strip(j), :]
            out_ref[pl.ds(first + LANES, below.shape[0]), tile(j)] = below
            out_ref[pl.ds(first, LANES), pl.ds(first + LANES, below.shape[0])] = below.T


def own_square_kernel(first_ref, rest_ref, packed_ref, gram_ref, square_ref):
    row, column = iotas()
    unpermute(first_ref, rest_ref, packed_ref, lax.axis_index("c"))
    mirror(packed_ref, gram_ref, row >= column)
    for n in range(0, HALF, 256):
        columns = pl.ds(n, 256)
        square_ref[:, columns] = jnp.dot(gram_ref[...], gram_ref[:, columns], preferred_element_type=jnp.float32)


def own_square(first, rest):
    return pl.pallas_call(
        own_square_kernel,
        out_shape=(
            jax.ShapeDtypeStruct((PACKED, LANES), first.dtype),
            jax.ShapeDtypeStruct((HALF, HALF), first.dtype),
            jax.ShapeDtypeStruct((HALF, HALF), jnp.float32),
        ),
        compiler_params=pltpu.CompilerParams(vmem_limit_bytes=12 * MIB),
        cost_estimate=pl.CostEstimate(
            flops=2 * HALF * HALF * HALF, bytes_accessed=8 * HALF * HALF, transcendentals=0
        ),
        name="own_square",
    )(first, rest)


def unpack_cross(own_ref, other_ref, cross_ref):
    row, column = iotas()
    for j in range(BLOCKS):
        first = j * LANES
        upper, theirs = (ref[pl.ds(2 * BELOW + first, LANES), :] for ref in (own_ref, other_ref))
        edge = jnp.broadcast_to(own_ref[pl.ds(EDGE, 16), :].astype(jnp.float32)[j : j + 1], (LANES, LANES))
        block = jnp.where(row < column, upper.astype(jnp.float32), theirs.T.astype(jnp.float32))
        cross_ref[pl.ds(first, LANES), tile(j)] = jnp.where(row == column, edge, block).astype(cross_ref.dtype)
        if j + 1 < BLOCKS:
            rows = pl.ds(BELOW + strip(j).start, strip(j).size)
            cross_ref[pl.ds(first + LANES, rows.size), tile(j)] = own_ref[rows, :]
            cross_ref[pl.ds(first, LANES), pl.ds(first + LANES, rows.size)] = other_ref[rows, :].T


def update_kernel(
    own_ref, first_ref, rest_ref, gram_ref, square_ref, x_ref, x_other_ref, out_ref,
    other_ref, cross_ref, gram_other_ref, mixing_ref,
):
    scale = math.sqrt(max(ROWS, COLS))
    step = 256
    row, column = iotas()
    unpermute(first_ref, rest_ref, other_ref, 1 - lax.axis_index("c"))
    unpack_cross(own_ref, other_ref, cross_ref)
    mirror(other_ref, gram_other_ref, row >= column)
    for n in range(0, HALF, step):
        columns = pl.ds(n, step)
        square = square_ref[:, columns] + lax.dot_general(
            cross_ref[...], cross_ref[columns, :], (((1,), (1,)), ((), ())), preferred_element_type=jnp.float32
        )
        gram = gram_ref[:, columns].astype(jnp.float32)
        mixing_ref[:, columns] = (coeff_b * gram + coeff_c * square).astype(mixing_ref.dtype)
    for n in range(0, HALF, step):
        columns = pl.ds(n, step)
        square = jnp.dot(gram_ref[...], cross_ref[:, columns], preferred_element_type=jnp.float32)
        square += jnp.dot(cross_ref[...], gram_other_ref[:, columns], preferred_element_type=jnp.float32)
        gram = cross_ref[:, columns].astype(jnp.float32)
        mixing_ref[:, pl.ds(HALF + n, step)] = (coeff_b * gram + coeff_c * square).astype(mixing_ref.dtype)
    for t in range(0, TILES, 2):
        columns = pl.ds(t * LANES, 2 * LANES)
        result = jnp.dot(mixing_ref[:, pl.ds(0, HALF)], x_ref[:, columns], preferred_element_type=jnp.float32)
        result += jnp.dot(mixing_ref[:, pl.ds(HALF, HALF)], x_other_ref[:, columns], preferred_element_type=jnp.float32)
        result = scale * (coeff_a * x_ref[:, columns].astype(jnp.float32) + result)
        for i in range(2):
            block = result[:, i * LANES : (i + 1) * LANES].reshape(CHIPS, PANEL, LANES)
            j = t + i
            if j < STRIPES:
                out_ref[j, :, pl.ds(0, PANEL), :] = block.astype(out_ref.dtype)
            else:
                top, bottom = block[:, : PANEL // 2], block[:, PANEL // 2 :]
                for side in range(2):
                    packed = halves(top, bottom, side == 0).astype(out_ref.dtype)
                    out_ref[2 * (j - STRIPES) + side, :, pl.ds(PANEL, PANEL // 2), :] = packed


def update_rows(*operands):
    kind = operands[0].dtype
    return pl.pallas_call(
        update_kernel,
        out_shape=jax.ShapeDtypeStruct((STRIPES, CHIPS, PANEL + PANEL // 2, LANES), kind),
        scratch_shapes=[
            pltpu.VMEM((PACKED, LANES), kind),
            pltpu.VMEM((HALF, HALF), kind),
            pltpu.VMEM((HALF, HALF), kind),
            pltpu.VMEM((HALF, ROWS), kind),
        ],
        compiler_params=pltpu.CompilerParams(vmem_limit_bytes=24 * MIB),
        cost_estimate=pl.CostEstimate(
            flops=4 * HALF * ROWS * ROWS - 2 * HALF * HALF * HALF, bytes_accessed=10 * HALF * ROWS, transcendentals=0
        ),
        name="update_rows",
    )(*operands)


def join_kernel(pieces_ref, out_ref, whole_ref, sems):
    copies = []
    for layer in range(STRIPES):
        for p in range(CHIPS):
            whole_ref[layer, :, tile(p)] = pieces_ref[layer, p, pl.ds(0, PANEL), :]
        for pair in range(CHIPS // 2):
            left = pieces_ref[layer, 2 * pair, pl.ds(PANEL, PANEL // 2), :]
            right = pieces_ref[layer, 2 * pair + 1, pl.ds(PANEL, PANEL // 2), :]
            for part in range(2):
                joined = halves(left, right, part == 0).astype(whole_ref.dtype)
                whole_ref[layer, pl.ds(part * PANEL // 2, PANEL // 2), tile(CHIPS + pair)] = joined
        copies.append(pltpu.make_async_copy(whole_ref.at[layer], out_ref.at[layer], sems.at[layer]))
        copies[-1].start()
    for copy in copies:
        copy.wait()


def join_columns(pieces):
    shape = (pieces.shape[0], PANEL, TILES * LANES)
    return pl.pallas_call(
        join_kernel,
        in_specs=[pl.BlockSpec(memory_space=pltpu.VMEM)],
        out_specs=pl.BlockSpec(memory_space=pl.ANY),
        out_shape=jax.ShapeDtypeStruct(shape, pieces.dtype),
        scratch_shapes=[pltpu.VMEM(shape, pieces.dtype), pltpu.SemaphoreType.DMA((pieces.shape[0],))],
        compiler_params=pltpu.CompilerParams(vmem_limit_bytes=12 * MIB),
        name="join_columns",
    )(pieces)


def swap_cores(value):
    return lax.ppermute(value, "c", [(0, 1), (1, 0)])


def shards(iterate):
    pieces = split_columns(iterate.reshape(PANEL, COLS))
    own = lax.all_to_all(pieces, CHIP_AXES, 0, 0, tiled=True).reshape(HALF, WIDTH)
    other = swap_cores(own)
    keep_a, send_a, diagonal = own_gram(own)
    arrived_a = exchange(send_a, 0, 0)
    keep_b, send_b, keep_c, send_c = cross_gram(diagonal, own, other)
    arrived_b, arrived_c = exchange(send_b, 1, 0), exchange(send_c, 2, 0)
    streams = [
        sum_over_chips(0, keep_a, after(arrived_a, send_b, send_c), arrived_b),
        sum_over_chips(1, keep_b, arrived_b),
        sum_over_chips(2, keep_c, arrived_c),
    ]
    first, rest = streams[0], jnp.concatenate(streams[1:], axis=1)
    first_other = swap_cores(first)
    rest_other = swap_cores(after(rest, first_other))
    packed, gram, square = own_square(first, rest)
    sent = update_rows(packed, first_other, rest_other, gram, square, own, other)
    sent = sent.reshape(STRIPES * CHIPS, PANEL + PANEL // 2, LANES)
    received = lax.all_to_all(sent, ALL_CHIPS, 0, 0, tiled=True)
    return join_columns(received.reshape(STRIPES, CHIPS, PANEL + PANEL // 2, LANES))


def solution(mesh):
    fine = Mesh(mesh.devices.reshape(4, 2, 4, 2, 2), ("z", "yl", "x", "yh", "c"))
    return jax.shard_map(
        shards,
        mesh=fine,
        in_specs=(P(("z", "yl"), ("x", "yh", "c"), None),),
        out_specs=P(None, ("x", "yh", "c"), ("z", "yl")),
        check_vma=False,
    )
```

```python
import math

import jax
import jax.numpy as jnp
from jax import lax
from jax.experimental import pallas as pl
from jax.experimental.pallas import tpu as pltpu
from jax.sharding import Mesh, PartitionSpec as P

coeff_a = 3.4445
coeff_b = -4.775
coeff_c = 2.0315

ROWS = 1536
COLS = 12288
LANES = 128
CHIPS = 8
STRIPES = 8
PANEL = ROWS // (2 * CHIPS)
HALF = ROWS // 2
WIDTH = COLS // CHIPS
TILES = COLS // STRIPES // LANES
BLOCKS = HALF // LANES
BELOW = LANES * BLOCKS * (BLOCKS - 1) // 2
EDGE = 2 * BELOW + HALF
PACKED = -(-(EDGE + BLOCKS) // (16 * CHIPS)) * 16 * CHIPS
PIECES = (240, 192, 160)
BASES = (0, CHIPS * PIECES[0], CHIPS * (PIECES[0] + PIECES[1]))
MIB = 1 << 20

CHIP_AXES = ("x", "yh")
ALL_CHIPS = ("z", "yl", "x", "yh")
ORDERS = (("abd", "bda", "dab"), ("bda", "dab", "abd"))


def halves(a, b, first):
    a, b = a.astype(jnp.float32), b.astype(jnp.float32)
    low = lax.broadcasted_iota(jnp.int32, a.shape, a.ndim - 1) < LANES // 2
    if first:
        return jnp.where(low, a, pltpu.roll(b, LANES // 2, a.ndim - 1))
    return jnp.where(low, pltpu.roll(a, LANES // 2, a.ndim - 1), b)


def tile(index):
    return pl.ds(index * LANES, LANES)


def place(stream, core):
    x, d = lax.axis_index("x"), lax.axis_index("yh")
    bit = {"a": lax.rem((x + 1) // 2, 2), "b": x // 2, "d": d}
    places = [4 * bit[i] + 2 * bit[j] + bit[k] for i, j, k in (orders[stream] for orders in ORDERS)]
    return places[0] + core * (places[1] - places[0])


def piece_rows(stream, position, base, core):
    piece = lax.bitwise_xor(place(stream, core), position)
    return pl.ds(base + pl.multiple_of(piece * PIECES[stream], 16), PIECES[stream])


def split_pieces(stream, whole_ref, base, keep_ref, send_ref):
    half, core = CHIPS // 2, lax.axis_index("c")
    for k in range(half):
        keep_ref[k] = whole_ref[piece_rows(stream, k, base, core), :]
        send_ref[k] = whole_ref[piece_rows(stream, k + half, base, core), :].astype(send_ref.dtype)


def half_shapes(stream, kind):
    shape = (CHIPS // 2, PIECES[stream], LANES)
    return [jax.ShapeDtypeStruct(shape, jnp.float32), jax.ShapeDtypeStruct(shape, kind)]


def split_kernel(x_ref, out_ref):
    for p in range(CHIPS):
        for j in range(STRIPES):
            out_ref[p, :, tile(j)] = x_ref[:, tile(TILES * j + p)]
        for m in range(STRIPES // 2):
            left = x_ref[:, tile(TILES * (2 * m) + CHIPS + p // 2)]
            right = x_ref[:, tile(TILES * (2 * m + 1) + CHIPS + p // 2)]
            out_ref[p, :, tile(STRIPES + m)] = halves(left, right, p % 2 == 0).astype(out_ref.dtype)


def split_columns(x):
    return pl.pallas_call(
        split_kernel,
        out_shape=jax.ShapeDtypeStruct((CHIPS, PANEL, WIDTH), x.dtype),
        compiler_params=pltpu.CompilerParams(vmem_limit_bytes=16 * MIB),
        name="split_columns",
    )(x)


def strip(j):
    below = (BLOCKS - 1 - j) * LANES
    start = LANES * sum(BLOCKS - 1 - i for i in range(j))
    return pl.ds(start, below)


def triangle(own_ref, ref, groups, store_below, store_diagonal):
    for group in groups:
        first = group[0] * LANES
        part = lax.dot_general(
            own_ref[pl.ds(first, HALF - first), :],
            ref[pl.ds(first, len(group) * LANES), :],
            (((1,), (1,)), ((), ())),
            preferred_element_type=jnp.float32,
        )
        for i, j in enumerate(group):
            columns = part[i * LANES :, i * LANES : (i + 1) * LANES]
            store_diagonal(j, columns[:LANES])
            if j + 1 < BLOCKS:
                store_below(strip(j), columns[LANES:])


def iotas():
    return [lax.broadcasted_iota(jnp.int32, (LANES, LANES), axis) for axis in range(2)]


def own_gram_kernel(own_ref, keep_ref, send_ref, diagonal_ref, whole_ref):
    def store_below(rows, value):
        whole_ref[rows, :] = value

    def store_diagonal(j, value):
        diagonal_ref[j] = value

    triangle(own_ref, own_ref, ((0, 1), (2, 3), (4, 5)), store_below, store_diagonal)
    split_pieces(0, whole_ref, 0, keep_ref, send_ref)


def own_gram(own):
    return pl.pallas_call(
        own_gram_kernel,
        out_shape=half_shapes(0, own.dtype) + [jax.ShapeDtypeStruct((BLOCKS, LANES, LANES), jnp.float32)],
        scratch_shapes=[pltpu.VMEM((BELOW, LANES), jnp.float32)],
        compiler_params=pltpu.CompilerParams(vmem_limit_bytes=8 * MIB),
        cost_estimate=pl.CostEstimate(
            flops=2 * (BELOW + 3 * HALF) * LANES * WIDTH, bytes_accessed=2 * HALF * WIDTH, transcendentals=0
        ),
        name="own_gram",
    )(own)


def cross_first_kernel(own_ref, other_ref, keep_ref, send_ref, diagonal_ref, whole_ref):
    def store_below(rows, value):
        whole_ref[rows, :] = value

    def store_diagonal(j, value):
        diagonal_ref[j] = value

    triangle(own_ref, other_ref, ((0, 1), (2,)), store_below, store_diagonal)
    split_pieces(1, whole_ref, 0, keep_ref, send_ref)


def cross_first(own, other):
    return pl.pallas_call(
        cross_first_kernel,
        out_shape=half_shapes(1, own.dtype) + [jax.ShapeDtypeStruct((BLOCKS // 2, LANES, LANES), jnp.float32)],
        scratch_shapes=[pltpu.VMEM((BASES[2] - BASES[1], LANES), jnp.float32)],
        compiler_params=pltpu.CompilerParams(vmem_limit_bytes=8 * MIB),
        cost_estimate=pl.CostEstimate(
            flops=4 * HALF * 2 * LANES * WIDTH, bytes_accessed=4 * HALF * WIDTH, transcendentals=0
        ),
        name="cross_first",
    )(own, other)


def cross_rest_kernel(diagonal_ref, cross_ref, own_ref, other_ref, keep_ref, send_ref, whole_ref):
    row, column = iotas()
    edges = []

    def store_below(rows, value):
        whole_ref[pl.ds(BELOW + rows.start - BASES[2], rows.size), :] = value

    def store_diagonal(j, value):
        block = pl.ds(2 * BELOW + j * LANES - BASES[2], LANES)
        whole_ref[block, :] = jnp.where(row >= column, diagonal_ref[j], value)
        edges.append(jnp.sum(jnp.where(row == column, value, 0.0), axis=0, keepdims=True))

    for j in range(BLOCKS // 2):
        store_diagonal(j, cross_ref[j])
    triangle(own_ref, other_ref, ((3,), (4, 5)), store_below, store_diagonal)
    edges.append(jnp.zeros((PACKED - EDGE - BLOCKS, LANES), jnp.float32))
    whole_ref[pl.ds(EDGE - BASES[2], PACKED - EDGE), :] = jnp.concatenate(edges)
    split_pieces(2, whole_ref, 0, keep_ref, send_ref)


def cross_rest(diagonal, cross, own, other):
    return pl.pallas_call(
        cross_rest_kernel,
        out_shape=half_shapes(2, own.dtype),
        scratch_shapes=[pltpu.VMEM((PACKED - BASES[2], LANES), jnp.float32)],
        compiler_params=pltpu.CompilerParams(vmem_limit_bytes=8 * MIB),
        cost_estimate=pl.CostEstimate(
            flops=2 * HALF * 2 * LANES * WIDTH, bytes_accessed=2 * HALF * WIDTH, transcendentals=0
        ),
        name="cross_rest",
    )(diagonal, cross, own, other)


def exchange(value, stream, hop):
    pairs = []
    for x in range(4):
        for d in range(2):
            for core in range(2):
                axis = ORDERS[core][stream][hop]
                to = {"a": (x ^ 1, d), "b": (3 - x, d), "d": (x, 1 - d)}[axis]
                pairs.append((4 * x + 2 * d + core, 4 * to[0] + 2 * to[1] + core))
    return lax.ppermute(value, ("x", "yh", "c"), pairs)


def wide(value):
    return value.astype(jnp.float32)


def after(value, *others):
    return lax.optimization_barrier((value, *others))[0]


def sum_over_chips(stream, keep, arrived, *others):
    kind = arrived.dtype
    half = (keep + wide(arrived)).astype(kind).reshape(2, 2, *keep.shape[1:])
    half = (wide(half) + wide(after(exchange(half, stream, 1), *others))[::-1]).astype(kind)
    half = (wide(half) + wide(exchange(half, stream, 2))[:, ::-1]).astype(kind).reshape(arrived.shape)
    return jnp.concatenate([half, exchange(half, stream, 0)])


def unpermute(streams, packed_ref, core):
    for s, pieces_ref in enumerate(streams):
        for k in range(CHIPS):
            packed_ref[piece_rows(s, k, BASES[s], core), :] = pieces_ref[k]


def mirror(packed_ref, out_ref, lower):
    for j in range(BLOCKS):
        first = j * LANES
        block = packed_ref[pl.ds(2 * BELOW + first, LANES), :]
        out_ref[pl.ds(first, LANES), tile(j)] = jnp.where(lower, block, block.T)
        if j + 1 < BLOCKS:
            below = packed_ref[strip(j), :]
            out_ref[pl.ds(first + LANES, below.shape[0]), tile(j)] = below
            out_ref[pl.ds(first, LANES), pl.ds(first + LANES, below.shape[0])] = below.T


def own_square_kernel(a_ref, b_ref, c_ref, packed_ref, gram_ref, square_ref):
    row, column = iotas()
    unpermute((a_ref, b_ref, c_ref), packed_ref, lax.axis_index("c"))
    mirror(packed_ref, gram_ref, row >= column)
    for n in range(0, HALF, 256):
        columns = pl.ds(n, 256)
        square_ref[:, columns] = jnp.dot(gram_ref[...], gram_ref[:, columns], preferred_element_type=jnp.float32)


def own_square(*streams):
    return pl.pallas_call(
        own_square_kernel,
        out_shape=(
            jax.ShapeDtypeStruct((PACKED, LANES), streams[0].dtype),
            jax.ShapeDtypeStruct((HALF, HALF), streams[0].dtype),
            jax.ShapeDtypeStruct((HALF, HALF), jnp.float32),
        ),
        compiler_params=pltpu.CompilerParams(vmem_limit_bytes=12 * MIB),
        cost_estimate=pl.CostEstimate(
            flops=2 * HALF * HALF * HALF, bytes_accessed=8 * HALF * HALF, transcendentals=0
        ),
        name="own_square",
    )(*streams)


def unpack_cross(own_ref, other_ref, cross_ref):
    row, column = iotas()
    for j in range(BLOCKS):
        first = j * LANES
        upper, theirs = (ref[pl.ds(2 * BELOW + first, LANES), :] for ref in (own_ref, other_ref))
        edge = jnp.broadcast_to(own_ref[pl.ds(EDGE, 16), :].astype(jnp.float32)[j : j + 1], (LANES, LANES))
        block = jnp.where(row < column, upper.astype(jnp.float32), theirs.T.astype(jnp.float32))
        cross_ref[pl.ds(first, LANES), tile(j)] = jnp.where(row == column, edge, block).astype(cross_ref.dtype)
        if j + 1 < BLOCKS:
            rows = pl.ds(BELOW + strip(j).start, strip(j).size)
            cross_ref[pl.ds(first + LANES, rows.size), tile(j)] = own_ref[rows, :]
            cross_ref[pl.ds(first, LANES), pl.ds(first + LANES, rows.size)] = other_ref[rows, :].T


def update_kernel(
    own_ref, a_ref, b_ref, c_ref, gram_ref, square_ref, x_ref, x_other_ref, out_ref,
    other_ref, cross_ref, gram_other_ref, mixing_ref,
):
    scale = math.sqrt(max(ROWS, COLS))
    step = 256
    row, column = iotas()
    unpermute((a_ref, b_ref, c_ref), other_ref, 1 - lax.axis_index("c"))
    unpack_cross(own_ref, other_ref, cross_ref)
    mirror(other_ref, gram_other_ref, row >= column)
    for n in range(0, HALF, step):
        columns = pl.ds(n, step)
        square = square_ref[:, columns] + lax.dot_general(
            cross_ref[...], cross_ref[columns, :], (((1,), (1,)), ((), ())), preferred_element_type=jnp.float32
        )
        gram = gram_ref[:, columns].astype(jnp.float32)
        mixing_ref[:, columns] = (coeff_b * gram + coeff_c * square).astype(mixing_ref.dtype)
    for n in range(0, HALF, step):
        columns = pl.ds(n, step)
        square = jnp.dot(gram_ref[...], cross_ref[:, columns], preferred_element_type=jnp.float32)
        square += jnp.dot(cross_ref[...], gram_other_ref[:, columns], preferred_element_type=jnp.float32)
        gram = cross_ref[:, columns].astype(jnp.float32)
        mixing_ref[:, pl.ds(HALF + n, step)] = (coeff_b * gram + coeff_c * square).astype(mixing_ref.dtype)
    for t in range(0, TILES, 2):
        columns = pl.ds(t * LANES, 2 * LANES)
        result = jnp.dot(mixing_ref[:, pl.ds(0, HALF)], x_ref[:, columns], preferred_element_type=jnp.float32)
        result += jnp.dot(mixing_ref[:, pl.ds(HALF, HALF)], x_other_ref[:, columns], preferred_element_type=jnp.float32)
        result = scale * (coeff_a * x_ref[:, columns].astype(jnp.float32) + result)
        for i in range(2):
            block = result[:, i * LANES : (i + 1) * LANES].reshape(CHIPS, PANEL, LANES)
            j = t + i
            if j < STRIPES:
                out_ref[j, :, pl.ds(0, PANEL), :] = block.astype(out_ref.dtype)
            else:
                top, bottom = block[:, : PANEL // 2], block[:, PANEL // 2 :]
                for side in range(2):
                    packed = halves(top, bottom, side == 0).astype(out_ref.dtype)
                    out_ref[2 * (j - STRIPES) + side, :, pl.ds(PANEL, PANEL // 2), :] = packed


def update_rows(*operands):
    kind = operands[0].dtype
    return pl.pallas_call(
        update_kernel,
        out_shape=jax.ShapeDtypeStruct((STRIPES, CHIPS, PANEL + PANEL // 2, LANES), kind),
        scratch_shapes=[
            pltpu.VMEM((PACKED, LANES), kind),
            pltpu.VMEM((HALF, HALF), kind),
            pltpu.VMEM((HALF, HALF), kind),
            pltpu.VMEM((HALF, ROWS), kind),
        ],
        compiler_params=pltpu.CompilerParams(vmem_limit_bytes=24 * MIB),
        cost_estimate=pl.CostEstimate(
            flops=4 * HALF * ROWS * ROWS - 2 * HALF * HALF * HALF, bytes_accessed=10 * HALF * ROWS, transcendentals=0
        ),
        name="update_rows",
    )(*operands)


def join_kernel(pieces_ref, out_ref, whole_ref, sems):
    copies = []
    for layer in range(STRIPES):
        for p in range(CHIPS):
            whole_ref[layer, :, tile(p)] = pieces_ref[layer, p, pl.ds(0, PANEL), :]
        for pair in range(CHIPS // 2):
            left = pieces_ref[layer, 2 * pair, pl.ds(PANEL, PANEL // 2), :]
            right = pieces_ref[layer, 2 * pair + 1, pl.ds(PANEL, PANEL // 2), :]
            for part in range(2):
                joined = halves(left, right, part == 0).astype(whole_ref.dtype)
                whole_ref[layer, pl.ds(part * PANEL // 2, PANEL // 2), tile(CHIPS + pair)] = joined
        copies.append(pltpu.make_async_copy(whole_ref.at[layer], out_ref.at[layer], sems.at[layer]))
        copies[-1].start()
    for copy in copies:
        copy.wait()


def join_columns(pieces):
    shape = (pieces.shape[0], PANEL, TILES * LANES)
    return pl.pallas_call(
        join_kernel,
        in_specs=[pl.BlockSpec(memory_space=pltpu.VMEM)],
        out_specs=pl.BlockSpec(memory_space=pl.ANY),
        out_shape=jax.ShapeDtypeStruct(shape, pieces.dtype),
        scratch_shapes=[pltpu.VMEM(shape, pieces.dtype), pltpu.SemaphoreType.DMA((pieces.shape[0],))],
        compiler_params=pltpu.CompilerParams(vmem_limit_bytes=12 * MIB),
        name="join_columns",
    )(pieces)


def swap_cores(value):
    return lax.ppermute(value, "c", [(0, 1), (1, 0)])


def shards(iterate):
    pieces = split_columns(iterate.reshape(PANEL, COLS))
    own = lax.all_to_all(pieces, CHIP_AXES, 0, 0, tiled=True).reshape(HALF, WIDTH)
    other = swap_cores(own)
    keep_a, send_a, diagonal = own_gram(own)
    arrived_a = exchange(send_a, 0, 0)
    keep_b, send_b, cross = cross_first(own, other)
    arrived_b = exchange(send_b, 1, 0)
    keep_c, send_c = cross_rest(diagonal, cross, own, other)
    arrived_c = exchange(send_c, 2, 0)
    streams = [
        sum_over_chips(0, keep_a, after(arrived_a, send_b), arrived_b),
        sum_over_chips(1, keep_b, arrived_b),
        sum_over_chips(2, keep_c, arrived_c),
    ]
    others = [swap_cores(streams[0])]
    others += [swap_cores(after(stream, others[0])) for stream in streams[1:]]
    packed, gram, square = own_square(*streams)
    sent = update_rows(packed, *others, gram, square, own, other)
    sent = sent.reshape(STRIPES * CHIPS, PANEL + PANEL // 2, LANES)
    received = lax.all_to_all(sent, ALL_CHIPS, 0, 0, tiled=True)
    return join_columns(received.reshape(STRIPES, CHIPS, PANEL + PANEL // 2, LANES))


def solution(mesh):
    fine = Mesh(mesh.devices.reshape(4, 2, 4, 2, 2), ("z", "yl", "x", "yh", "c"))
    return jax.shard_map(
        shards,
        mesh=fine,
        in_specs=(P(("z", "yl"), ("x", "yh", "c"), None),),
        out_specs=P(None, ("x", "yh", "c"), ("z", "yl")),
        check_vma=False,
    )
```

```python
import math

import jax
import jax.numpy as jnp
from jax import lax
from jax.experimental import pallas as pl
from jax.experimental.pallas import tpu as pltpu
from jax.sharding import Mesh, PartitionSpec as P

coeff_a = 3.4445
coeff_b = -4.775
coeff_c = 2.0315

ROWS = 1536
COLS = 12288
LANES = 128
CHIPS = 8
STRIPES = 8
PANEL = ROWS // (2 * CHIPS)
HALF = ROWS // 2
WIDTH = COLS // CHIPS
TILES = COLS // STRIPES // LANES
BLOCKS = HALF // LANES
BELOW = LANES * BLOCKS * (BLOCKS - 1) // 2
EDGE = 2 * BELOW + HALF
PACKED = -(-(EDGE + BLOCKS) // (16 * CHIPS)) * 16 * CHIPS
PIECES = (240, 176, 176)
BASES = (0, CHIPS * PIECES[0], CHIPS * (PIECES[0] + PIECES[1]))
MIB = 1 << 20

CHIP_AXES = ("x", "yh")
ALL_CHIPS = ("z", "yl", "x", "yh")
ORDERS = (("abd", "bda", "dab"), ("bda", "dab", "abd"))


def halves(a, b, first):
    a, b = a.astype(jnp.float32), b.astype(jnp.float32)
    low = lax.broadcasted_iota(jnp.int32, a.shape, a.ndim - 1) < LANES // 2
    if first:
        return jnp.where(low, a, pltpu.roll(b, LANES // 2, a.ndim - 1))
    return jnp.where(low, pltpu.roll(a, LANES // 2, a.ndim - 1), b)


def tile(index):
    return pl.ds(index * LANES, LANES)


def place(stream, core):
    x, d = lax.axis_index("x"), lax.axis_index("yh")
    bit = {"a": lax.rem((x + 1) // 2, 2), "b": x // 2, "d": d}
    places = [4 * bit[i] + 2 * bit[j] + bit[k] for i, j, k in (orders[stream] for orders in ORDERS)]
    return places[0] + core * (places[1] - places[0])


def piece_rows(stream, position, base, core):
    piece = lax.bitwise_xor(place(stream, core), position)
    return pl.ds(base + pl.multiple_of(piece * PIECES[stream], 16), PIECES[stream])


def split_pieces(stream, whole_ref, base, keep_ref, send_ref):
    half, core = CHIPS // 2, lax.axis_index("c")
    for k in range(half):
        keep_ref[k] = whole_ref[piece_rows(stream, k, base, core), :]
        send_ref[k] = whole_ref[piece_rows(stream, k + half, base, core), :].astype(send_ref.dtype)


def half_shapes(stream, kind):
    shape = (CHIPS // 2, PIECES[stream], LANES)
    return [jax.ShapeDtypeStruct(shape, jnp.float32), jax.ShapeDtypeStruct(shape, kind)]


def split_kernel(x_ref, out_ref):
    for p in range(CHIPS):
        for j in range(STRIPES):
            out_ref[p, :, tile(j)] = x_ref[:, tile(TILES * j + p)]
        for m in range(STRIPES // 2):
            left = x_ref[:, tile(TILES * (2 * m) + CHIPS + p // 2)]
            right = x_ref[:, tile(TILES * (2 * m + 1) + CHIPS + p // 2)]
            out_ref[p, :, tile(STRIPES + m)] = halves(left, right, p % 2 == 0).astype(out_ref.dtype)


def split_columns(x):
    return pl.pallas_call(
        split_kernel,
        out_shape=jax.ShapeDtypeStruct((CHIPS, PANEL, WIDTH), x.dtype),
        compiler_params=pltpu.CompilerParams(vmem_limit_bytes=16 * MIB),
        name="split_columns",
    )(x)


def strip(j):
    below = (BLOCKS - 1 - j) * LANES
    start = LANES * sum(BLOCKS - 1 - i for i in range(j))
    return pl.ds(start, below)


def triangle(own_ref, ref, store_below, store_diagonal):
    for j in range(0, BLOCKS, 2):
        first = j * LANES
        part = lax.dot_general(
            own_ref[pl.ds(first, HALF - first), :],
            ref[pl.ds(first, 2 * LANES), :],
            (((1,), (1,)), ((), ())),
            preferred_element_type=jnp.float32,
        )
        for i in range(2):
            columns = part[i * LANES :, i * LANES : (i + 1) * LANES]
            store_diagonal(j + i, columns[:LANES])
            if j + i + 1 < BLOCKS:
                store_below(strip(j + i), columns[LANES:])


def iotas():
    return [lax.broadcasted_iota(jnp.int32, (LANES, LANES), axis) for axis in range(2)]


def own_gram_kernel(own_ref, keep_ref, send_ref, diagonal_ref, whole_ref):
    def store_below(rows, value):
        whole_ref[rows, :] = value

    def store_diagonal(j, value):
        diagonal_ref[j] = value

    triangle(own_ref, own_ref, store_below, store_diagonal)
    split_pieces(0, whole_ref, 0, keep_ref, send_ref)


def own_gram(own):
    return pl.pallas_call(
        own_gram_kernel,
        out_shape=half_shapes(0, own.dtype) + [jax.ShapeDtypeStruct((BLOCKS, LANES, LANES), jnp.float32)],
        scratch_shapes=[pltpu.VMEM((BELOW, LANES), jnp.float32)],
        compiler_params=pltpu.CompilerParams(vmem_limit_bytes=8 * MIB),
        cost_estimate=pl.CostEstimate(
            flops=2 * (BELOW + 3 * HALF) * LANES * WIDTH, bytes_accessed=2 * HALF * WIDTH, transcendentals=0
        ),
        name="own_gram",
    )(own)


def cross_gram_kernel(
    diagonal_ref, own_ref, other_ref, keep_b_ref, send_b_ref, keep_c_ref, send_c_ref, whole_ref
):
    row, column = iotas()
    edges = []

    def store_below(rows, value):
        whole_ref[rows, :] = value

    def store_diagonal(j, value):
        whole_ref[pl.ds(BELOW + j * LANES, LANES), :] = jnp.where(row >= column, diagonal_ref[j], value)
        edges.append(jnp.sum(jnp.where(row == column, value, 0.0), axis=0, keepdims=True))

    triangle(own_ref, other_ref, store_below, store_diagonal)
    edges.append(jnp.zeros((PACKED - EDGE - BLOCKS, LANES), jnp.float32))
    whole_ref[pl.ds(EDGE - BASES[1], PACKED - EDGE), :] = jnp.concatenate(edges)
    split_pieces(1, whole_ref, 0, keep_b_ref, send_b_ref)
    split_pieces(2, whole_ref, BASES[2] - BASES[1], keep_c_ref, send_c_ref)


def cross_gram(diagonal, own, other):
    return pl.pallas_call(
        cross_gram_kernel,
        out_shape=half_shapes(1, own.dtype) + half_shapes(2, own.dtype),
        scratch_shapes=[pltpu.VMEM((PACKED - BASES[1], LANES), jnp.float32)],
        compiler_params=pltpu.CompilerParams(vmem_limit_bytes=12 * MIB),
        cost_estimate=pl.CostEstimate(
            flops=2 * (BELOW + 3 * HALF) * LANES * WIDTH, bytes_accessed=4 * HALF * WIDTH, transcendentals=0
        ),
        name="cross_gram",
    )(diagonal, own, other)


def exchange(value, stream, hop):
    pairs = []
    for x in range(4):
        for d in range(2):
            for core in range(2):
                axis = ORDERS[core][stream][hop]
                to = {"a": (x ^ 1, d), "b": (3 - x, d), "d": (x, 1 - d)}[axis]
                pairs.append((4 * x + 2 * d + core, 4 * to[0] + 2 * to[1] + core))
    return lax.ppermute(value, ("x", "yh", "c"), pairs)


def wide(value):
    return value.astype(jnp.float32)


def after(value, *others):
    return lax.optimization_barrier((value, *others))[0]


def add_first(keep, arrived):
    return (keep + wide(arrived)).astype(arrived.dtype).reshape(2, 2, *keep.shape[1:])


def add_second(half, arrived):
    return (wide(half) + wide(arrived)[::-1]).astype(half.dtype)


def add_third(half, arrived):
    return (wide(half) + wide(arrived)[:, ::-1]).astype(half.dtype).reshape(CHIPS // 2, *half.shape[2:])


def unpermute(first_ref, rest_ref, packed_ref, core):
    places = ((first_ref, 0), (rest_ref, 0), (rest_ref, PIECES[1]))
    for s, (pieces_ref, start) in enumerate(places):
        for k in range(CHIPS):
            packed_ref[piece_rows(s, k, BASES[s], core), :] = pieces_ref[k, pl.ds(start, PIECES[s]), :]


def mirror(packed_ref, out_ref, lower):
    for j in range(BLOCKS):
        first = j * LANES
        block = packed_ref[pl.ds(2 * BELOW + first, LANES), :]
        out_ref[pl.ds(first, LANES), tile(j)] = jnp.where(lower, block, block.T)
        if j + 1 < BLOCKS:
            below = packed_ref[strip(j), :]
            out_ref[pl.ds(first + LANES, below.shape[0]), tile(j)] = below
            out_ref[pl.ds(first, LANES), pl.ds(first + LANES, below.shape[0])] = below.T


def own_square_kernel(first_ref, rest_ref, packed_ref, gram_ref, square_ref):
    row, column = iotas()
    unpermute(first_ref, rest_ref, packed_ref, lax.axis_index("c"))
    mirror(packed_ref, gram_ref, row >= column)
    for n in range(0, HALF, 256):
        columns = pl.ds(n, 256)
        square_ref[:, columns] = jnp.dot(gram_ref[...], gram_ref[:, columns], preferred_element_type=jnp.float32)


def own_square(first, rest):
    return pl.pallas_call(
        own_square_kernel,
        out_shape=(
            jax.ShapeDtypeStruct((PACKED, LANES), first.dtype),
            jax.ShapeDtypeStruct((HALF, HALF), first.dtype),
            jax.ShapeDtypeStruct((HALF, HALF), jnp.float32),
        ),
        compiler_params=pltpu.CompilerParams(vmem_limit_bytes=12 * MIB),
        cost_estimate=pl.CostEstimate(
            flops=2 * HALF * HALF * HALF, bytes_accessed=8 * HALF * HALF, transcendentals=0
        ),
        name="own_square",
    )(first, rest)


def unpack_cross(own_ref, other_ref, cross_ref):
    row, column = iotas()
    for j in range(BLOCKS):
        first = j * LANES
        upper, theirs = (ref[pl.ds(2 * BELOW + first, LANES), :] for ref in (own_ref, other_ref))
        edge = jnp.broadcast_to(own_ref[pl.ds(EDGE, 16), :].astype(jnp.float32)[j : j + 1], (LANES, LANES))
        block = jnp.where(row < column, upper.astype(jnp.float32), theirs.T.astype(jnp.float32))
        cross_ref[pl.ds(first, LANES), tile(j)] = jnp.where(row == column, edge, block).astype(cross_ref.dtype)
        if j + 1 < BLOCKS:
            rows = pl.ds(BELOW + strip(j).start, strip(j).size)
            cross_ref[pl.ds(first + LANES, rows.size), tile(j)] = own_ref[rows, :]
            cross_ref[pl.ds(first, LANES), pl.ds(first + LANES, rows.size)] = other_ref[rows, :].T


def update_kernel(
    own_ref, first_ref, rest_ref, gram_ref, square_ref, x_ref, x_other_ref, out_ref,
    other_ref, cross_ref, gram_other_ref, mixing_ref,
):
    scale = math.sqrt(max(ROWS, COLS))
    step = 256
    row, column = iotas()
    unpermute(first_ref, rest_ref, other_ref, 1 - lax.axis_index("c"))
    unpack_cross(own_ref, other_ref, cross_ref)
    mirror(other_ref, gram_other_ref, row >= column)
    for n in range(0, HALF, step):
        columns = pl.ds(n, step)
        square = square_ref[:, columns] + lax.dot_general(
            cross_ref[...], cross_ref[columns, :], (((1,), (1,)), ((), ())), preferred_element_type=jnp.float32
        )
        gram = gram_ref[:, columns].astype(jnp.float32)
        mixing_ref[:, columns] = (coeff_b * gram + coeff_c * square).astype(mixing_ref.dtype)
    for n in range(0, HALF, step):
        columns = pl.ds(n, step)
        square = jnp.dot(gram_ref[...], cross_ref[:, columns], preferred_element_type=jnp.float32)
        square += jnp.dot(cross_ref[...], gram_other_ref[:, columns], preferred_element_type=jnp.float32)
        gram = cross_ref[:, columns].astype(jnp.float32)
        mixing_ref[:, pl.ds(HALF + n, step)] = (coeff_b * gram + coeff_c * square).astype(mixing_ref.dtype)
    for t in range(0, TILES, 2):
        columns = pl.ds(t * LANES, 2 * LANES)
        result = jnp.dot(mixing_ref[:, pl.ds(0, HALF)], x_ref[:, columns], preferred_element_type=jnp.float32)
        result += jnp.dot(mixing_ref[:, pl.ds(HALF, HALF)], x_other_ref[:, columns], preferred_element_type=jnp.float32)
        result = scale * (coeff_a * x_ref[:, columns].astype(jnp.float32) + result)
        for i in range(2):
            block = result[:, i * LANES : (i + 1) * LANES].reshape(CHIPS, PANEL, LANES)
            j = t + i
            if j < STRIPES:
                out_ref[j, :, pl.ds(0, PANEL), :] = block.astype(out_ref.dtype)
            else:
                top, bottom = block[:, : PANEL // 2], block[:, PANEL // 2 :]
                for side in range(2):
                    packed = halves(top, bottom, side == 0).astype(out_ref.dtype)
                    out_ref[2 * (j - STRIPES) + side, :, pl.ds(PANEL, PANEL // 2), :] = packed


def update_rows(*operands):
    kind = operands[0].dtype
    return pl.pallas_call(
        update_kernel,
        out_shape=jax.ShapeDtypeStruct((STRIPES, CHIPS, PANEL + PANEL // 2, LANES), kind),
        scratch_shapes=[
            pltpu.VMEM((PACKED, LANES), kind),
            pltpu.VMEM((HALF, HALF), kind),
            pltpu.VMEM((HALF, HALF), kind),
            pltpu.VMEM((HALF, ROWS), kind),
        ],
        compiler_params=pltpu.CompilerParams(vmem_limit_bytes=24 * MIB),
        cost_estimate=pl.CostEstimate(
            flops=4 * HALF * ROWS * ROWS - 2 * HALF * HALF * HALF, bytes_accessed=10 * HALF * ROWS, transcendentals=0
        ),
        name="update_rows",
    )(*operands)


def join_kernel(pieces_ref, out_ref, whole_ref, sems):
    copies = []
    for layer in range(STRIPES):
        for p in range(CHIPS):
            whole_ref[layer, :, tile(p)] = pieces_ref[layer, p, pl.ds(0, PANEL), :]
        for pair in range(CHIPS // 2):
            left = pieces_ref[layer, 2 * pair, pl.ds(PANEL, PANEL // 2), :]
            right = pieces_ref[layer, 2 * pair + 1, pl.ds(PANEL, PANEL // 2), :]
            for part in range(2):
                joined = halves(left, right, part == 0).astype(whole_ref.dtype)
                whole_ref[layer, pl.ds(part * PANEL // 2, PANEL // 2), tile(CHIPS + pair)] = joined
        copies.append(pltpu.make_async_copy(whole_ref.at[layer], out_ref.at[layer], sems.at[layer]))
        copies[-1].start()
    for copy in copies:
        copy.wait()


def join_columns(pieces):
    shape = (pieces.shape[0], PANEL, TILES * LANES)
    return pl.pallas_call(
        join_kernel,
        in_specs=[pl.BlockSpec(memory_space=pltpu.VMEM)],
        out_specs=pl.BlockSpec(memory_space=pl.ANY),
        out_shape=jax.ShapeDtypeStruct(shape, pieces.dtype),
        scratch_shapes=[pltpu.VMEM(shape, pieces.dtype), pltpu.SemaphoreType.DMA((pieces.shape[0],))],
        compiler_params=pltpu.CompilerParams(vmem_limit_bytes=12 * MIB),
        name="join_columns",
    )(pieces)


def swap_cores(value):
    return lax.ppermute(value, "c", [(0, 1), (1, 0)])


def shards(iterate):
    pieces = split_columns(iterate.reshape(PANEL, COLS))
    own = lax.all_to_all(pieces, CHIP_AXES, 0, 0, tiled=True).reshape(HALF, WIDTH)
    other = swap_cores(own)
    keep_a, send_a, diagonal = own_gram(own)
    arrived_a = exchange(send_a, 0, 0)
    keep_b, send_b, keep_c, send_c = cross_gram(diagonal, own, other)
    arrived_b, arrived_c = exchange(send_b, 1, 0), exchange(send_c, 2, 0)
    half_a = add_first(keep_a, after(arrived_a, send_b, send_c))
    half_b, half_c = add_first(keep_b, arrived_b), add_first(keep_c, arrived_c)
    next_a, next_b, next_c = exchange(half_a, 0, 1), exchange(half_b, 1, 1), exchange(half_c, 2, 1)
    half_a = add_second(half_a, after(next_a, arrived_b))
    half_a = add_third(half_a, exchange(half_a, 0, 2))
    half_b = add_second(half_b, next_b)
    next_b = exchange(half_b, 1, 2)
    half_c = add_second(half_c, after(next_c, half_a))
    next_c = exchange(half_c, 2, 2)
    first = jnp.concatenate([half_a, exchange(half_a, 0, 0)])
    half_b = add_third(half_b, next_b)
    half_c = add_third(half_c, after(next_c, first))
    rest = [jnp.concatenate([half, exchange(half, s, 0)]) for s, half in ((1, half_b), (2, half_c))]
    rest = jnp.concatenate(rest, axis=1)
    first_other = swap_cores(first)
    rest_other = swap_cores(after(rest, first_other))
    packed, gram, square = own_square(first, rest)
    sent = update_rows(packed, first_other, rest_other, gram, square, own, other)
    sent = sent.reshape(STRIPES * CHIPS, PANEL + PANEL // 2, LANES)
    received = lax.all_to_all(sent, ALL_CHIPS, 0, 0, tiled=True)
    return join_columns(received.reshape(STRIPES, CHIPS, PANEL + PANEL // 2, LANES))


def solution(mesh):
    fine = Mesh(mesh.devices.reshape(4, 2, 4, 2, 2), ("z", "yl", "x", "yh", "c"))
    return jax.shard_map(
        shards,
        mesh=fine,
        in_specs=(P(("z", "yl"), ("x", "yh", "c"), None),),
        out_specs=P(None, ("x", "yh", "c"), ("z", "yl")),
        check_vma=False,
    )
```

```python
import math

import jax
import jax.numpy as jnp
from jax import lax
from jax.experimental import pallas as pl
from jax.experimental.pallas import tpu as pltpu
from jax.sharding import Mesh, PartitionSpec as P

coeff_a = 3.4445
coeff_b = -4.775
coeff_c = 2.0315

ROWS = 1536
COLS = 12288
LANES = 128
CHIPS = 8
STRIPES = 8
PANEL = ROWS // (2 * CHIPS)
HALF = ROWS // 2
WIDTH = COLS // CHIPS
TILES = COLS // STRIPES // LANES
BLOCKS = HALF // LANES
BELOW = LANES * BLOCKS * (BLOCKS - 1) // 2
EDGE = 2 * BELOW + HALF
PACKED = -(-(EDGE + BLOCKS) // (16 * CHIPS)) * 16 * CHIPS
PIECES = (240, 192, 160)
BASES = (0, CHIPS * PIECES[0], CHIPS * (PIECES[0] + PIECES[1]))
MIB = 1 << 20

CHIP_AXES = ("x", "yh")
ALL_CHIPS = ("z", "yl", "x", "yh")
ORDERS = (("abd", "bda", "dab"), ("bda", "dab", "abd"))


def halves(a, b, first):
    a, b = a.astype(jnp.float32), b.astype(jnp.float32)
    low = lax.broadcasted_iota(jnp.int32, a.shape, a.ndim - 1) < LANES // 2
    if first:
        return jnp.where(low, a, pltpu.roll(b, LANES // 2, a.ndim - 1))
    return jnp.where(low, pltpu.roll(a, LANES // 2, a.ndim - 1), b)


def tile(index):
    return pl.ds(index * LANES, LANES)


def place(stream, core):
    x, d = lax.axis_index("x"), lax.axis_index("yh")
    bit = {"a": lax.rem((x + 1) // 2, 2), "b": x // 2, "d": d}
    places = [4 * bit[i] + 2 * bit[j] + bit[k] for i, j, k in (orders[stream] for orders in ORDERS)]
    return places[0] + core * (places[1] - places[0])


def piece_rows(stream, position, base, core):
    piece = lax.bitwise_xor(place(stream, core), position)
    return pl.ds(base + pl.multiple_of(piece * PIECES[stream], 16), PIECES[stream])


def split_pieces(stream, whole_ref, base, keep_ref, send_ref):
    half, core = CHIPS // 2, lax.axis_index("c")
    for k in range(half):
        keep_ref[k] = whole_ref[piece_rows(stream, k, base, core), :]
        send_ref[k] = whole_ref[piece_rows(stream, k + half, base, core), :].astype(send_ref.dtype)


def half_shapes(stream, kind):
    shape = (CHIPS // 2, PIECES[stream], LANES)
    return [jax.ShapeDtypeStruct(shape, jnp.float32), jax.ShapeDtypeStruct(shape, kind)]


def split_kernel(x_ref, out_ref):
    for p in range(CHIPS):
        for j in range(STRIPES):
            out_ref[p, :, tile(j)] = x_ref[:, tile(TILES * j + p)]
        for m in range(STRIPES // 2):
            left = x_ref[:, tile(TILES * (2 * m) + CHIPS + p // 2)]
            right = x_ref[:, tile(TILES * (2 * m + 1) + CHIPS + p // 2)]
            out_ref[p, :, tile(STRIPES + m)] = halves(left, right, p % 2 == 0).astype(out_ref.dtype)


def split_columns(x):
    return pl.pallas_call(
        split_kernel,
        out_shape=jax.ShapeDtypeStruct((CHIPS, PANEL, WIDTH), x.dtype),
        compiler_params=pltpu.CompilerParams(vmem_limit_bytes=16 * MIB),
        name="split_columns",
    )(x)


def strip(j):
    below = (BLOCKS - 1 - j) * LANES
    start = LANES * sum(BLOCKS - 1 - i for i in range(j))
    return pl.ds(start, below)


def triangle(own_ref, ref, store_below, store_diagonal):
    for j in range(0, BLOCKS, 2):
        first = j * LANES
        part = lax.dot_general(
            own_ref[pl.ds(first, HALF - first), :],
            ref[pl.ds(first, 2 * LANES), :],
            (((1,), (1,)), ((), ())),
            preferred_element_type=jnp.float32,
        )
        for i in range(2):
            columns = part[i * LANES :, i * LANES : (i + 1) * LANES]
            store_diagonal(j + i, columns[:LANES])
            if j + i + 1 < BLOCKS:
                store_below(strip(j + i), columns[LANES:])


def iotas():
    return [lax.broadcasted_iota(jnp.int32, (LANES, LANES), axis) for axis in range(2)]


def own_gram_kernel(own_ref, keep_ref, send_ref, diagonal_ref, whole_ref):
    def store_below(rows, value):
        whole_ref[rows, :] = value

    def store_diagonal(j, value):
        diagonal_ref[j] = value

    triangle(own_ref, own_ref, store_below, store_diagonal)
    split_pieces(0, whole_ref, 0, keep_ref, send_ref)


def own_gram(own):
    return pl.pallas_call(
        own_gram_kernel,
        out_shape=half_shapes(0, own.dtype) + [jax.ShapeDtypeStruct((BLOCKS, LANES, LANES), jnp.float32)],
        scratch_shapes=[pltpu.VMEM((BELOW, LANES), jnp.float32)],
        compiler_params=pltpu.CompilerParams(vmem_limit_bytes=8 * MIB),
        cost_estimate=pl.CostEstimate(
            flops=2 * (BELOW + 3 * HALF) * LANES * WIDTH, bytes_accessed=2 * HALF * WIDTH, transcendentals=0
        ),
        name="own_gram",
    )(own)


def cross_gram_kernel(
    diagonal_ref, own_ref, other_ref, keep_b_ref, send_b_ref, keep_c_ref, send_c_ref, whole_ref
):
    row, column = iotas()
    edges = []

    def store_below(rows, value):
        whole_ref[rows, :] = value

    def store_diagonal(j, value):
        whole_ref[pl.ds(BELOW + j * LANES, LANES), :] = jnp.where(row >= column, diagonal_ref[j], value)
        edges.append(jnp.sum(jnp.where(row == column, value, 0.0), axis=0, keepdims=True))

    triangle(own_ref, other_ref, store_below, store_diagonal)
    edges.append(jnp.zeros((PACKED - EDGE - BLOCKS, LANES), jnp.float32))
    whole_ref[pl.ds(EDGE - BASES[1], PACKED - EDGE), :] = jnp.concatenate(edges)
    split_pieces(1, whole_ref, 0, keep_b_ref, send_b_ref)
    split_pieces(2, whole_ref, BASES[2] - BASES[1], keep_c_ref, send_c_ref)


def cross_gram(diagonal, own, other):
    return pl.pallas_call(
        cross_gram_kernel,
        out_shape=half_shapes(1, own.dtype) + half_shapes(2, own.dtype),
        scratch_shapes=[pltpu.VMEM((PACKED - BASES[1], LANES), jnp.float32)],
        compiler_params=pltpu.CompilerParams(vmem_limit_bytes=12 * MIB),
        cost_estimate=pl.CostEstimate(
            flops=2 * (BELOW + 3 * HALF) * LANES * WIDTH, bytes_accessed=4 * HALF * WIDTH, transcendentals=0
        ),
        name="cross_gram",
    )(diagonal, own, other)


def exchange(value, stream, hop):
    pairs = []
    for x in range(4):
        for d in range(2):
            for core in range(2):
                axis = ORDERS[core][stream][hop]
                to = {"a": (x ^ 1, d), "b": (3 - x, d), "d": (x, 1 - d)}[axis]
                pairs.append((4 * x + 2 * d + core, 4 * to[0] + 2 * to[1] + core))
    return lax.ppermute(value, ("x", "yh", "c"), pairs)


def wide(value):
    return value.astype(jnp.float32)


def after(value, *others):
    return lax.optimization_barrier((value, *others))[0]


def add_first(keep, arrived):
    return (keep + wide(arrived)).astype(arrived.dtype).reshape(2, 2, *keep.shape[1:])


def add_second(half, arrived):
    return (wide(half) + wide(arrived)[::-1]).astype(half.dtype)


def add_third(half, arrived):
    return (wide(half) + wide(arrived)[:, ::-1]).astype(half.dtype).reshape(CHIPS // 2, *half.shape[2:])


def unpermute(streams, packed_ref, core):
    for s, pieces_ref in enumerate(streams):
        for k in range(CHIPS):
            packed_ref[piece_rows(s, k, BASES[s], core), :] = pieces_ref[k]


def mirror(packed_ref, out_ref, lower):
    for j in range(BLOCKS):
        first = j * LANES
        block = packed_ref[pl.ds(2 * BELOW + first, LANES), :]
        out_ref[pl.ds(first, LANES), tile(j)] = jnp.where(lower, block, block.T)
        if j + 1 < BLOCKS:
            below = packed_ref[strip(j), :]
            out_ref[pl.ds(first + LANES, below.shape[0]), tile(j)] = below
            out_ref[pl.ds(first, LANES), pl.ds(first + LANES, below.shape[0])] = below.T


def own_square_kernel(a_ref, b_ref, c_ref, packed_ref, gram_ref, square_ref):
    row, column = iotas()
    unpermute((a_ref, b_ref, c_ref), packed_ref, lax.axis_index("c"))
    mirror(packed_ref, gram_ref, row >= column)
    for n in range(0, HALF, 256):
        columns = pl.ds(n, 256)
        square_ref[:, columns] = jnp.dot(gram_ref[...], gram_ref[:, columns], preferred_element_type=jnp.float32)


def own_square(*streams):
    return pl.pallas_call(
        own_square_kernel,
        out_shape=(
            jax.ShapeDtypeStruct((PACKED, LANES), streams[0].dtype),
            jax.ShapeDtypeStruct((HALF, HALF), streams[0].dtype),
            jax.ShapeDtypeStruct((HALF, HALF), jnp.float32),
        ),
        compiler_params=pltpu.CompilerParams(vmem_limit_bytes=12 * MIB),
        cost_estimate=pl.CostEstimate(
            flops=2 * HALF * HALF * HALF, bytes_accessed=8 * HALF * HALF, transcendentals=0
        ),
        name="own_square",
    )(*streams)


def unpack_cross(own_ref, other_ref, cross_ref):
    row, column = iotas()
    for j in range(BLOCKS):
        first = j * LANES
        upper, theirs = (ref[pl.ds(2 * BELOW + first, LANES), :] for ref in (own_ref, other_ref))
        edge = jnp.broadcast_to(own_ref[pl.ds(EDGE, 16), :].astype(jnp.float32)[j : j + 1], (LANES, LANES))
        block = jnp.where(row < column, upper.astype(jnp.float32), theirs.T.astype(jnp.float32))
        cross_ref[pl.ds(first, LANES), tile(j)] = jnp.where(row == column, edge, block).astype(cross_ref.dtype)
        if j + 1 < BLOCKS:
            rows = pl.ds(BELOW + strip(j).start, strip(j).size)
            cross_ref[pl.ds(first + LANES, rows.size), tile(j)] = own_ref[rows, :]
            cross_ref[pl.ds(first, LANES), pl.ds(first + LANES, rows.size)] = other_ref[rows, :].T


def update_kernel(
    own_ref, a_ref, b_ref, c_ref, gram_ref, square_ref, x_ref, x_other_ref, out_ref,
    other_ref, cross_ref, gram_other_ref, mixing_ref,
):
    scale = math.sqrt(max(ROWS, COLS))
    step = 256
    row, column = iotas()
    unpermute((a_ref, b_ref, c_ref), other_ref, 1 - lax.axis_index("c"))
    unpack_cross(own_ref, other_ref, cross_ref)
    mirror(other_ref, gram_other_ref, row >= column)
    for n in range(0, HALF, step):
        columns = pl.ds(n, step)
        square = square_ref[:, columns] + lax.dot_general(
            cross_ref[...], cross_ref[columns, :], (((1,), (1,)), ((), ())), preferred_element_type=jnp.float32
        )
        gram = gram_ref[:, columns].astype(jnp.float32)
        mixing_ref[:, columns] = (coeff_b * gram + coeff_c * square).astype(mixing_ref.dtype)
    for n in range(0, HALF, step):
        columns = pl.ds(n, step)
        square = jnp.dot(gram_ref[...], cross_ref[:, columns], preferred_element_type=jnp.float32)
        square += jnp.dot(cross_ref[...], gram_other_ref[:, columns], preferred_element_type=jnp.float32)
        gram = cross_ref[:, columns].astype(jnp.float32)
        mixing_ref[:, pl.ds(HALF + n, step)] = (coeff_b * gram + coeff_c * square).astype(mixing_ref.dtype)
    for t in range(0, TILES, 2):
        columns = pl.ds(t * LANES, 2 * LANES)
        result = jnp.dot(mixing_ref[:, pl.ds(0, HALF)], x_ref[:, columns], preferred_element_type=jnp.float32)
        result += jnp.dot(mixing_ref[:, pl.ds(HALF, HALF)], x_other_ref[:, columns], preferred_element_type=jnp.float32)
        result = scale * (coeff_a * x_ref[:, columns].astype(jnp.float32) + result)
        for i in range(2):
            block = result[:, i * LANES : (i + 1) * LANES].reshape(CHIPS, PANEL, LANES)
            j = t + i
            if j < STRIPES:
                out_ref[j, :, pl.ds(0, PANEL), :] = block.astype(out_ref.dtype)
            else:
                top, bottom = block[:, : PANEL // 2], block[:, PANEL // 2 :]
                for side in range(2):
                    packed = halves(top, bottom, side == 0).astype(out_ref.dtype)
                    out_ref[2 * (j - STRIPES) + side, :, pl.ds(PANEL, PANEL // 2), :] = packed


def update_rows(*operands):
    kind = operands[0].dtype
    return pl.pallas_call(
        update_kernel,
        out_shape=jax.ShapeDtypeStruct((STRIPES, CHIPS, PANEL + PANEL // 2, LANES), kind),
        scratch_shapes=[
            pltpu.VMEM((PACKED, LANES), kind),
            pltpu.VMEM((HALF, HALF), kind),
            pltpu.VMEM((HALF, HALF), kind),
            pltpu.VMEM((HALF, ROWS), kind),
        ],
        compiler_params=pltpu.CompilerParams(vmem_limit_bytes=24 * MIB),
        cost_estimate=pl.CostEstimate(
            flops=4 * HALF * ROWS * ROWS - 2 * HALF * HALF * HALF, bytes_accessed=10 * HALF * ROWS, transcendentals=0
        ),
        name="update_rows",
    )(*operands)


def join_kernel(pieces_ref, out_ref, whole_ref, sems):
    copies = []
    for layer in range(STRIPES):
        for p in range(CHIPS):
            whole_ref[layer, :, tile(p)] = pieces_ref[layer, p, pl.ds(0, PANEL), :]
        for pair in range(CHIPS // 2):
            left = pieces_ref[layer, 2 * pair, pl.ds(PANEL, PANEL // 2), :]
            right = pieces_ref[layer, 2 * pair + 1, pl.ds(PANEL, PANEL // 2), :]
            for part in range(2):
                joined = halves(left, right, part == 0).astype(whole_ref.dtype)
                whole_ref[layer, pl.ds(part * PANEL // 2, PANEL // 2), tile(CHIPS + pair)] = joined
        copies.append(pltpu.make_async_copy(whole_ref.at[layer], out_ref.at[layer], sems.at[layer]))
        copies[-1].start()
    for copy in copies:
        copy.wait()


def join_columns(pieces):
    shape = (pieces.shape[0], PANEL, TILES * LANES)
    return pl.pallas_call(
        join_kernel,
        in_specs=[pl.BlockSpec(memory_space=pltpu.VMEM)],
        out_specs=pl.BlockSpec(memory_space=pl.ANY),
        out_shape=jax.ShapeDtypeStruct(shape, pieces.dtype),
        scratch_shapes=[pltpu.VMEM(shape, pieces.dtype), pltpu.SemaphoreType.DMA((pieces.shape[0],))],
        compiler_params=pltpu.CompilerParams(vmem_limit_bytes=12 * MIB),
        name="join_columns",
    )(pieces)


def swap_cores(value):
    return lax.ppermute(value, "c", [(0, 1), (1, 0)])


def shards(iterate):
    pieces = split_columns(iterate.reshape(PANEL, COLS))
    own = lax.all_to_all(pieces, CHIP_AXES, 0, 0, tiled=True).reshape(HALF, WIDTH)
    other = swap_cores(own)
    keep_a, send_a, diagonal = own_gram(own)
    arrived_a = exchange(send_a, 0, 0)
    keep_b, send_b, keep_c, send_c = cross_gram(diagonal, own, other)
    arrived_b, arrived_c = exchange(send_b, 1, 0), exchange(send_c, 2, 0)
    half_a = add_first(keep_a, after(arrived_a, send_b, send_c))
    half_b, half_c = add_first(keep_b, arrived_b), add_first(keep_c, arrived_c)
    next_a, next_b, next_c = exchange(half_a, 0, 1), exchange(half_b, 1, 1), exchange(half_c, 2, 1)
    half_a = add_second(half_a, after(next_a, half_b))
    next_a = exchange(half_a, 0, 2)
    half_b = add_second(half_b, next_b)
    half_a = add_third(half_a, after(next_a, half_b))
    next_b = exchange(half_b, 1, 2)
    half_c = add_second(half_c, after(next_c, half_a))
    next_c = exchange(half_c, 2, 2)
    half_b = add_third(half_b, next_b)
    first = jnp.concatenate([half_a, after(exchange(half_a, 0, 0), half_b)])
    half_c = add_third(half_c, after(next_c, first))
    streams = [first] + [jnp.concatenate([half, exchange(half, s, 0)]) for s, half in ((1, half_b), (2, half_c))]
    others = [swap_cores(first)]
    others += [swap_cores(after(stream, others[0])) for stream in streams[1:]]
    packed, gram, square = own_square(*streams)
    sent = update_rows(packed, *others, gram, square, own, other)
    sent = sent.reshape(STRIPES * CHIPS, PANEL + PANEL // 2, LANES)
    received = lax.all_to_all(sent, ALL_CHIPS, 0, 0, tiled=True)
    return join_columns(received.reshape(STRIPES, CHIPS, PANEL + PANEL // 2, LANES))


def solution(mesh):
    fine = Mesh(mesh.devices.reshape(4, 2, 4, 2, 2), ("z", "yl", "x", "yh", "c"))
    return jax.shard_map(
        shards,
        mesh=fine,
        in_specs=(P(("z", "yl"), ("x", "yh", "c"), None),),
        out_specs=P(None, ("x", "yh", "c"), ("z", "yl")),
        check_vma=False,
    )
```

```python
import math

import jax
import jax.numpy as jnp
from jax import lax
from jax.experimental import pallas as pl
from jax.experimental.pallas import tpu as pltpu
from jax.sharding import Mesh, PartitionSpec as P

coeff_a = 3.4445
coeff_b = -4.775
coeff_c = 2.0315

ROWS = 1536
COLS = 12288
LANES = 128
CHIPS = 8
STRIPES = 8
PANEL = ROWS // (2 * CHIPS)
HALF = ROWS // 2
WIDTH = COLS // CHIPS
TILES = COLS // STRIPES // LANES
BLOCKS = HALF // LANES
BELOW = LANES * BLOCKS * (BLOCKS - 1) // 2
EDGE = 2 * BELOW + HALF
PACKED = -(-(EDGE + BLOCKS) // (16 * CHIPS)) * 16 * CHIPS
PIECES = (240, 192, 160)
BASES = (0, CHIPS * PIECES[0], CHIPS * (PIECES[0] + PIECES[1]))
MIB = 1 << 20

CHIP_AXES = ("x", "yh")
ALL_CHIPS = ("z", "yl", "x", "yh")
ORDERS = (("abd", "bda", "dab"), ("bda", "dab", "abd"))


def halves(a, b, first):
    a, b = a.astype(jnp.float32), b.astype(jnp.float32)
    low = lax.broadcasted_iota(jnp.int32, a.shape, a.ndim - 1) < LANES // 2
    if first:
        return jnp.where(low, a, pltpu.roll(b, LANES // 2, a.ndim - 1))
    return jnp.where(low, pltpu.roll(a, LANES // 2, a.ndim - 1), b)


def tile(index):
    return pl.ds(index * LANES, LANES)


def place(stream, core):
    x, d = lax.axis_index("x"), lax.axis_index("yh")
    bit = {"a": lax.rem((x + 1) // 2, 2), "b": x // 2, "d": d}
    places = [4 * bit[i] + 2 * bit[j] + bit[k] for i, j, k in (orders[stream] for orders in ORDERS)]
    return places[0] + core * (places[1] - places[0])


def piece_rows(stream, position, base, core):
    piece = lax.bitwise_xor(place(stream, core), position)
    return pl.ds(base + pl.multiple_of(piece * PIECES[stream], 16), PIECES[stream])


def split_pieces(stream, whole_ref, base, keep_ref, send_ref):
    half, core = CHIPS // 2, lax.axis_index("c")
    for k in range(half):
        keep_ref[k] = whole_ref[piece_rows(stream, k, base, core), :]
        send_ref[k] = whole_ref[piece_rows(stream, k + half, base, core), :].astype(send_ref.dtype)


def half_shapes(stream, kind):
    shape = (CHIPS // 2, PIECES[stream], LANES)
    return [jax.ShapeDtypeStruct(shape, jnp.float32), jax.ShapeDtypeStruct(shape, kind)]


def split_kernel(x_ref, out_ref):
    for p in range(CHIPS):
        for j in range(STRIPES):
            out_ref[p, :, tile(j)] = x_ref[:, tile(TILES * j + p)]
        for m in range(STRIPES // 2):
            left = x_ref[:, tile(TILES * (2 * m) + CHIPS + p // 2)]
            right = x_ref[:, tile(TILES * (2 * m + 1) + CHIPS + p // 2)]
            out_ref[p, :, tile(STRIPES + m)] = halves(left, right, p % 2 == 0).astype(out_ref.dtype)


def split_columns(x):
    return pl.pallas_call(
        split_kernel,
        out_shape=jax.ShapeDtypeStruct((CHIPS, PANEL, WIDTH), x.dtype),
        compiler_params=pltpu.CompilerParams(vmem_limit_bytes=16 * MIB),
        name="split_columns",
    )(x)


def strip(j):
    below = (BLOCKS - 1 - j) * LANES
    start = LANES * sum(BLOCKS - 1 - i for i in range(j))
    return pl.ds(start, below)


def triangle(own_ref, ref, store_below, store_diagonal):
    for j in range(0, BLOCKS, 2):
        first = j * LANES
        part = lax.dot_general(
            own_ref[pl.ds(first, HALF - first), :],
            ref[pl.ds(first, 2 * LANES), :],
            (((1,), (1,)), ((), ())),
            preferred_element_type=jnp.float32,
        )
        for i in range(2):
            columns = part[i * LANES :, i * LANES : (i + 1) * LANES]
            store_diagonal(j + i, columns[:LANES])
            if j + i + 1 < BLOCKS:
                store_below(strip(j + i), columns[LANES:])


def iotas():
    return [lax.broadcasted_iota(jnp.int32, (LANES, LANES), axis) for axis in range(2)]


def own_gram_kernel(own_ref, keep_ref, send_ref, diagonal_ref, whole_ref):
    def store_below(rows, value):
        whole_ref[rows, :] = value

    def store_diagonal(j, value):
        diagonal_ref[j] = value

    triangle(own_ref, own_ref, store_below, store_diagonal)
    split_pieces(0, whole_ref, 0, keep_ref, send_ref)


def own_gram(own):
    return pl.pallas_call(
        own_gram_kernel,
        out_shape=half_shapes(0, own.dtype) + [jax.ShapeDtypeStruct((BLOCKS, LANES, LANES), jnp.float32)],
        scratch_shapes=[pltpu.VMEM((BELOW, LANES), jnp.float32)],
        compiler_params=pltpu.CompilerParams(vmem_limit_bytes=8 * MIB),
        cost_estimate=pl.CostEstimate(
            flops=2 * (BELOW + 3 * HALF) * LANES * WIDTH, bytes_accessed=2 * HALF * WIDTH, transcendentals=0
        ),
        name="own_gram",
    )(own)


def cross_gram_kernel(
    diagonal_ref, own_ref, other_ref, keep_b_ref, send_b_ref, keep_c_ref, send_c_ref, whole_ref
):
    row, column = iotas()
    edges = []

    def store_below(rows, value):
        whole_ref[rows, :] = value

    def store_diagonal(j, value):
        whole_ref[pl.ds(BELOW + j * LANES, LANES), :] = jnp.where(row >= column, diagonal_ref[j], value)
        edges.append(jnp.sum(jnp.where(row == column, value, 0.0), axis=0, keepdims=True))

    triangle(own_ref, other_ref, store_below, store_diagonal)
    edges.append(jnp.zeros((PACKED - EDGE - BLOCKS, LANES), jnp.float32))
    whole_ref[pl.ds(EDGE - BASES[1], PACKED - EDGE), :] = jnp.concatenate(edges)
    split_pieces(1, whole_ref, 0, keep_b_ref, send_b_ref)
    split_pieces(2, whole_ref, BASES[2] - BASES[1], keep_c_ref, send_c_ref)


def cross_gram(diagonal, own, other):
    return pl.pallas_call(
        cross_gram_kernel,
        out_shape=half_shapes(1, own.dtype) + half_shapes(2, own.dtype),
        scratch_shapes=[pltpu.VMEM((PACKED - BASES[1], LANES), jnp.float32)],
        compiler_params=pltpu.CompilerParams(vmem_limit_bytes=12 * MIB),
        cost_estimate=pl.CostEstimate(
            flops=2 * (BELOW + 3 * HALF) * LANES * WIDTH, bytes_accessed=4 * HALF * WIDTH, transcendentals=0
        ),
        name="cross_gram",
    )(diagonal, own, other)


def exchange(value, stream, hop):
    pairs = []
    for x in range(4):
        for d in range(2):
            for core in range(2):
                axis = ORDERS[core][stream][hop]
                to = {"a": (x ^ 1, d), "b": (3 - x, d), "d": (x, 1 - d)}[axis]
                pairs.append((4 * x + 2 * d + core, 4 * to[0] + 2 * to[1] + core))
    return lax.ppermute(value, ("x", "yh", "c"), pairs)


def wide(value):
    return value.astype(jnp.float32)


def after(value, *others):
    return lax.optimization_barrier((value, *others))[0]


def add_first(keep, arrived):
    return (keep + wide(arrived)).astype(arrived.dtype).reshape(2, 2, *keep.shape[1:])


def add_second(half, arrived):
    return (wide(half) + wide(arrived)[::-1]).astype(half.dtype)


def add_third(half, arrived):
    return (wide(half) + wide(arrived)[:, ::-1]).astype(half.dtype).reshape(CHIPS // 2, *half.shape[2:])


def unpermute(streams, packed_ref, core):
    for s, pieces_ref in enumerate(streams):
        for k in range(CHIPS):
            packed_ref[piece_rows(s, k, BASES[s], core), :] = pieces_ref[k]


def mirror(packed_ref, out_ref, lower):
    for j in range(BLOCKS):
        first = j * LANES
        block = packed_ref[pl.ds(2 * BELOW + first, LANES), :]
        out_ref[pl.ds(first, LANES), tile(j)] = jnp.where(lower, block, block.T)
        if j + 1 < BLOCKS:
            below = packed_ref[strip(j), :]
            out_ref[pl.ds(first + LANES, below.shape[0]), tile(j)] = below
            out_ref[pl.ds(first, LANES), pl.ds(first + LANES, below.shape[0])] = below.T


def own_square_kernel(a_ref, b_ref, c_ref, packed_ref, gram_ref, square_ref):
    row, column = iotas()
    unpermute((a_ref, b_ref, c_ref), packed_ref, lax.axis_index("c"))
    mirror(packed_ref, gram_ref, row >= column)
    for n in range(0, HALF, 256):
        columns = pl.ds(n, 256)
        square_ref[:, columns] = jnp.dot(gram_ref[...], gram_ref[:, columns], preferred_element_type=jnp.float32)


def own_square(*streams):
    return pl.pallas_call(
        own_square_kernel,
        out_shape=(
            jax.ShapeDtypeStruct((PACKED, LANES), streams[0].dtype),
            jax.ShapeDtypeStruct((HALF, HALF), streams[0].dtype),
            jax.ShapeDtypeStruct((HALF, HALF), jnp.float32),
        ),
        compiler_params=pltpu.CompilerParams(vmem_limit_bytes=12 * MIB),
        cost_estimate=pl.CostEstimate(
            flops=2 * HALF * HALF * HALF, bytes_accessed=8 * HALF * HALF, transcendentals=0
        ),
        name="own_square",
    )(*streams)


def unpack_cross(own_ref, other_ref, cross_ref):
    row, column = iotas()
    for j in range(BLOCKS):
        first = j * LANES
        upper, theirs = (ref[pl.ds(2 * BELOW + first, LANES), :] for ref in (own_ref, other_ref))
        edge = jnp.broadcast_to(own_ref[pl.ds(EDGE, 16), :].astype(jnp.float32)[j : j + 1], (LANES, LANES))
        block = jnp.where(row < column, upper.astype(jnp.float32), theirs.T.astype(jnp.float32))
        cross_ref[pl.ds(first, LANES), tile(j)] = jnp.where(row == column, edge, block).astype(cross_ref.dtype)
        if j + 1 < BLOCKS:
            rows = pl.ds(BELOW + strip(j).start, strip(j).size)
            cross_ref[pl.ds(first + LANES, rows.size), tile(j)] = own_ref[rows, :]
            cross_ref[pl.ds(first, LANES), pl.ds(first + LANES, rows.size)] = other_ref[rows, :].T


def update_kernel(
    own_ref, a_ref, b_ref, c_ref, gram_ref, square_ref, x_ref, x_other_ref, out_ref,
    other_ref, cross_ref, gram_other_ref, mixing_ref,
):
    scale = math.sqrt(max(ROWS, COLS))
    step = 256
    row, column = iotas()
    unpermute((a_ref, b_ref, c_ref), other_ref, 1 - lax.axis_index("c"))
    unpack_cross(own_ref, other_ref, cross_ref)
    mirror(other_ref, gram_other_ref, row >= column)
    for n in range(0, HALF, step):
        columns = pl.ds(n, step)
        square = square_ref[:, columns] + lax.dot_general(
            cross_ref[...], cross_ref[columns, :], (((1,), (1,)), ((), ())), preferred_element_type=jnp.float32
        )
        gram = gram_ref[:, columns].astype(jnp.float32)
        mixing_ref[:, columns] = (coeff_b * gram + coeff_c * square).astype(mixing_ref.dtype)
    for n in range(0, HALF, step):
        columns = pl.ds(n, step)
        square = jnp.dot(gram_ref[...], cross_ref[:, columns], preferred_element_type=jnp.float32)
        square += jnp.dot(cross_ref[...], gram_other_ref[:, columns], preferred_element_type=jnp.float32)
        gram = cross_ref[:, columns].astype(jnp.float32)
        mixing_ref[:, pl.ds(HALF + n, step)] = (coeff_b * gram + coeff_c * square).astype(mixing_ref.dtype)
    for t in range(0, TILES, 2):
        columns = pl.ds(t * LANES, 2 * LANES)
        result = jnp.dot(mixing_ref[:, pl.ds(0, HALF)], x_ref[:, columns], preferred_element_type=jnp.float32)
        result += jnp.dot(mixing_ref[:, pl.ds(HALF, HALF)], x_other_ref[:, columns], preferred_element_type=jnp.float32)
        result = scale * (coeff_a * x_ref[:, columns].astype(jnp.float32) + result)
        for i in range(2):
            block = result[:, i * LANES : (i + 1) * LANES].reshape(CHIPS, PANEL, LANES)
            j = t + i
            if j < STRIPES:
                out_ref[j, :, pl.ds(0, PANEL), :] = block.astype(out_ref.dtype)
            else:
                top, bottom = block[:, : PANEL // 2], block[:, PANEL // 2 :]
                for side in range(2):
                    packed = halves(top, bottom, side == 0).astype(out_ref.dtype)
                    out_ref[2 * (j - STRIPES) + side, :, pl.ds(PANEL, PANEL // 2), :] = packed


def update_rows(*operands):
    kind = operands[0].dtype
    return pl.pallas_call(
        update_kernel,
        out_shape=jax.ShapeDtypeStruct((STRIPES, CHIPS, PANEL + PANEL // 2, LANES), kind),
        scratch_shapes=[
            pltpu.VMEM((PACKED, LANES), kind),
            pltpu.VMEM((HALF, HALF), kind),
            pltpu.VMEM((HALF, HALF), kind),
            pltpu.VMEM((HALF, ROWS), kind),
        ],
        compiler_params=pltpu.CompilerParams(vmem_limit_bytes=24 * MIB),
        cost_estimate=pl.CostEstimate(
            flops=4 * HALF * ROWS * ROWS - 2 * HALF * HALF * HALF, bytes_accessed=10 * HALF * ROWS, transcendentals=0
        ),
        name="update_rows",
    )(*operands)


def join_kernel(pieces_ref, out_ref, whole_ref, sems):
    copies = []
    for layer in range(STRIPES):
        for p in range(CHIPS):
            whole_ref[layer, :, tile(p)] = pieces_ref[layer, p, pl.ds(0, PANEL), :]
        for pair in range(CHIPS // 2):
            left = pieces_ref[layer, 2 * pair, pl.ds(PANEL, PANEL // 2), :]
            right = pieces_ref[layer, 2 * pair + 1, pl.ds(PANEL, PANEL // 2), :]
            for part in range(2):
                joined = halves(left, right, part == 0).astype(whole_ref.dtype)
                whole_ref[layer, pl.ds(part * PANEL // 2, PANEL // 2), tile(CHIPS + pair)] = joined
        copies.append(pltpu.make_async_copy(whole_ref.at[layer], out_ref.at[layer], sems.at[layer]))
        copies[-1].start()
    for copy in copies:
        copy.wait()


def join_columns(pieces):
    shape = (pieces.shape[0], PANEL, TILES * LANES)
    return pl.pallas_call(
        join_kernel,
        in_specs=[pl.BlockSpec(memory_space=pltpu.VMEM)],
        out_specs=pl.BlockSpec(memory_space=pl.ANY),
        out_shape=jax.ShapeDtypeStruct(shape, pieces.dtype),
        scratch_shapes=[pltpu.VMEM(shape, pieces.dtype), pltpu.SemaphoreType.DMA((pieces.shape[0],))],
        compiler_params=pltpu.CompilerParams(vmem_limit_bytes=12 * MIB),
        name="join_columns",
    )(pieces)


def swap_cores(value):
    return lax.ppermute(value, "c", [(0, 1), (1, 0)])


def shards(iterate):
    pieces = split_columns(iterate.reshape(PANEL, COLS))
    own = lax.all_to_all(pieces, CHIP_AXES, 0, 0, tiled=True).reshape(HALF, WIDTH)
    other = swap_cores(own)
    keep_a, send_a, diagonal = own_gram(own)
    arrived_a = exchange(send_a, 0, 0)
    keep_b, send_b, keep_c, send_c = cross_gram(diagonal, own, other)
    arrived_b, arrived_c = exchange(send_b, 1, 0), exchange(send_c, 2, 0)
    half_a = add_first(keep_a, after(arrived_a, send_b, send_c))
    half_b, half_c = add_first(keep_b, arrived_b), add_first(keep_c, arrived_c)
    next_a, next_b, next_c = exchange(half_a, 0, 1), exchange(half_b, 1, 1), exchange(half_c, 2, 1)
    half_a = add_second(half_a, after(next_a, half_b))
    next_a = exchange(half_a, 0, 2)
    half_b = add_second(half_b, next_b)
    half_a = add_third(half_a, after(next_a, half_b))
    next_b = exchange(half_b, 1, 2)
    half_c = add_second(half_c, after(next_c, half_a))
    next_c = exchange(half_c, 2, 2)
    half_b = add_third(half_b, next_b)
    first = jnp.concatenate([half_a, after(exchange(half_a, 0, 0), half_b, next_c)])
    half_c = add_third(half_c, next_c)
    streams = [first] + [jnp.concatenate([half, exchange(half, s, 0)]) for s, half in ((1, half_b), (2, half_c))]
    others = [swap_cores(first)]
    others += [swap_cores(stream) for stream in streams[1:]]
    packed, gram, square = own_square(*streams)
    sent = update_rows(packed, *others, gram, square, own, other)
    sent = sent.reshape(STRIPES * CHIPS, PANEL + PANEL // 2, LANES)
    received = lax.all_to_all(sent, ALL_CHIPS, 0, 0, tiled=True)
    return join_columns(received.reshape(STRIPES, CHIPS, PANEL + PANEL // 2, LANES))


def solution(mesh):
    fine = Mesh(mesh.devices.reshape(4, 2, 4, 2, 2), ("z", "yl", "x", "yh", "c"))
    return jax.shard_map(
        shards,
        mesh=fine,
        in_specs=(P(("z", "yl"), ("x", "yh", "c"), None),),
        out_specs=P(None, ("x", "yh", "c"), ("z", "yl")),
        check_vma=False,
    )
```

```python
import math

import jax
import jax.numpy as jnp
from jax import lax
from jax.experimental import pallas as pl
from jax.experimental.pallas import tpu as pltpu
from jax.sharding import Mesh, PartitionSpec as P

coeff_a = 3.4445
coeff_b = -4.775
coeff_c = 2.0315

ROWS = 1536
COLS = 12288
LANES = 128
CHIPS = 8
STRIPES = 8
PANEL = ROWS // (2 * CHIPS)
HALF = ROWS // 2
WIDTH = COLS // CHIPS
TILES = COLS // STRIPES // LANES
BLOCKS = HALF // LANES
BELOW = LANES * BLOCKS * (BLOCKS - 1) // 2
EDGE = 2 * BELOW + HALF
PACKED = -(-(EDGE + BLOCKS) // (16 * CHIPS)) * 16 * CHIPS
PIECES = (240, 208, 144)
BASES = (0, CHIPS * PIECES[0], CHIPS * (PIECES[0] + PIECES[1]))
MIB = 1 << 20

CHIP_AXES = ("x", "yh")
ALL_CHIPS = ("z", "yl", "x", "yh")
ORDERS = (("abd", "bda", "dab"), ("bda", "dab", "abd"))


def halves(a, b, first):
    a, b = a.astype(jnp.float32), b.astype(jnp.float32)
    low = lax.broadcasted_iota(jnp.int32, a.shape, a.ndim - 1) < LANES // 2
    if first:
        return jnp.where(low, a, pltpu.roll(b, LANES // 2, a.ndim - 1))
    return jnp.where(low, pltpu.roll(a, LANES // 2, a.ndim - 1), b)


def tile(index):
    return pl.ds(index * LANES, LANES)


def place(stream, core):
    x, d = lax.axis_index("x"), lax.axis_index("yh")
    bit = {"a": lax.rem((x + 1) // 2, 2), "b": x // 2, "d": d}
    places = [4 * bit[i] + 2 * bit[j] + bit[k] for i, j, k in (orders[stream] for orders in ORDERS)]
    return places[0] + core * (places[1] - places[0])


def piece_rows(stream, position, base, core):
    piece = lax.bitwise_xor(place(stream, core), position)
    return pl.ds(base + pl.multiple_of(piece * PIECES[stream], 16), PIECES[stream])


def split_pieces(stream, whole_ref, base, keep_ref, send_ref):
    half, core = CHIPS // 2, lax.axis_index("c")
    for k in range(half):
        keep_ref[k] = whole_ref[piece_rows(stream, k, base, core), :]
        send_ref[k] = whole_ref[piece_rows(stream, k + half, base, core), :].astype(send_ref.dtype)


def half_shapes(stream, kind):
    shape = (CHIPS // 2, PIECES[stream], LANES)
    return [jax.ShapeDtypeStruct(shape, jnp.float32), jax.ShapeDtypeStruct(shape, kind)]


def split_kernel(x_ref, out_ref):
    for p in range(CHIPS):
        for j in range(STRIPES):
            out_ref[p, :, tile(j)] = x_ref[:, tile(TILES * j + p)]
        for m in range(STRIPES // 2):
            left = x_ref[:, tile(TILES * (2 * m) + CHIPS + p // 2)]
            right = x_ref[:, tile(TILES * (2 * m + 1) + CHIPS + p // 2)]
            out_ref[p, :, tile(STRIPES + m)] = halves(left, right, p % 2 == 0).astype(out_ref.dtype)


def split_columns(x):
    return pl.pallas_call(
        split_kernel,
        out_shape=jax.ShapeDtypeStruct((CHIPS, PANEL, WIDTH), x.dtype),
        compiler_params=pltpu.CompilerParams(vmem_limit_bytes=16 * MIB),
        name="split_columns",
    )(x)


def strip(j):
    below = (BLOCKS - 1 - j) * LANES
    start = LANES * sum(BLOCKS - 1 - i for i in range(j))
    return pl.ds(start, below)


def triangle(own_ref, ref, store_below, store_diagonal):
    for j in range(0, BLOCKS, 2):
        first = j * LANES
        part = lax.dot_general(
            own_ref[pl.ds(first, HALF - first), :],
            ref[pl.ds(first, 2 * LANES), :],
            (((1,), (1,)), ((), ())),
            preferred_element_type=jnp.float32,
        )
        for i in range(2):
            columns = part[i * LANES :, i * LANES : (i + 1) * LANES]
            store_diagonal(j + i, columns[:LANES])
            if j + i + 1 < BLOCKS:
                store_below(strip(j + i), columns[LANES:])


def iotas():
    return [lax.broadcasted_iota(jnp.int32, (LANES, LANES), axis) for axis in range(2)]


def own_gram_kernel(own_ref, keep_ref, send_ref, diagonal_ref, whole_ref):
    def store_below(rows, value):
        whole_ref[rows, :] = value

    def store_diagonal(j, value):
        diagonal_ref[j] = value

    triangle(own_ref, own_ref, store_below, store_diagonal)
    split_pieces(0, whole_ref, 0, keep_ref, send_ref)


def own_gram(own):
    return pl.pallas_call(
        own_gram_kernel,
        out_shape=half_shapes(0, own.dtype) + [jax.ShapeDtypeStruct((BLOCKS, LANES, LANES), jnp.float32)],
        scratch_shapes=[pltpu.VMEM((BELOW, LANES), jnp.float32)],
        compiler_params=pltpu.CompilerParams(vmem_limit_bytes=8 * MIB),
        cost_estimate=pl.CostEstimate(
            flops=2 * (BELOW + 3 * HALF) * LANES * WIDTH, bytes_accessed=2 * HALF * WIDTH, transcendentals=0
        ),
        name="own_gram",
    )(own)


def cross_gram_kernel(
    diagonal_ref, own_ref, other_ref, keep_b_ref, send_b_ref, keep_c_ref, send_c_ref, whole_ref
):
    row, column = iotas()
    edges = []

    def store_below(rows, value):
        whole_ref[rows, :] = value

    def store_diagonal(j, value):
        whole_ref[pl.ds(BELOW + j * LANES, LANES), :] = jnp.where(row >= column, diagonal_ref[j], value)
        edges.append(jnp.sum(jnp.where(row == column, value, 0.0), axis=0, keepdims=True))

    triangle(own_ref, other_ref, store_below, store_diagonal)
    edges.append(jnp.zeros((PACKED - EDGE - BLOCKS, LANES), jnp.float32))
    whole_ref[pl.ds(EDGE - BASES[1], PACKED - EDGE), :] = jnp.concatenate(edges)
    split_pieces(1, whole_ref, 0, keep_b_ref, send_b_ref)
    split_pieces(2, whole_ref, BASES[2] - BASES[1], keep_c_ref, send_c_ref)


def cross_gram(diagonal, own, other):
    return pl.pallas_call(
        cross_gram_kernel,
        out_shape=half_shapes(1, own.dtype) + half_shapes(2, own.dtype),
        scratch_shapes=[pltpu.VMEM((PACKED - BASES[1], LANES), jnp.float32)],
        compiler_params=pltpu.CompilerParams(vmem_limit_bytes=12 * MIB),
        cost_estimate=pl.CostEstimate(
            flops=2 * (BELOW + 3 * HALF) * LANES * WIDTH, bytes_accessed=4 * HALF * WIDTH, transcendentals=0
        ),
        name="cross_gram",
    )(diagonal, own, other)


def exchange(value, stream, hop):
    pairs = []
    for x in range(4):
        for d in range(2):
            for core in range(2):
                axis = ORDERS[core][stream][hop]
                to = {"a": (x ^ 1, d), "b": (3 - x, d), "d": (x, 1 - d)}[axis]
                pairs.append((4 * x + 2 * d + core, 4 * to[0] + 2 * to[1] + core))
    return lax.ppermute(value, ("x", "yh", "c"), pairs)


def wide(value):
    return value.astype(jnp.float32)


def after(value, *others):
    return lax.optimization_barrier((value, *others))[0]


def add_first(keep, arrived):
    return (keep + wide(arrived)).astype(arrived.dtype).reshape(2, 2, *keep.shape[1:])


def add_second(half, arrived):
    return (wide(half) + wide(arrived)[::-1]).astype(half.dtype)


def add_third(half, arrived):
    return (wide(half) + wide(arrived)[:, ::-1]).astype(half.dtype).reshape(CHIPS // 2, *half.shape[2:])


def unpermute(streams, packed_ref, core):
    for s, pieces_ref in enumerate(streams):
        for k in range(CHIPS):
            packed_ref[piece_rows(s, k, BASES[s], core), :] = pieces_ref[k]


def mirror(packed_ref, out_ref, lower):
    for j in range(BLOCKS):
        first = j * LANES
        block = packed_ref[pl.ds(2 * BELOW + first, LANES), :]
        out_ref[pl.ds(first, LANES), tile(j)] = jnp.where(lower, block, block.T)
        if j + 1 < BLOCKS:
            below = packed_ref[strip(j), :]
            out_ref[pl.ds(first + LANES, below.shape[0]), tile(j)] = below
            out_ref[pl.ds(first, LANES), pl.ds(first + LANES, below.shape[0])] = below.T


def own_square_kernel(a_ref, b_ref, c_ref, packed_ref, gram_ref, square_ref):
    row, column = iotas()
    unpermute((a_ref, b_ref, c_ref), packed_ref, lax.axis_index("c"))
    mirror(packed_ref, gram_ref, row >= column)
    for n in range(0, HALF, 256):
        columns = pl.ds(n, 256)
        square_ref[:, columns] = jnp.dot(gram_ref[...], gram_ref[:, columns], preferred_element_type=jnp.float32)


def own_square(*streams):
    return pl.pallas_call(
        own_square_kernel,
        out_shape=(
            jax.ShapeDtypeStruct((PACKED, LANES), streams[0].dtype),
            jax.ShapeDtypeStruct((HALF, HALF), streams[0].dtype),
            jax.ShapeDtypeStruct((HALF, HALF), jnp.float32),
        ),
        compiler_params=pltpu.CompilerParams(vmem_limit_bytes=12 * MIB),
        cost_estimate=pl.CostEstimate(
            flops=2 * HALF * HALF * HALF, bytes_accessed=8 * HALF * HALF, transcendentals=0
        ),
        name="own_square",
    )(*streams)


def unpack_cross(own_ref, other_ref, cross_ref):
    row, column = iotas()
    for j in range(BLOCKS):
        first = j * LANES
        upper, theirs = (ref[pl.ds(2 * BELOW + first, LANES), :] for ref in (own_ref, other_ref))
        edge = jnp.broadcast_to(own_ref[pl.ds(EDGE, 16), :].astype(jnp.float32)[j : j + 1], (LANES, LANES))
        block = jnp.where(row < column, upper.astype(jnp.float32), theirs.T.astype(jnp.float32))
        cross_ref[pl.ds(first, LANES), tile(j)] = jnp.where(row == column, edge, block).astype(cross_ref.dtype)
        if j + 1 < BLOCKS:
            rows = pl.ds(BELOW + strip(j).start, strip(j).size)
            cross_ref[pl.ds(first + LANES, rows.size), tile(j)] = own_ref[rows, :]
            cross_ref[pl.ds(first, LANES), pl.ds(first + LANES, rows.size)] = other_ref[rows, :].T


def update_kernel(
    own_ref, a_ref, b_ref, c_ref, gram_ref, square_ref, x_ref, x_other_ref, out_ref,
    other_ref, cross_ref, gram_other_ref, mixing_ref,
):
    scale = math.sqrt(max(ROWS, COLS))
    step = 256
    row, column = iotas()
    unpermute((a_ref, b_ref, c_ref), other_ref, 1 - lax.axis_index("c"))
    unpack_cross(own_ref, other_ref, cross_ref)
    mirror(other_ref, gram_other_ref, row >= column)
    for n in range(0, HALF, step):
        columns = pl.ds(n, step)
        square = square_ref[:, columns] + lax.dot_general(
            cross_ref[...], cross_ref[columns, :], (((1,), (1,)), ((), ())), preferred_element_type=jnp.float32
        )
        gram = gram_ref[:, columns].astype(jnp.float32)
        mixing_ref[:, columns] = (coeff_b * gram + coeff_c * square).astype(mixing_ref.dtype)
    for n in range(0, HALF, step):
        columns = pl.ds(n, step)
        square = jnp.dot(gram_ref[...], cross_ref[:, columns], preferred_element_type=jnp.float32)
        square += jnp.dot(cross_ref[...], gram_other_ref[:, columns], preferred_element_type=jnp.float32)
        gram = cross_ref[:, columns].astype(jnp.float32)
        mixing_ref[:, pl.ds(HALF + n, step)] = (coeff_b * gram + coeff_c * square).astype(mixing_ref.dtype)
    for t in range(0, TILES, 2):
        columns = pl.ds(t * LANES, 2 * LANES)
        result = jnp.dot(mixing_ref[:, pl.ds(0, HALF)], x_ref[:, columns], preferred_element_type=jnp.float32)
        result += jnp.dot(mixing_ref[:, pl.ds(HALF, HALF)], x_other_ref[:, columns], preferred_element_type=jnp.float32)
        result = scale * (coeff_a * x_ref[:, columns].astype(jnp.float32) + result)
        for i in range(2):
            block = result[:, i * LANES : (i + 1) * LANES].reshape(CHIPS, PANEL, LANES)
            j = t + i
            if j < STRIPES:
                out_ref[j, :, pl.ds(0, PANEL), :] = block.astype(out_ref.dtype)
            else:
                top, bottom = block[:, : PANEL // 2], block[:, PANEL // 2 :]
                for side in range(2):
                    packed = halves(top, bottom, side == 0).astype(out_ref.dtype)
                    out_ref[2 * (j - STRIPES) + side, :, pl.ds(PANEL, PANEL // 2), :] = packed


def update_rows(*operands):
    kind = operands[0].dtype
    return pl.pallas_call(
        update_kernel,
        out_shape=jax.ShapeDtypeStruct((STRIPES, CHIPS, PANEL + PANEL // 2, LANES), kind),
        scratch_shapes=[
            pltpu.VMEM((PACKED, LANES), kind),
            pltpu.VMEM((HALF, HALF), kind),
            pltpu.VMEM((HALF, HALF), kind),
            pltpu.VMEM((HALF, ROWS), kind),
        ],
        compiler_params=pltpu.CompilerParams(vmem_limit_bytes=24 * MIB),
        cost_estimate=pl.CostEstimate(
            flops=4 * HALF * ROWS * ROWS - 2 * HALF * HALF * HALF, bytes_accessed=10 * HALF * ROWS, transcendentals=0
        ),
        name="update_rows",
    )(*operands)


def join_kernel(pieces_ref, out_ref, whole_ref, sems):
    copies = []
    for layer in range(STRIPES):
        for p in range(CHIPS):
            whole_ref[layer, :, tile(p)] = pieces_ref[layer, p, pl.ds(0, PANEL), :]
        for pair in range(CHIPS // 2):
            left = pieces_ref[layer, 2 * pair, pl.ds(PANEL, PANEL // 2), :]
            right = pieces_ref[layer, 2 * pair + 1, pl.ds(PANEL, PANEL // 2), :]
            for part in range(2):
                joined = halves(left, right, part == 0).astype(whole_ref.dtype)
                whole_ref[layer, pl.ds(part * PANEL // 2, PANEL // 2), tile(CHIPS + pair)] = joined
        copies.append(pltpu.make_async_copy(whole_ref.at[layer], out_ref.at[layer], sems.at[layer]))
        copies[-1].start()
    for copy in copies:
        copy.wait()


def join_columns(pieces):
    shape = (pieces.shape[0], PANEL, TILES * LANES)
    return pl.pallas_call(
        join_kernel,
        in_specs=[pl.BlockSpec(memory_space=pltpu.VMEM)],
        out_specs=pl.BlockSpec(memory_space=pl.ANY),
        out_shape=jax.ShapeDtypeStruct(shape, pieces.dtype),
        scratch_shapes=[pltpu.VMEM(shape, pieces.dtype), pltpu.SemaphoreType.DMA((pieces.shape[0],))],
        compiler_params=pltpu.CompilerParams(vmem_limit_bytes=12 * MIB),
        name="join_columns",
    )(pieces)


def swap_cores(value):
    return lax.ppermute(value, "c", [(0, 1), (1, 0)])


def shards(iterate):
    pieces = split_columns(iterate.reshape(PANEL, COLS))
    own = lax.all_to_all(pieces, CHIP_AXES, 0, 0, tiled=True).reshape(HALF, WIDTH)
    other = swap_cores(own)
    keep_a, send_a, diagonal = own_gram(own)
    arrived_a = exchange(send_a, 0, 0)
    keep_b, send_b, keep_c, send_c = cross_gram(diagonal, own, other)
    arrived_b, arrived_c = exchange(send_b, 1, 0), exchange(send_c, 2, 0)
    half_a = add_first(keep_a, after(arrived_a, send_b, send_c))
    half_b, half_c = add_first(keep_b, arrived_b), add_first(keep_c, arrived_c)
    next_a, next_b, next_c = exchange(half_a, 0, 1), exchange(half_b, 1, 1), exchange(half_c, 2, 1)
    half_a = add_second(half_a, after(next_a, half_b))
    next_a = exchange(half_a, 0, 2)
    half_b = add_second(half_b, next_b)
    half_a = add_third(half_a, after(next_a, half_b))
    next_b = exchange(half_b, 1, 2)
    half_c = add_second(half_c, after(next_c, half_a))
    next_c = exchange(half_c, 2, 2)
    half_b = add_third(half_b, next_b)
    first = jnp.concatenate([half_a, after(exchange(half_a, 0, 0), half_b, next_c)])
    half_c = add_third(half_c, next_c)
    streams = [first] + [jnp.concatenate([half, exchange(half, s, 0)]) for s, half in ((1, half_b), (2, half_c))]
    others = [swap_cores(first)]
    others += [swap_cores(stream) for stream in streams[1:]]
    packed, gram, square = own_square(*streams)
    sent = update_rows(packed, *others, gram, square, own, other)
    sent = sent.reshape(STRIPES * CHIPS, PANEL + PANEL // 2, LANES)
    received = lax.all_to_all(sent, ALL_CHIPS, 0, 0, tiled=True)
    return join_columns(received.reshape(STRIPES, CHIPS, PANEL + PANEL // 2, LANES))


def solution(mesh):
    fine = Mesh(mesh.devices.reshape(4, 2, 4, 2, 2), ("z", "yl", "x", "yh", "c"))
    return jax.shard_map(
        shards,
        mesh=fine,
        in_specs=(P(("z", "yl"), ("x", "yh", "c"), None),),
        out_specs=P(None, ("x", "yh", "c"), ("z", "yl")),
        check_vma=False,
    )
```

```python
import math

import jax
import jax.numpy as jnp
from jax import lax
from jax.experimental import pallas as pl
from jax.experimental.pallas import tpu as pltpu
from jax.sharding import Mesh, PartitionSpec as P

coeff_a = 3.4445
coeff_b = -4.775
coeff_c = 2.0315

ROWS = 1536
COLS = 12288
LANES = 128
CHIPS = 8
STRIPES = 8
PANEL = ROWS // (2 * CHIPS)
HALF = ROWS // 2
WIDTH = COLS // CHIPS
TILES = COLS // STRIPES // LANES
BLOCKS = HALF // LANES
BELOW = LANES * BLOCKS * (BLOCKS - 1) // 2
EDGE = 2 * BELOW + HALF
PACKED = -(-(EDGE + BLOCKS) // (16 * CHIPS)) * 16 * CHIPS
PIECES = (240, 176, 176)
BASES = (0, CHIPS * PIECES[0], CHIPS * (PIECES[0] + PIECES[1]))
MIB = 1 << 20

CHIP_AXES = ("x", "yh")
ALL_CHIPS = ("z", "yl", "x", "yh")
ORDERS = (("abd", "bda", "dab"), ("bda", "dab", "abd"))


def halves(a, b, first):
    a, b = a.astype(jnp.float32), b.astype(jnp.float32)
    low = lax.broadcasted_iota(jnp.int32, a.shape, a.ndim - 1) < LANES // 2
    if first:
        return jnp.where(low, a, pltpu.roll(b, LANES // 2, a.ndim - 1))
    return jnp.where(low, pltpu.roll(a, LANES // 2, a.ndim - 1), b)


def tile(index):
    return pl.ds(index * LANES, LANES)


def place(stream, core):
    x, d = lax.axis_index("x"), lax.axis_index("yh")
    bit = {"a": lax.rem((x + 1) // 2, 2), "b": x // 2, "d": d}
    places = [4 * bit[i] + 2 * bit[j] + bit[k] for i, j, k in (orders[stream] for orders in ORDERS)]
    return places[0] + core * (places[1] - places[0])


def piece_rows(stream, position, base, core):
    piece = lax.bitwise_xor(place(stream, core), position)
    return pl.ds(base + pl.multiple_of(piece * PIECES[stream], 16), PIECES[stream])


def split_pieces(stream, whole_ref, base, keep_ref, send_ref):
    half, core = CHIPS // 2, lax.axis_index("c")
    for k in range(half):
        keep_ref[k] = whole_ref[piece_rows(stream, k, base, core), :]
        send_ref[k] = whole_ref[piece_rows(stream, k + half, base, core), :].astype(send_ref.dtype)


def half_shapes(stream, kind):
    shape = (CHIPS // 2, PIECES[stream], LANES)
    return [jax.ShapeDtypeStruct(shape, jnp.float32), jax.ShapeDtypeStruct(shape, kind)]


def split_kernel(x_ref, out_ref):
    for p in range(CHIPS):
        for j in range(STRIPES):
            out_ref[p, :, tile(j)] = x_ref[:, tile(TILES * j + p)]
        for m in range(STRIPES // 2):
            left = x_ref[:, tile(TILES * (2 * m) + CHIPS + p // 2)]
            right = x_ref[:, tile(TILES * (2 * m + 1) + CHIPS + p // 2)]
            out_ref[p, :, tile(STRIPES + m)] = halves(left, right, p % 2 == 0).astype(out_ref.dtype)


def split_columns(x):
    return pl.pallas_call(
        split_kernel,
        out_shape=jax.ShapeDtypeStruct((CHIPS, PANEL, WIDTH), x.dtype),
        compiler_params=pltpu.CompilerParams(vmem_limit_bytes=16 * MIB),
        name="split_columns",
    )(x)


def strip(j):
    below = (BLOCKS - 1 - j) * LANES
    start = LANES * sum(BLOCKS - 1 - i for i in range(j))
    return pl.ds(start, below)


def triangle(own_ref, ref, store_below, store_diagonal):
    for j in range(0, BLOCKS, 2):
        first = j * LANES
        part = lax.dot_general(
            own_ref[pl.ds(first, HALF - first), :],
            ref[pl.ds(first, 2 * LANES), :],
            (((1,), (1,)), ((), ())),
            preferred_element_type=jnp.float32,
        )
        for i in range(2):
            columns = part[i * LANES :, i * LANES : (i + 1) * LANES]
            store_diagonal(j + i, columns[:LANES])
            if j + i + 1 < BLOCKS:
                store_below(strip(j + i), columns[LANES:])


def iotas():
    return [lax.broadcasted_iota(jnp.int32, (LANES, LANES), axis) for axis in range(2)]


def own_gram_kernel(own_ref, keep_ref, send_ref, diagonal_ref, whole_ref):
    def store_below(rows, value):
        whole_ref[rows, :] = value

    def store_diagonal(j, value):
        diagonal_ref[j] = value

    triangle(own_ref, own_ref, store_below, store_diagonal)
    split_pieces(0, whole_ref, 0, keep_ref, send_ref)


def own_gram(own):
    return pl.pallas_call(
        own_gram_kernel,
        out_shape=half_shapes(0, own.dtype) + [jax.ShapeDtypeStruct((BLOCKS, LANES, LANES), jnp.float32)],
        scratch_shapes=[pltpu.VMEM((BELOW, LANES), jnp.float32)],
        compiler_params=pltpu.CompilerParams(vmem_limit_bytes=8 * MIB),
        cost_estimate=pl.CostEstimate(
            flops=2 * (BELOW + 3 * HALF) * LANES * WIDTH, bytes_accessed=2 * HALF * WIDTH, transcendentals=0
        ),
        name="own_gram",
    )(own)


def cross_gram_kernel(
    diagonal_ref, own_ref, other_ref, keep_b_ref, send_b_ref, keep_c_ref, send_c_ref, whole_ref
):
    row, column = iotas()
    edges = []

    def store_below(rows, value):
        whole_ref[rows, :] = value

    def store_diagonal(j, value):
        whole_ref[pl.ds(BELOW + j * LANES, LANES), :] = jnp.where(row >= column, diagonal_ref[j], value)
        edges.append(jnp.sum(jnp.where(row == column, value, 0.0), axis=0, keepdims=True))

    triangle(own_ref, other_ref, store_below, store_diagonal)
    edges.append(jnp.zeros((PACKED - EDGE - BLOCKS, LANES), jnp.float32))
    whole_ref[pl.ds(EDGE - BASES[1], PACKED - EDGE), :] = jnp.concatenate(edges)
    split_pieces(1, whole_ref, 0, keep_b_ref, send_b_ref)
    split_pieces(2, whole_ref, BASES[2] - BASES[1], keep_c_ref, send_c_ref)


def cross_gram(diagonal, own, other):
    return pl.pallas_call(
        cross_gram_kernel,
        out_shape=half_shapes(1, own.dtype) + half_shapes(2, own.dtype),
        scratch_shapes=[pltpu.VMEM((PACKED - BASES[1], LANES), jnp.float32)],
        compiler_params=pltpu.CompilerParams(vmem_limit_bytes=12 * MIB),
        cost_estimate=pl.CostEstimate(
            flops=2 * (BELOW + 3 * HALF) * LANES * WIDTH, bytes_accessed=4 * HALF * WIDTH, transcendentals=0
        ),
        name="cross_gram",
    )(diagonal, own, other)


def exchange(value, stream, hop):
    pairs = []
    for x in range(4):
        for d in range(2):
            for core in range(2):
                axis = ORDERS[core][stream][hop]
                to = {"a": (x ^ 1, d), "b": (3 - x, d), "d": (x, 1 - d)}[axis]
                pairs.append((4 * x + 2 * d + core, 4 * to[0] + 2 * to[1] + core))
    return lax.ppermute(value, ("x", "yh", "c"), pairs)


def wide(value):
    return value.astype(jnp.float32)


def after(value, *others):
    return lax.optimization_barrier((value, *others))[0]


def add_first(keep, arrived):
    return (keep + wide(arrived)).astype(arrived.dtype).reshape(2, 2, *keep.shape[1:])


def add_second(half, arrived):
    return (wide(half) + wide(arrived)[::-1]).astype(half.dtype)


def add_third(half, arrived):
    return (wide(half) + wide(arrived)[:, ::-1]).astype(half.dtype).reshape(CHIPS // 2, *half.shape[2:])


def unpermute(streams, packed_ref, core):
    for s, pieces_ref in enumerate(streams):
        for k in range(CHIPS):
            packed_ref[piece_rows(s, k, BASES[s], core), :] = pieces_ref[k]


def mirror(packed_ref, out_ref, lower):
    for j in range(BLOCKS):
        first = j * LANES
        block = packed_ref[pl.ds(2 * BELOW + first, LANES), :]
        out_ref[pl.ds(first, LANES), tile(j)] = jnp.where(lower, block, block.T)
        if j + 1 < BLOCKS:
            below = packed_ref[strip(j), :]
            out_ref[pl.ds(first + LANES, below.shape[0]), tile(j)] = below
            out_ref[pl.ds(first, LANES), pl.ds(first + LANES, below.shape[0])] = below.T


def own_square_kernel(a_ref, b_ref, c_ref, packed_ref, gram_ref, square_ref):
    row, column = iotas()
    unpermute((a_ref, b_ref, c_ref), packed_ref, lax.axis_index("c"))
    mirror(packed_ref, gram_ref, row >= column)
    for n in range(0, HALF, 256):
        columns = pl.ds(n, 256)
        square_ref[:, columns] = jnp.dot(gram_ref[...], gram_ref[:, columns], preferred_element_type=jnp.float32)


def own_square(*streams):
    return pl.pallas_call(
        own_square_kernel,
        out_shape=(
            jax.ShapeDtypeStruct((PACKED, LANES), streams[0].dtype),
            jax.ShapeDtypeStruct((HALF, HALF), streams[0].dtype),
            jax.ShapeDtypeStruct((HALF, HALF), jnp.float32),
        ),
        compiler_params=pltpu.CompilerParams(vmem_limit_bytes=12 * MIB),
        cost_estimate=pl.CostEstimate(
            flops=2 * HALF * HALF * HALF, bytes_accessed=8 * HALF * HALF, transcendentals=0
        ),
        name="own_square",
    )(*streams)


def unpack_cross(own_ref, other_ref, cross_ref):
    row, column = iotas()
    for j in range(BLOCKS):
        first = j * LANES
        upper, theirs = (ref[pl.ds(2 * BELOW + first, LANES), :] for ref in (own_ref, other_ref))
        edge = jnp.broadcast_to(own_ref[pl.ds(EDGE, 16), :].astype(jnp.float32)[j : j + 1], (LANES, LANES))
        block = jnp.where(row < column, upper.astype(jnp.float32), theirs.T.astype(jnp.float32))
        cross_ref[pl.ds(first, LANES), tile(j)] = jnp.where(row == column, edge, block).astype(cross_ref.dtype)
        if j + 1 < BLOCKS:
            rows = pl.ds(BELOW + strip(j).start, strip(j).size)
            cross_ref[pl.ds(first + LANES, rows.size), tile(j)] = own_ref[rows, :]
            cross_ref[pl.ds(first, LANES), pl.ds(first + LANES, rows.size)] = other_ref[rows, :].T


def update_kernel(
    own_ref, a_ref, b_ref, c_ref, gram_ref, square_ref, x_ref, x_other_ref, out_ref,
    other_ref, cross_ref, gram_other_ref, mixing_ref,
):
    scale = math.sqrt(max(ROWS, COLS))
    step = 256
    row, column = iotas()
    unpermute((a_ref, b_ref, c_ref), other_ref, 1 - lax.axis_index("c"))
    unpack_cross(own_ref, other_ref, cross_ref)
    mirror(other_ref, gram_other_ref, row >= column)
    for n in range(0, HALF, step):
        columns = pl.ds(n, step)
        square = square_ref[:, columns] + lax.dot_general(
            cross_ref[...], cross_ref[columns, :], (((1,), (1,)), ((), ())), preferred_element_type=jnp.float32
        )
        gram = gram_ref[:, columns].astype(jnp.float32)
        mixing_ref[:, columns] = (coeff_b * gram + coeff_c * square).astype(mixing_ref.dtype)
    for n in range(0, HALF, step):
        columns = pl.ds(n, step)
        square = jnp.dot(gram_ref[...], cross_ref[:, columns], preferred_element_type=jnp.float32)
        square += jnp.dot(cross_ref[...], gram_other_ref[:, columns], preferred_element_type=jnp.float32)
        gram = cross_ref[:, columns].astype(jnp.float32)
        mixing_ref[:, pl.ds(HALF + n, step)] = (coeff_b * gram + coeff_c * square).astype(mixing_ref.dtype)
    for t in range(0, TILES, 2):
        columns = pl.ds(t * LANES, 2 * LANES)
        result = jnp.dot(mixing_ref[:, pl.ds(0, HALF)], x_ref[:, columns], preferred_element_type=jnp.float32)
        result += jnp.dot(mixing_ref[:, pl.ds(HALF, HALF)], x_other_ref[:, columns], preferred_element_type=jnp.float32)
        result = scale * (coeff_a * x_ref[:, columns].astype(jnp.float32) + result)
        for i in range(2):
            block = result[:, i * LANES : (i + 1) * LANES].reshape(CHIPS, PANEL, LANES)
            j = t + i
            if j < STRIPES:
                out_ref[j, :, pl.ds(0, PANEL), :] = block.astype(out_ref.dtype)
            else:
                top, bottom = block[:, : PANEL // 2], block[:, PANEL // 2 :]
                for side in range(2):
                    packed = halves(top, bottom, side == 0).astype(out_ref.dtype)
                    out_ref[2 * (j - STRIPES) + side, :, pl.ds(PANEL, PANEL // 2), :] = packed


def update_rows(*operands):
    kind = operands[0].dtype
    return pl.pallas_call(
        update_kernel,
        out_shape=jax.ShapeDtypeStruct((STRIPES, CHIPS, PANEL + PANEL // 2, LANES), kind),
        scratch_shapes=[
            pltpu.VMEM((PACKED, LANES), kind),
            pltpu.VMEM((HALF, HALF), kind),
            pltpu.VMEM((HALF, HALF), kind),
            pltpu.VMEM((HALF, ROWS), kind),
        ],
        compiler_params=pltpu.CompilerParams(vmem_limit_bytes=24 * MIB),
        cost_estimate=pl.CostEstimate(
            flops=4 * HALF * ROWS * ROWS - 2 * HALF * HALF * HALF, bytes_accessed=10 * HALF * ROWS, transcendentals=0
        ),
        name="update_rows",
    )(*operands)


def join_kernel(pieces_ref, out_ref, whole_ref, sems):
    copies = []
    for layer in range(STRIPES):
        for p in range(CHIPS):
            whole_ref[layer, :, tile(p)] = pieces_ref[layer, p, pl.ds(0, PANEL), :]
        for pair in range(CHIPS // 2):
            left = pieces_ref[layer, 2 * pair, pl.ds(PANEL, PANEL // 2), :]
            right = pieces_ref[layer, 2 * pair + 1, pl.ds(PANEL, PANEL // 2), :]
            for part in range(2):
                joined = halves(left, right, part == 0).astype(whole_ref.dtype)
                whole_ref[layer, pl.ds(part * PANEL // 2, PANEL // 2), tile(CHIPS + pair)] = joined
        copies.append(pltpu.make_async_copy(whole_ref.at[layer], out_ref.at[layer], sems.at[layer]))
        copies[-1].start()
    for copy in copies:
        copy.wait()


def join_columns(pieces):
    shape = (pieces.shape[0], PANEL, TILES * LANES)
    return pl.pallas_call(
        join_kernel,
        in_specs=[pl.BlockSpec(memory_space=pltpu.VMEM)],
        out_specs=pl.BlockSpec(memory_space=pl.ANY),
        out_shape=jax.ShapeDtypeStruct(shape, pieces.dtype),
        scratch_shapes=[pltpu.VMEM(shape, pieces.dtype), pltpu.SemaphoreType.DMA((pieces.shape[0],))],
        compiler_params=pltpu.CompilerParams(vmem_limit_bytes=12 * MIB),
        name="join_columns",
    )(pieces)


def swap_cores(value):
    return lax.ppermute(value, "c", [(0, 1), (1, 0)])


def shards(iterate):
    pieces = split_columns(iterate.reshape(PANEL, COLS))
    own = lax.all_to_all(pieces, CHIP_AXES, 0, 0, tiled=True).reshape(HALF, WIDTH)
    other = swap_cores(own)
    keep_a, send_a, diagonal = own_gram(own)
    arrived_a = exchange(send_a, 0, 0)
    keep_b, send_b, keep_c, send_c = cross_gram(diagonal, own, other)
    arrived_b, arrived_c = exchange(send_b, 1, 0), exchange(send_c, 2, 0)
    half_a = add_first(keep_a, after(arrived_a, send_b, send_c))
    half_b, half_c = add_first(keep_b, arrived_b), add_first(keep_c, arrived_c)
    next_a, next_b, next_c = exchange(half_a, 0, 1), exchange(half_b, 1, 1), exchange(half_c, 2, 1)
    half_a = add_second(half_a, after(next_a, half_b))
    next_a = exchange(half_a, 0, 2)
    half_b = add_second(half_b, next_b)
    half_a = add_third(half_a, after(next_a, half_b))
    next_b = exchange(half_b, 1, 2)
    half_c = add_second(half_c, after(next_c, half_a))
    next_c = exchange(half_c, 2, 2)
    half_b = add_third(half_b, next_b)
    first = jnp.concatenate([half_a, after(exchange(half_a, 0, 0), half_b, next_c)])
    half_c = add_third(half_c, next_c)
    streams = [first] + [jnp.concatenate([half, exchange(half, s, 0)]) for s, half in ((1, half_b), (2, half_c))]
    others = [swap_cores(first)]
    others += [swap_cores(stream) for stream in streams[1:]]
    packed, gram, square = own_square(*streams)
    sent = update_rows(packed, *others, gram, square, own, other)
    sent = sent.reshape(STRIPES * CHIPS, PANEL + PANEL // 2, LANES)
    received = lax.all_to_all(sent, ALL_CHIPS, 0, 0, tiled=True)
    return join_columns(received.reshape(STRIPES, CHIPS, PANEL + PANEL // 2, LANES))


def solution(mesh):
    fine = Mesh(mesh.devices.reshape(4, 2, 4, 2, 2), ("z", "yl", "x", "yh", "c"))
    return jax.shard_map(
        shards,
        mesh=fine,
        in_specs=(P(("z", "yl"), ("x", "yh", "c"), None),),
        out_specs=P(None, ("x", "yh", "c"), ("z", "yl")),
        check_vma=False,
    )
```

```python
import math

import jax
import jax.numpy as jnp
from jax import lax
from jax.experimental import pallas as pl
from jax.experimental.pallas import tpu as pltpu
from jax.sharding import Mesh, PartitionSpec as P

coeff_a = 3.4445
coeff_b = -4.775
coeff_c = 2.0315

ROWS = 1536
COLS = 12288
LANES = 128
CHIPS = 8
STRIPES = 8
PANEL = ROWS // (2 * CHIPS)
HALF = ROWS // 2
WIDTH = COLS // CHIPS
TILES = COLS // STRIPES // LANES
BLOCKS = HALF // LANES
BELOW = LANES * BLOCKS * (BLOCKS - 1) // 2
EDGE = 2 * BELOW + HALF
PACKED = -(-(EDGE + BLOCKS) // (16 * CHIPS)) * 16 * CHIPS
PIECES = (240, 192, 160)
BASES = (0, CHIPS * PIECES[0], CHIPS * (PIECES[0] + PIECES[1]))
MIB = 1 << 20

CHIP_AXES = ("x", "yh")
ALL_CHIPS = ("z", "yl", "x", "yh")
ORDERS = (("abd", "bda", "dab"), ("dab", "abd", "bda"))


def halves(a, b, first):
    a, b = a.astype(jnp.float32), b.astype(jnp.float32)
    low = lax.broadcasted_iota(jnp.int32, a.shape, a.ndim - 1) < LANES // 2
    if first:
        return jnp.where(low, a, pltpu.roll(b, LANES // 2, a.ndim - 1))
    return jnp.where(low, pltpu.roll(a, LANES // 2, a.ndim - 1), b)


def tile(index):
    return pl.ds(index * LANES, LANES)


def place(stream, core):
    x, d = lax.axis_index("x"), lax.axis_index("yh")
    bit = {"a": lax.rem((x + 1) // 2, 2), "b": x // 2, "d": d}
    places = [4 * bit[i] + 2 * bit[j] + bit[k] for i, j, k in (orders[stream] for orders in ORDERS)]
    return places[0] + core * (places[1] - places[0])


def piece_rows(stream, position, base, core):
    piece = lax.bitwise_xor(place(stream, core), position)
    return pl.ds(base + pl.multiple_of(piece * PIECES[stream], 16), PIECES[stream])


def split_pieces(stream, whole_ref, base, keep_ref, send_ref):
    half, core = CHIPS // 2, lax.axis_index("c")
    for k in range(half):
        keep_ref[k] = whole_ref[piece_rows(stream, k, base, core), :]
        send_ref[k] = whole_ref[piece_rows(stream, k + half, base, core), :].astype(send_ref.dtype)


def half_shapes(stream, kind):
    shape = (CHIPS // 2, PIECES[stream], LANES)
    return [jax.ShapeDtypeStruct(shape, jnp.float32), jax.ShapeDtypeStruct(shape, kind)]


def split_kernel(x_ref, out_ref):
    for p in range(CHIPS):
        for j in range(STRIPES):
            out_ref[p, :, tile(j)] = x_ref[:, tile(TILES * j + p)]
        for m in range(STRIPES // 2):
            left = x_ref[:, tile(TILES * (2 * m) + CHIPS + p // 2)]
            right = x_ref[:, tile(TILES * (2 * m + 1) + CHIPS + p // 2)]
            out_ref[p, :, tile(STRIPES + m)] = halves(left, right, p % 2 == 0).astype(out_ref.dtype)


def split_columns(x):
    return pl.pallas_call(
        split_kernel,
        out_shape=jax.ShapeDtypeStruct((CHIPS, PANEL, WIDTH), x.dtype),
        compiler_params=pltpu.CompilerParams(vmem_limit_bytes=16 * MIB),
        name="split_columns",
    )(x)


def strip(j):
    below = (BLOCKS - 1 - j) * LANES
    start = LANES * sum(BLOCKS - 1 - i for i in range(j))
    return pl.ds(start, below)


def triangle(own_ref, ref, store_below, store_diagonal):
    for j in range(0, BLOCKS, 2):
        first = j * LANES
        part = lax.dot_general(
            own_ref[pl.ds(first, HALF - first), :],
            ref[pl.ds(first, 2 * LANES), :],
            (((1,), (1,)), ((), ())),
            preferred_element_type=jnp.float32,
        )
        for i in range(2):
            columns = part[i * LANES :, i * LANES : (i + 1) * LANES]
            store_diagonal(j + i, columns[:LANES])
            if j + i + 1 < BLOCKS:
                store_below(strip(j + i), columns[LANES:])


def iotas():
    return [lax.broadcasted_iota(jnp.int32, (LANES, LANES), axis) for axis in range(2)]


def own_gram_kernel(own_ref, keep_ref, send_ref, diagonal_ref, whole_ref):
    def store_below(rows, value):
        whole_ref[rows, :] = value

    def store_diagonal(j, value):
        diagonal_ref[j] = value

    triangle(own_ref, own_ref, store_below, store_diagonal)
    split_pieces(0, whole_ref, 0, keep_ref, send_ref)


def own_gram(own):
    return pl.pallas_call(
        own_gram_kernel,
        out_shape=half_shapes(0, own.dtype) + [jax.ShapeDtypeStruct((BLOCKS, LANES, LANES), jnp.float32)],
        scratch_shapes=[pltpu.VMEM((BELOW, LANES), jnp.float32)],
        compiler_params=pltpu.CompilerParams(vmem_limit_bytes=8 * MIB),
        cost_estimate=pl.CostEstimate(
            flops=2 * (BELOW + 3 * HALF) * LANES * WIDTH, bytes_accessed=2 * HALF * WIDTH, transcendentals=0
        ),
        name="own_gram",
    )(own)


def cross_gram_kernel(
    diagonal_ref, own_ref, other_ref, keep_b_ref, send_b_ref, keep_c_ref, send_c_ref, whole_ref
):
    row, column = iotas()
    edges = []

    def store_below(rows, value):
        whole_ref[rows, :] = value

    def store_diagonal(j, value):
        whole_ref[pl.ds(BELOW + j * LANES, LANES), :] = jnp.where(row >= column, diagonal_ref[j], value)
        edges.append(jnp.sum(jnp.where(row == column, value, 0.0), axis=0, keepdims=True))

    triangle(own_ref, other_ref, store_below, store_diagonal)
    edges.append(jnp.zeros((PACKED - EDGE - BLOCKS, LANES), jnp.float32))
    whole_ref[pl.ds(EDGE - BASES[1], PACKED - EDGE), :] = jnp.concatenate(edges)
    split_pieces(1, whole_ref, 0, keep_b_ref, send_b_ref)
    split_pieces(2, whole_ref, BASES[2] - BASES[1], keep_c_ref, send_c_ref)


def cross_gram(diagonal, own, other):
    return pl.pallas_call(
        cross_gram_kernel,
        out_shape=half_shapes(1, own.dtype) + half_shapes(2, own.dtype),
        scratch_shapes=[pltpu.VMEM((PACKED - BASES[1], LANES), jnp.float32)],
        compiler_params=pltpu.CompilerParams(vmem_limit_bytes=12 * MIB),
        cost_estimate=pl.CostEstimate(
            flops=2 * (BELOW + 3 * HALF) * LANES * WIDTH, bytes_accessed=4 * HALF * WIDTH, transcendentals=0
        ),
        name="cross_gram",
    )(diagonal, own, other)


def exchange(value, stream, hop):
    pairs = []
    for x in range(4):
        for d in range(2):
            for core in range(2):
                axis = ORDERS[core][stream][hop]
                to = {"a": (x ^ 1, d), "b": (3 - x, d), "d": (x, 1 - d)}[axis]
                pairs.append((4 * x + 2 * d + core, 4 * to[0] + 2 * to[1] + core))
    return lax.ppermute(value, ("x", "yh", "c"), pairs)


def wide(value):
    return value.astype(jnp.float32)


def after(value, *others):
    return lax.optimization_barrier((value, *others))[0]


def add_first(keep, arrived):
    return (keep + wide(arrived)).astype(arrived.dtype).reshape(2, 2, *keep.shape[1:])


def add_second(half, arrived):
    return (wide(half) + wide(arrived)[::-1]).astype(half.dtype)


def add_third(half, arrived):
    return (wide(half) + wide(arrived)[:, ::-1]).astype(half.dtype).reshape(CHIPS // 2, *half.shape[2:])


def unpermute(streams, packed_ref, core):
    for s, pieces_ref in enumerate(streams):
        for k in range(CHIPS):
            packed_ref[piece_rows(s, k, BASES[s], core), :] = pieces_ref[k]


def mirror(packed_ref, out_ref, lower):
    for j in range(BLOCKS):
        first = j * LANES
        block = packed_ref[pl.ds(2 * BELOW + first, LANES), :]
        out_ref[pl.ds(first, LANES), tile(j)] = jnp.where(lower, block, block.T)
        if j + 1 < BLOCKS:
            below = packed_ref[strip(j), :]
            out_ref[pl.ds(first + LANES, below.shape[0]), tile(j)] = below
            out_ref[pl.ds(first, LANES), pl.ds(first + LANES, below.shape[0])] = below.T


def own_square_kernel(a_ref, b_ref, c_ref, packed_ref, gram_ref, square_ref):
    row, column = iotas()
    unpermute((a_ref, b_ref, c_ref), packed_ref, lax.axis_index("c"))
    mirror(packed_ref, gram_ref, row >= column)
    for n in range(0, HALF, 256):
        columns = pl.ds(n, 256)
        square_ref[:, columns] = jnp.dot(gram_ref[...], gram_ref[:, columns], preferred_element_type=jnp.float32)


def own_square(*streams):
    return pl.pallas_call(
        own_square_kernel,
        out_shape=(
            jax.ShapeDtypeStruct((PACKED, LANES), streams[0].dtype),
            jax.ShapeDtypeStruct((HALF, HALF), streams[0].dtype),
            jax.ShapeDtypeStruct((HALF, HALF), jnp.float32),
        ),
        compiler_params=pltpu.CompilerParams(vmem_limit_bytes=12 * MIB),
        cost_estimate=pl.CostEstimate(
            flops=2 * HALF * HALF * HALF, bytes_accessed=8 * HALF * HALF, transcendentals=0
        ),
        name="own_square",
    )(*streams)


def unpack_cross(own_ref, other_ref, cross_ref):
    row, column = iotas()
    for j in range(BLOCKS):
        first = j * LANES
        upper, theirs = (ref[pl.ds(2 * BELOW + first, LANES), :] for ref in (own_ref, other_ref))
        edge = jnp.broadcast_to(own_ref[pl.ds(EDGE, 16), :].astype(jnp.float32)[j : j + 1], (LANES, LANES))
        block = jnp.where(row < column, upper.astype(jnp.float32), theirs.T.astype(jnp.float32))
        cross_ref[pl.ds(first, LANES), tile(j)] = jnp.where(row == column, edge, block).astype(cross_ref.dtype)
        if j + 1 < BLOCKS:
            rows = pl.ds(BELOW + strip(j).start, strip(j).size)
            cross_ref[pl.ds(first + LANES, rows.size), tile(j)] = own_ref[rows, :]
            cross_ref[pl.ds(first, LANES), pl.ds(first + LANES, rows.size)] = other_ref[rows, :].T


def update_kernel(
    own_ref, a_ref, b_ref, c_ref, gram_ref, square_ref, x_ref, x_other_ref, out_ref,
    other_ref, cross_ref, gram_other_ref, mixing_ref,
):
    scale = math.sqrt(max(ROWS, COLS))
    step = 256
    row, column = iotas()
    unpermute((a_ref, b_ref, c_ref), other_ref, 1 - lax.axis_index("c"))
    unpack_cross(own_ref, other_ref, cross_ref)
    mirror(other_ref, gram_other_ref, row >= column)
    for n in range(0, HALF, step):
        columns = pl.ds(n, step)
        square = square_ref[:, columns] + lax.dot_general(
            cross_ref[...], cross_ref[columns, :], (((1,), (1,)), ((), ())), preferred_element_type=jnp.float32
        )
        gram = gram_ref[:, columns].astype(jnp.float32)
        mixing_ref[:, columns] = (coeff_b * gram + coeff_c * square).astype(mixing_ref.dtype)
    for n in range(0, HALF, step):
        columns = pl.ds(n, step)
        square = jnp.dot(gram_ref[...], cross_ref[:, columns], preferred_element_type=jnp.float32)
        square += jnp.dot(cross_ref[...], gram_other_ref[:, columns], preferred_element_type=jnp.float32)
        gram = cross_ref[:, columns].astype(jnp.float32)
        mixing_ref[:, pl.ds(HALF + n, step)] = (coeff_b * gram + coeff_c * square).astype(mixing_ref.dtype)
    for t in range(0, TILES, 2):
        columns = pl.ds(t * LANES, 2 * LANES)
        result = jnp.dot(mixing_ref[:, pl.ds(0, HALF)], x_ref[:, columns], preferred_element_type=jnp.float32)
        result += jnp.dot(mixing_ref[:, pl.ds(HALF, HALF)], x_other_ref[:, columns], preferred_element_type=jnp.float32)
        result = scale * (coeff_a * x_ref[:, columns].astype(jnp.float32) + result)
        for i in range(2):
            block = result[:, i * LANES : (i + 1) * LANES].reshape(CHIPS, PANEL, LANES)
            j = t + i
            if j < STRIPES:
                out_ref[j, :, pl.ds(0, PANEL), :] = block.astype(out_ref.dtype)
            else:
                top, bottom = block[:, : PANEL // 2], block[:, PANEL // 2 :]
                for side in range(2):
                    packed = halves(top, bottom, side == 0).astype(out_ref.dtype)
                    out_ref[2 * (j - STRIPES) + side, :, pl.ds(PANEL, PANEL // 2), :] = packed


def update_rows(*operands):
    kind = operands[0].dtype
    return pl.pallas_call(
        update_kernel,
        out_shape=jax.ShapeDtypeStruct((STRIPES, CHIPS, PANEL + PANEL // 2, LANES), kind),
        scratch_shapes=[
            pltpu.VMEM((PACKED, LANES), kind),
            pltpu.VMEM((HALF, HALF), kind),
            pltpu.VMEM((HALF, HALF), kind),
            pltpu.VMEM((HALF, ROWS), kind),
        ],
        compiler_params=pltpu.CompilerParams(vmem_limit_bytes=24 * MIB),
        cost_estimate=pl.CostEstimate(
            flops=4 * HALF * ROWS * ROWS - 2 * HALF * HALF * HALF, bytes_accessed=10 * HALF * ROWS, transcendentals=0
        ),
        name="update_rows",
    )(*operands)


def join_kernel(pieces_ref, out_ref, whole_ref, sems):
    copies = []
    for layer in range(STRIPES):
        for p in range(CHIPS):
            whole_ref[layer, :, tile(p)] = pieces_ref[layer, p, pl.ds(0, PANEL), :]
        for pair in range(CHIPS // 2):
            left = pieces_ref[layer, 2 * pair, pl.ds(PANEL, PANEL // 2), :]
            right = pieces_ref[layer, 2 * pair + 1, pl.ds(PANEL, PANEL // 2), :]
            for part in range(2):
                joined = halves(left, right, part == 0).astype(whole_ref.dtype)
                whole_ref[layer, pl.ds(part * PANEL // 2, PANEL // 2), tile(CHIPS + pair)] = joined
        copies.append(pltpu.make_async_copy(whole_ref.at[layer], out_ref.at[layer], sems.at[layer]))
        copies[-1].start()
    for copy in copies:
        copy.wait()


def join_columns(pieces):
    shape = (pieces.shape[0], PANEL, TILES * LANES)
    return pl.pallas_call(
        join_kernel,
        in_specs=[pl.BlockSpec(memory_space=pltpu.VMEM)],
        out_specs=pl.BlockSpec(memory_space=pl.ANY),
        out_shape=jax.ShapeDtypeStruct(shape, pieces.dtype),
        scratch_shapes=[pltpu.VMEM(shape, pieces.dtype), pltpu.SemaphoreType.DMA((pieces.shape[0],))],
        compiler_params=pltpu.CompilerParams(vmem_limit_bytes=12 * MIB),
        name="join_columns",
    )(pieces)


def swap_cores(value):
    return lax.ppermute(value, "c", [(0, 1), (1, 0)])


def shards(iterate):
    pieces = split_columns(iterate.reshape(PANEL, COLS))
    own = lax.all_to_all(pieces, CHIP_AXES, 0, 0, tiled=True).reshape(HALF, WIDTH)
    other = swap_cores(own)
    keep_a, send_a, diagonal = own_gram(own)
    arrived_a = exchange(send_a, 0, 0)
    keep_b, send_b, keep_c, send_c = cross_gram(diagonal, own, other)
    arrived_b, arrived_c = exchange(send_b, 1, 0), exchange(send_c, 2, 0)
    half_a = add_first(keep_a, after(arrived_a, send_b, send_c))
    half_b, half_c = add_first(keep_b, arrived_b), add_first(keep_c, arrived_c)
    next_a, next_b, next_c = exchange(half_a, 0, 1), exchange(half_b, 1, 1), exchange(half_c, 2, 1)
    half_a = add_second(half_a, after(next_a, half_b))
    next_a = exchange(half_a, 0, 2)
    half_b = add_second(half_b, next_b)
    half_a = add_third(half_a, after(next_a, half_b))
    next_b = exchange(half_b, 1, 2)
    half_c = add_second(half_c, after(next_c, half_a))
    next_c = exchange(half_c, 2, 2)
    half_b = add_third(half_b, next_b)
    first = jnp.concatenate([half_a, after(exchange(half_a, 0, 0), half_b, next_c)])
    half_c = add_third(half_c, next_c)
    streams = [first] + [jnp.concatenate([half, exchange(half, s, 0)]) for s, half in ((1, half_b), (2, half_c))]
    others = [swap_cores(first)]
    others += [swap_cores(stream) for stream in streams[1:]]
    packed, gram, square = own_square(*streams)
    sent = update_rows(packed, *others, gram, square, own, other)
    sent = sent.reshape(STRIPES * CHIPS, PANEL + PANEL // 2, LANES)
    received = lax.all_to_all(sent, ALL_CHIPS, 0, 0, tiled=True)
    return join_columns(received.reshape(STRIPES, CHIPS, PANEL + PANEL // 2, LANES))


def solution(mesh):
    fine = Mesh(mesh.devices.reshape(4, 2, 4, 2, 2), ("z", "yl", "x", "yh", "c"))
    return jax.shard_map(
        shards,
        mesh=fine,
        in_specs=(P(("z", "yl"), ("x", "yh", "c"), None),),
        out_specs=P(None, ("x", "yh", "c"), ("z", "yl")),
        check_vma=False,
    )
```
